32 devices in a mesh: rows: 4 (over y, x), ffn: 8 (over z, core).
Axes of the slice: x: 2, y: 2, z: 4, core: 2. Of those that a mesh axis runs over, the one named last changes fastest.
Arguments:
- tokens: bfloat16 [32768, 1024], P(('rows', 'ffn')), may hold values from -6 to 6
- lengths: int32 [32], P(('rows', 'ffn')), may hold values from 128 to 1024, as said below
- cotangent: bfloat16 [32768, 1024], P(('rows', 'ffn')), may hold values from -6 to 6
- ln_attn_gain: float32 [1024], replicated, may hold values from 0.1 to 1.9
- ln_attn_bias: float32 [1024], replicated, may hold values from -1.75 to 1.75
- w_query: bfloat16 [1024, 1024], P(('rows', 'ffn')), may hold values from -0.1875 to 0.1875
- query_bias: float32 [1024], replicated, may hold values from -3 to 3
- w_key: bfloat16 [1024, 1024], P(('rows', 'ffn')), may hold values from -0.1875 to 0.1875
- w_value: bfloat16 [1024, 1024], P(('rows', 'ffn')), may hold values from -0.1875 to 0.1875
- value_bias: float32 [1024], replicated, may hold values from -3 to 3
- head_scale: float32 [16], replicated, may hold values from 0.3 to 3
- w_out: bfloat16 [1024, 1024], P(('rows', 'ffn')), may hold values from -0.1875 to 0.1875
- out_bias: float32 [1024], replicated, may hold values from -3 to 3
- post_gain: float32 [1024], replicated, may hold values from 0.1 to 1.9
- post_bias: float32 [1024], replicated, may hold values from -1.75 to 1.75
- ffn_gain: float32 [1024], replicated, may hold values from 0.1 to 1.9
- ffn_bias: float32 [1024], replicated, may hold values from -1.75 to 1.75
- w_up: bfloat16 [1024, 4096], P('rows', 'ffn'), may hold values from -1 to 1
- up_bias: float32 [4096], replicated, may hold values from -3 to 3
- mid_gain: float32 [4096], replicated, may hold values from 0.1 to 1.9
- mid_bias: float32 [4096], replicated, may hold values from -1.75 to 1.75
- w_down: bfloat16 [1024, 4096], P('rows', 'ffn'), may hold values from -0.09375 to 0.09375
- down_bias: float32 [1024], replicated, may hold values from -3 to 3
Outputs:
- result: float32 [32768, 1024], P(('rows', 'ffn'))
- grad_tokens: float32 [32768, 1024], P(('rows', 'ffn'))
- grad_ln_attn_gain: float32 [1024], replicated
- grad_ln_attn_bias: float32 [1024], replicated
- grad_w_query: float32 [1024, 1024], P(('rows', 'ffn'))
- grad_query_bias: float32 [1024], replicated
- grad_w_key: float32 [1024, 1024], P(('rows', 'ffn'))
- grad_w_value: float32 [1024, 1024], P(('rows', 'ffn'))
- grad_value_bias: float32 [1024], replicated
- grad_head_scale: float32 [16], replicated
- grad_w_out: float32 [1024, 1024], P(('rows', 'ffn'))
- grad_out_bias: float32 [1024], replicated
- grad_post_gain: float32 [1024], replicated
- grad_post_bias: float32 [1024], replicated
- grad_ffn_gain: float32 [1024], replicated
- grad_ffn_bias: float32 [1024], replicated
- grad_w_up: float32 [1024, 4096], P('rows', 'ffn')
- grad_up_bias: float32 [4096], P('ffn')
- grad_mid_gain: float32 [4096], P('ffn')
- grad_mid_bias: float32 [4096], P('ffn')
- grad_w_down: float32 [1024, 4096], P('rows', 'ffn')
- grad_down_bias: float32 [1024], replicated
The draws below stay inside these ranges and needn't reach their ends.
Inputs may be any that keep to these rules, and one draw needn't show every extreme that they name: `lengths`: each sequence has between 128 and 1024 valid tokens, at the start of its slots; some sequence has exactly 1024.
All inputs are finite; a program needn't handle non-finite values.
Results may differ from the reference program's by a relative error of at most 0.013.
Values may be sent and summed in bfloat16 or wider, within the bound.
A program may use at most 320 MiB of HBM per device.

```python
import math
import jax
import jax.numpy as jnp
from jax import lax

D = 1024
H = 16
FF = 4096
SEQ = 1024
SEQS = 32
TOKENS = 32768


def draw_lengths(key, part):
    first_key, second_key, third_key = jax.random.split(jax.random.fold_in(key, 11), 3)
    divisor = jax.random.randint(first_key, (SEQS,), 1, 9)
    extra = jax.random.randint(second_key, (SEQS,), 0, max(1, SEQ // 8))
    lengths_drawn = jnp.minimum(SEQ // divisor + extra, SEQ)
    longest = jax.random.randint(third_key, (), 0, SEQS)
    return jnp.where(jnp.arange(SEQS) == longest, SEQ, lengths_drawn).astype(jnp.int32)


def draw_w_up(key, part):
    first_key, second_key = jax.random.split(jax.random.fold_in(key, 23))
    column = jnp.arange(FF).astype(jnp.float32) / FF
    entries = jnp.clip(jax.random.normal(first_key, (D, FF), jnp.float32), -6.0, 6.0)
    jitter = jax.random.uniform(second_key, (FF,), jnp.float32, -0.5, 0.5)
    column_scale = jnp.exp(column * 1.8 - 0.9 + jitter * 1.1)
    return (entries * column_scale[None, :] / math.sqrt(D)).astype(jnp.bfloat16)


def levels(own_key, dims, shards, low, top_value):
    loudness = 1.0
    for axis_at, shards_of in shards:
        draws = jax.random.uniform(jax.random.fold_in(jax.random.fold_in(own_key, 6), axis_at), (shards_of,), jnp.float32, low / len(shards), top_value / len(shards))
        loudness = loudness * jnp.repeat(jnp.exp(draws), dims[axis_at] // shards_of).reshape((-1,) + (1,) * (len(dims) - 1 - axis_at))
    return loudness


def centred(stream_key, dims, scale, limit, pieces=(), kind=jnp.bfloat16):
    level = levels(stream_key, dims, pieces, -0.22, 0.18) if pieces else 1.0
    array = jax.random.normal(stream_key, dims, jnp.float32) * scale * level
    return jnp.minimum(jnp.maximum(array, -limit), limit).astype(kind)


def setup_inputs(seed: int = 0) -> dict:
    seeds = jax.random.split(jax.random.key(seed), 24)
    return {
        "tokens": centred(seeds[0], (TOKENS, D), 1.0, 6.0, ((0, 32),)),
        "lengths": draw_lengths(jax.random.fold_in(seeds[23], 71), 0),
        "cotangent": centred(seeds[2], (TOKENS, D), 1.0, 6.0, ((0, 32),)),
        "ln_attn_gain": jnp.clip(1.0 + 0.18 * jax.random.normal(seeds[3], (D,), jnp.float32), 0.1, 1.9),
        "ln_attn_bias": centred(seeds[4], (D,), 0.3, 1.75, (), jnp.float32),
        "w_query": centred(seeds[5], (D, D), D ** -0.5, 0.1875, ((0, 32),)),
        "query_bias": centred(seeds[6], (D,), 0.5, 3.0, (), jnp.float32),
        "w_key": centred(seeds[7], (D, D), D ** -0.5, 0.1875, ((0, 32),)),
        "w_value": centred(seeds[8], (D, D), D ** -0.5, 0.1875, ((0, 32),)),
        "value_bias": centred(seeds[9], (D,), 0.5, 3.0, (), jnp.float32),
        "head_scale": jnp.clip(jnp.exp(jax.random.uniform(seeds[10], (H,), jnp.float32, math.log(0.3), math.log(3.0))), 0.3, 3.0),
        "w_out": centred(seeds[11], (D, D), D ** -0.5, 0.1875, ((0, 32),)),
        "out_bias": centred(seeds[12], (D,), 0.5, 3.0, (), jnp.float32),
        "post_gain": jnp.clip(1.0 + 0.18 * jax.random.normal(seeds[13], (D,), jnp.float32), 0.1, 1.9),
        "post_bias": centred(seeds[14], (D,), 0.3, 1.75, (), jnp.float32),
        "ffn_gain": jnp.clip(1.0 + 0.18 * jax.random.normal(seeds[15], (D,), jnp.float32), 0.1, 1.9),
        "ffn_bias": centred(seeds[16], (D,), 0.3, 1.75, (), jnp.float32),
        "w_up": draw_w_up(jax.random.fold_in(seeds[23], 71), 0),
        "up_bias": centred(seeds[18], (FF,), 0.5, 3.0, (), jnp.float32),
        "mid_gain": jnp.clip(1.0 + 0.18 * jax.random.normal(seeds[19], (FF,), jnp.float32), 0.1, 1.9),
        "mid_bias": centred(seeds[20], (FF,), 0.3, 1.75, (), jnp.float32),
        "w_down": centred(seeds[21], (D, FF), FF ** -0.5, 0.09375, ((0, 4), (1, 8))),
        "down_bias": centred(seeds[22], (D,), 0.5, 3.0, (), jnp.float32),
    }


@jax.custom_vjp
def low(v):
    return lax.optimization_barrier(v.astype(jnp.bfloat16)).astype(jnp.float32)

@jax.custom_vjp
def low_back(v):
    return v

def low_keep(v):
    return (low(v), None)

def low_pass(kept, grad):
    return (grad,)

def back_keep(v):
    return (v, None)

def back_low(kept, grad):
    return (low(grad),)
low.defvjp(low_keep, low_pass)
low_back.defvjp(back_keep, back_low)
HIGHEST_PRECISION = lax.Precision.HIGHEST
epsilon = 1e-05

def layer_norm(values, gain, shift):
    center = lax.optimization_barrier(jnp.mean(values, axis=-1, keepdims=True))
    centered = values - center
    spread = lax.optimization_barrier(jnp.mean(centered * centered, axis=-1, keepdims=True))
    return centered * lax.rsqrt(spread + epsilon) * gain + shift

def project(values, weight):
    return jnp.einsum('gtd,de->gte', values, weight, precision=HIGHEST_PRECISION)

def layer_group(inputs, lengths_group, params):
    ln_attn_gain, ln_attn_bias, w_query, query_bias, w_key, w_value, value_bias, head_scale, w_out, out_bias, post_gain, post_bias, ffn_gain, ffn_bias, w_up, up_bias, mid_gain, mid_bias, w_down, down_bias = params
    groups, seq_len, width = inputs.shape
    head_count = head_scale.shape[0]
    head_size = width // head_count
    positions = jnp.arange(seq_len)
    heads_shape = (groups, seq_len, head_count, head_size)
    normed = low(layer_norm(inputs, ln_attn_gain, ln_attn_bias))
    queries = low(low_back(project(normed, w_query) + query_bias)).reshape(heads_shape)
    key_rows = low(low_back(project(normed, w_key))).reshape(heads_shape)
    value_rows = low(low_back(project(normed, w_value) + value_bias)).reshape(heads_shape)
    scores = jnp.einsum('gqhd,gkhd->ghqk', queries, key_rows, precision=HIGHEST_PRECISION) * head_size ** (-0.5)
    scores = low_back(scores)
    allowed = (positions[None, :] <= positions[:, None])[None, None] & (positions[None, None, None, :] < lengths_group[:, None, None, None])
    scores = jnp.where(allowed, scores, -1e+30)
    probs = low(jax.nn.softmax(scores, axis=-1))
    context = low_back(jnp.einsum('ghqk,gkhd->gqhd', probs, value_rows, precision=HIGHEST_PRECISION))
    scaled = low((context * head_scale[:, None]).reshape(groups, seq_len, width))
    projected = low_back(project(scaled, w_out) + out_bias)
    mixed = inputs + layer_norm(projected, post_gain, post_bias)
    second = low(layer_norm(mixed, ffn_gain, ffn_bias))
    pre_act = low_back(project(second, w_up) + up_bias)
    activated = jax.nn.gelu(pre_act, approximate=False)
    row_mean = lax.optimization_barrier(jnp.mean(activated, axis=-1, keepdims=True))
    spread = lax.optimization_barrier(jnp.mean(activated * activated, axis=-1, keepdims=True)) - row_mean * row_mean
    middle = low((activated - row_mean) * lax.rsqrt(spread + epsilon) * mid_gain + mid_bias)
    branch = low_back(jnp.einsum('gtf,df->gtd', middle, w_down, precision=HIGHEST_PRECISION) + down_bias)
    combined = mixed + branch
    valid_rows = positions[None, :] < lengths_group[:, None]
    return jnp.where(valid_rows[..., None], combined, 0.0)
checked_group = jax.checkpoint(layer_group)

def reference(tokens, lengths, cotangent, ln_attn_gain, ln_attn_bias, w_query, query_bias, w_key, w_value, value_bias, head_scale, w_out, out_bias, post_gain, post_bias, ffn_gain, ffn_bias, w_up, up_bias, mid_gain, mid_bias, w_down, down_bias):
    params = tuple((item.astype(jnp.float32) for item in (ln_attn_gain, ln_attn_bias, w_query, query_bias, w_key, w_value, value_bias, head_scale, w_out, out_bias, post_gain, post_bias, ffn_gain, ffn_bias, w_up, up_bias, mid_gain, mid_bias, w_down, down_bias)))
    seq_count = lengths.shape[0]
    width = tokens.shape[1]
    seq_len = tokens.shape[0] // seq_count
    group = math.gcd(seq_count, max(1, 4096 // seq_len))
    steps_count = seq_count // group
    inputs = tokens.astype(jnp.float32).reshape(steps_count, group, seq_len, width)
    lengths_grouped = lengths.astype(jnp.int32).reshape(steps_count, group)

    def forward(inputs_all, params_all):

        def one_group(pair):
            return checked_group(pair[0], pair[1], params_all)
        return lax.map(one_group, (inputs_all, lengths_grouped))
    combined, pullback = jax.vjp(forward, inputs, params)
    grad_inputs, grads = pullback(cotangent.astype(jnp.float32).reshape(steps_count, group, seq_len, width))
    return (combined.reshape(-1, width), grad_inputs.reshape(-1, width), grads[0], grads[1], grads[2], grads[3], grads[4], grads[5], grads[6], grads[7], grads[8], grads[9], grads[10], grads[11], grads[12], grads[13], grads[14], grads[15], grads[16], grads[17], grads[18], grads[19])
```

```python
import functools
import math

import jax
import jax.numpy as jnp
from jax import lax
from jax.experimental import pallas as pl
from jax.experimental.pallas import tpu as pltpu
from jax.sharding import PartitionSpec as P

epsilon = 1e-05
masked_score = -1e30
F32 = jnp.float32
BF16 = jnp.bfloat16
MIB = 1 << 20
BOTH = ("rows", "ffn")


def dot_nn(left, right):
    return lax.dot_general(left, right, (((1,), (0,)), ((), ())), preferred_element_type=F32)


def dot_nt(left, right):
    return lax.dot_general(left, right, (((1,), (1,)), ((), ())), preferred_element_type=F32)


def dot_tn(left, right):
    return lax.dot_general(left, right, (((0,), (0,)), ((), ())), preferred_element_type=F32)


def params(limit=56 * MIB, **kw):
    return pltpu.CompilerParams(vmem_limit_bytes=limit, **kw)


def whole(shape):
    return pl.BlockSpec(shape, lambda *_: (0,) * len(shape), pipeline_mode=pl.Buffered(1))


def out_whole(shape):
    return pl.BlockSpec(shape, lambda *_: (0,) * len(shape))


def sds(shape, dtype):
    return jax.ShapeDtypeStruct(shape, dtype)


def norm_parts(values):
    center = jnp.mean(values, axis=-1, keepdims=True)
    centered = values - center
    spread = jnp.mean(centered * centered, axis=-1, keepdims=True)
    inverse = lax.rsqrt(spread + epsilon)
    return centered * inverse, inverse


def norm_back(grad_hat, hat, inverse):
    return (
        grad_hat
        - jnp.mean(grad_hat, axis=-1, keepdims=True)
        - hat * jnp.mean(grad_hat * hat, axis=-1, keepdims=True)
    ) * inverse


def col_sum(values):
    return jnp.sum(values, axis=0, keepdims=True)


def qkv_kernel(x_ref, gain_ref, bias_ref, wq_ref, qb_ref, wk_ref, wv_ref, vb_ref, h_ref, q_ref, k_ref, v_ref, *, factor):
    hat, _ = norm_parts(x_ref[...].astype(F32))
    h = (hat * gain_ref[...] + bias_ref[...]).astype(BF16)
    h_ref[...] = h
    queries = (dot_nn(h, wq_ref[...]) + qb_ref[...]).astype(BF16)
    q_ref[...] = (queries.astype(F32) * factor).astype(BF16)
    k_ref[...] = dot_nn(h, wk_ref[...]).astype(BF16)
    v_ref[...] = (dot_nn(h, wv_ref[...]) + vb_ref[...]).astype(BF16)


def project_qkv(x, gain, bias, wq, qb, wk, wv, vb, factor, block):
    seq, width = x.shape
    rows = pl.BlockSpec((block, width), lambda i: (i, 0))
    vec = whole((1, width))
    mat = whole((width, width))
    return pl.pallas_call(
        functools.partial(qkv_kernel, factor=factor),
        grid=(seq // block,),
        in_specs=[rows, vec, vec, mat, vec, mat, mat, vec],
        out_specs=[rows] * 4,
        out_shape=[sds((seq, width), BF16)] * 4,
        compiler_params=params(),
        cost_estimate=pl.CostEstimate(
            flops=6 * seq * width * width, bytes_accessed=16 * seq * width, transcendentals=0
        ),
        name="project_qkv",
    )(x, gain, bias, wq, qb, wk, wv, vb)


def attend_kernel(length_ref, scale_ref, q_ref, k_ref, v_ref, c_ref, lse_ref, *, block, head):
    pair = pl.program_id(0)
    seq, lanes = q_ref.shape
    length = length_ref[0]
    lane = lax.broadcasted_iota(jnp.int32, (block, lanes), 1)
    for i in range(seq // block):
        keys_here = (i + 1) * block
        rows = slice(i * block, (i + 1) * block)
        q = q_ref[rows, :]
        k = k_ref[:keys_here, :]
        v = v_ref[:keys_here, :]
        key_pos = lax.broadcasted_iota(jnp.int32, (block, keys_here), 1)
        row_pos = lax.broadcasted_iota(jnp.int32, (block, keys_here), 0) + i * block
        allowed = key_pos < jnp.minimum(row_pos + 1, length)
        ctx = None
        totals = []
        for n in range(2):
            mine = (lane < head) if n == 0 else (lane >= head)
            scores = dot_nt(jnp.where(mine, q, 0), k)
            scores = jnp.where(allowed, scores, masked_score)
            peak = jnp.max(scores, axis=-1, keepdims=True)
            weights = jnp.exp(scores - peak)
            total = jnp.sum(weights, axis=-1, keepdims=True)
            part = dot_nn(weights.astype(BF16), v) * (scale_ref[2 * pair + n] / total)
            ctx = part if n == 0 else jnp.where(lane < head, ctx, part)
            totals.append(peak + jnp.log(total))
        c_ref[rows, :] = ctx.astype(BF16)
        lse_ref[0, rows, :] = jnp.where(lane < head, totals[0], totals[1])


def attend_forward(length, scale, q, k, v, block, head):
    seq, width = q.shape
    lanes = 2 * head
    cols = pl.BlockSpec((seq, lanes), lambda p: (0, p))
    smem = pl.BlockSpec(memory_space=pltpu.SMEM)
    pairs = width // lanes
    return pl.pallas_call(
        functools.partial(attend_kernel, block=block, head=head),
        grid=(pairs,),
        in_specs=[smem, smem, cols, cols, cols],
        out_specs=[cols, pl.BlockSpec((1, seq, lanes), lambda p: (p, 0, 0))],
        out_shape=[sds((seq, width), BF16), sds((pairs, seq, lanes), F32)],
        compiler_params=params(),
        cost_estimate=pl.CostEstimate(
            flops=8 * seq * seq * width, bytes_accessed=12 * seq * width, transcendentals=seq * seq * 16
        ),
        name="attend_forward",
    )(length, scale, q, k, v)


def attend_back_kernel(
    length_ref, q_ref, k_ref, v_ref, g_ref, lse_ref, inner_ref, dq_ref, dk_ref, dv_ref, dq_s, *, block, head, factor
):
    seq, lanes = q_ref.shape
    length = length_ref[0]
    lane_q = lax.broadcasted_iota(jnp.int32, (seq, lanes), 1)
    dq_s[...] = jnp.zeros_like(dq_s)
    q_all = q_ref[...]
    g_all = g_ref[...]
    zero = jnp.zeros_like(q_all)
    q_heads = [jnp.where(lane_q < head, q_all, zero), jnp.where(lane_q >= head, q_all, zero)]
    g_heads = [jnp.where(lane_q < head, g_all, zero), jnp.where(lane_q >= head, g_all, zero)]
    for j in range(seq // block):
        start = j * block
        width = seq - start
        k = k_ref[start : start + block, :]
        v = v_ref[start : start + block, :]
        key_pos = lax.broadcasted_iota(jnp.int32, (block, width), 0) + start
        row_pos = lax.broadcasted_iota(jnp.int32, (block, width), 1) + start
        allowed = (key_pos <= row_pos) & (key_pos < length)
        dk = dv = None
        dqs = []
        for n in range(2):
            q = q_heads[n][start:, :]
            g = g_heads[n][start:, :]
            scores = dot_nt(k, q)
            probs = jnp.where(allowed, jnp.exp(scores - lse_ref[0, n : n + 1, start:]), 0.0)
            grad_probs = dot_nt(v, g)
            grad_scores = (probs * (grad_probs - inner_ref[0, n : n + 1, start:])).astype(BF16)
            dv_part = dot_nn(probs.astype(BF16), g)
            dk_part = dot_nn(grad_scores, q)
            dv = dv_part if n == 0 else dv + dv_part
            dk = dk_part if n == 0 else dk + dk_part
            dqs.append(dot_tn(grad_scores, k))
        dq_s[start:, :] += jnp.where(lane_q[start:, :] < head, dqs[0], dqs[1])
        dk_ref[start : start + block, :] = dk.astype(BF16)
        dv_ref[start : start + block, :] = dv.astype(BF16)
    dq_ref[...] = (dq_s[...] * factor).astype(BF16)


def attend_backward(length, q, k, v, g, lse_rows, inner_rows, block, head, factor):
    seq, width = q.shape
    lanes = 2 * head
    cols = pl.BlockSpec((seq, lanes), lambda p: (0, p))
    smem = pl.BlockSpec(memory_space=pltpu.SMEM)
    pairs = width // lanes
    rowspec = pl.BlockSpec((1, 2, seq), lambda p: (p, 0, 0))
    return pl.pallas_call(
        functools.partial(attend_back_kernel, block=block, head=head, factor=factor),
        grid=(pairs,),
        in_specs=[smem, cols, cols, cols, cols, rowspec, rowspec],
        out_specs=[cols] * 3,
        out_shape=[sds((seq, width), BF16)] * 3,
        scratch_shapes=[pltpu.VMEM((seq, lanes), F32)],
        compiler_params=params(),
        cost_estimate=pl.CostEstimate(
            flops=20 * seq * seq * width, bytes_accessed=16 * seq * width, transcendentals=seq * seq * 16
        ),
        name="attend_backward",
    )(length, q, k, v, g, lse_rows, inner_rows)


def out_kernel(c_ref, w_ref, ob_ref, x_ref, pg_ref, pb_ref, fg_ref, fb_ref, o_ref, x2_ref, h2_ref):
    o = dot_nn(c_ref[...], w_ref[...]) + ob_ref[...]
    o_ref[...] = o
    hat, _ = norm_parts(o)
    x2 = x_ref[...].astype(F32) + (hat * pg_ref[...] + pb_ref[...])
    x2_ref[...] = x2
    hat2, _ = norm_parts(x2)
    h2_ref[...] = (hat2 * fg_ref[...] + fb_ref[...]).astype(BF16)


def out_forward(c, w, ob, x, pg, pb, fg, fb, block):
    seq, width = c.shape
    rows = pl.BlockSpec((block, width), lambda i: (i, 0))
    vec = whole((1, width))
    return pl.pallas_call(
        out_kernel,
        grid=(seq // block,),
        in_specs=[rows, whole((width, width)), vec, rows, vec, vec, vec, vec],
        out_specs=[rows] * 3,
        out_shape=[sds((seq, width), F32), sds((seq, width), F32), sds((seq, width), BF16)],
        compiler_params=params(),
        cost_estimate=pl.CostEstimate(flops=2 * seq * width * width, bytes_accessed=16 * seq * width, transcendentals=0),
        name="out_forward",
    )(c, w, ob, x, pg, pb, fg, fb)


def ffn_kernel(
    length_ref, h2_ref, ct_ref, x2_ref, wup_ref, wdn_ref, ub_ref, mg_ref, mb_ref, db_ref,
    res_ref, dh2_ref, m_ref, du_ref, gub_ref, gmg_ref, gmb_ref, gdb_ref,
    e_s, gp_s, dm_s,
):
    step = pl.program_id(0)
    block, width = h2_ref.shape
    nb, _, hb = wup_ref.shape
    units = nb * hb
    row = lax.broadcasted_iota(jnp.int32, (block, width), 0) + step * block
    valid = row < length_ref[0]
    h2 = h2_ref[...]
    dfr = jnp.where(valid, ct_ref[...].astype(F32), 0.0).astype(BF16)

    @pl.when(step == 0)
    def _():
        gub_ref[...] = jnp.zeros_like(gub_ref)
        gmg_ref[...] = jnp.zeros_like(gmg_ref)
        gmb_ref[...] = jnp.zeros_like(gmb_ref)
        gdb_ref[...] = jnp.zeros_like(gdb_ref)

    gdb_ref[...] += col_sum(dfr.astype(F32))

    def first(j, sums):
        u = dot_nn(h2, wup_ref[j]) + ub_ref[j]
        dm = dot_nn(dfr, wdn_ref[j])
        cdf = 0.5 * (1.0 + lax.erf(u * math.sqrt(0.5)))
        e = u * cdf
        gp = cdf + u * (jnp.exp(u * u * -0.5) * (1.0 / math.sqrt(2.0 * math.pi)))
        dmh = dm * mg_ref[j]
        e_s[j] = e
        gp_s[j] = gp
        dm_s[j] = dm
        terms = (e, e * e, dmh, dmh * e)
        return tuple(s + jnp.sum(t, axis=-1, keepdims=True) for s, t in zip(sums, terms))

    zero = jnp.zeros((block, 1), F32)
    sum_e, sum_ee, sum_d, sum_de = lax.fori_loop(0, nb, first, (zero,) * 4)
    mu = sum_e / units
    inverse = lax.rsqrt(sum_ee / units - mu * mu + epsilon)
    mean_d = sum_d / units
    mean_dh = (sum_de - mu * sum_d) * inverse / units

    def second(j, sums):
        f, dh2 = sums
        ehat = (e_s[j] - mu) * inverse
        dm = dm_s[j]
        m = (ehat * mg_ref[j] + mb_ref[j]).astype(BF16)
        m_ref[j] = m
        f = f + dot_nt(m, wdn_ref[j])
        de = (dm * mg_ref[j] - mean_d - ehat * mean_dh) * inverse
        du = (de * gp_s[j]).astype(BF16)
        du_ref[j] = du
        dh2 = dh2 + dot_nt(du, wup_ref[j])
        gub_ref[j] += col_sum(du.astype(F32))
        gmg_ref[j] += col_sum(dm * ehat)
        gmb_ref[j] += col_sum(dm)
        return f, dh2

    zeros = jnp.zeros((block, width), F32)
    f, dh2 = lax.fori_loop(0, nb, second, (zeros, zeros))
    res_ref[...] = jnp.where(valid, x2_ref[...] + f + db_ref[...], 0.0)
    dh2_ref[...] = dh2


def feed_forward(length, h2, ct, x2, wup, wdn, ub, mg, mb, db, block):
    seq, width = h2.shape
    nb, _, hb = wup.shape
    rows = pl.BlockSpec((block, width), lambda i: (i, 0))
    smem = pl.BlockSpec(memory_space=pltpu.SMEM)
    units = whole((nb, 1, hb))
    blocks = pl.BlockSpec((nb, block, hb), lambda i: (0, i, 0))
    sums = out_whole((nb, 1, hb))
    return pl.pallas_call(
        ffn_kernel,
        grid=(seq // block,),
        in_specs=[
            smem, rows, rows, rows, whole((nb, width, hb)), whole((nb, width, hb)),
            units, units, units, whole((1, width)),
        ],
        out_specs=[rows, rows, blocks, blocks, sums, sums, sums, out_whole((1, width))],
        out_shape=[
            sds((seq, width), F32), sds((seq, width), F32), sds((nb, seq, hb), BF16), sds((nb, seq, hb), BF16),
            sds((nb, 1, hb), F32), sds((nb, 1, hb), F32), sds((nb, 1, hb), F32), sds((1, width), F32),
        ],
        scratch_shapes=[pltpu.VMEM((nb, block, hb), F32)] * 3,
        compiler_params=params(60 * MIB),
        cost_estimate=pl.CostEstimate(
            flops=16 * seq * width * nb * hb, bytes_accessed=60 * MIB, transcendentals=2 * seq * nb * hb
        ),
        name="feed_forward",
    )(length, h2, ct, x2, wup, wdn, ub, mg, mb, db)


def ffn_weights_kernel(length_ref, h2_ref, ct_ref, m_ref, du_ref, gup_ref, gdn_ref, h2t_s, dft_s):
    seq, width = h2_ref.shape

    @pl.when(pl.program_id(0) == 0)
    def _():
        row = lax.broadcasted_iota(jnp.int32, (seq, width), 0)
        dfr = jnp.where(row < length_ref[0], ct_ref[...], 0)
        h2t_s[...] = h2_ref[...].T
        dft_s[...] = dfr.T

    gdn_ref[0] = dot_nn(dft_s[...], m_ref[0]).astype(BF16)
    gup_ref[0] = dot_nn(h2t_s[...], du_ref[0]).astype(BF16)


def ffn_weight_grads(length, h2, ct, m, du):
    seq, width = h2.shape
    nb, _, hb = m.shape
    smem = pl.BlockSpec(memory_space=pltpu.SMEM)
    block = pl.BlockSpec((1, seq, hb), lambda j: (j, 0, 0))
    out = pl.BlockSpec((1, width, hb), lambda j: (j, 0, 0))
    return pl.pallas_call(
        ffn_weights_kernel,
        grid=(nb,),
        in_specs=[smem, whole((seq, width)), whole((seq, width)), block, block],
        out_specs=[out, out],
        out_shape=[sds((nb, width, hb), BF16)] * 2,
        scratch_shapes=[pltpu.VMEM((width, seq), BF16)] * 2,
        compiler_params=params(),
        cost_estimate=pl.CostEstimate(
            flops=4 * seq * width * nb * hb, bytes_accessed=36 * MIB, transcendentals=0
        ),
        name="ffn_weight_grads",
    )(length, h2, ct, m, du)


def out_back_kernel(
    length_ref, dh2_ref, ct_ref, x2_ref, o_ref, c_ref, w_ref, fg_ref, pg_ref, hs_ref,
    dx2_ref, dor_ref, g_ref, dcc_ref, gfg_ref, gfb_ref, gpg_ref, gpb_ref, gob_ref,
):
    step = pl.program_id(0)
    block, width = dh2_ref.shape
    row = lax.broadcasted_iota(jnp.int32, (block, width), 0) + step * block
    dy = jnp.where(row < length_ref[0], ct_ref[...].astype(F32), 0.0)

    @pl.when(step == 0)
    def _():
        for ref in (gfg_ref, gfb_ref, gpg_ref, gpb_ref, gob_ref):
            ref[...] = jnp.zeros_like(ref)

    dh2 = dh2_ref[...]
    hat2, inverse2 = norm_parts(x2_ref[...])
    gfg_ref[...] += col_sum(dh2 * hat2)
    gfb_ref[...] += col_sum(dh2)
    dx2 = dy + norm_back(dh2 * fg_ref[...], hat2, inverse2)
    dx2_ref[...] = dx2
    hat, inverse = norm_parts(o_ref[...])
    gpg_ref[...] += col_sum(dx2 * hat)
    gpb_ref[...] += col_sum(dx2)
    dor = norm_back(dx2 * pg_ref[...], hat, inverse).astype(BF16)
    dor_ref[...] = dor
    gob_ref[...] += col_sum(dor.astype(F32))
    dc = dot_nt(dor, w_ref[...])
    g_ref[...] = (dc * hs_ref[...]).astype(BF16)
    dcc_ref[...] = dc * c_ref[...].astype(F32)


def out_backward(length, dh2, ct, x2, o, c, w, fg, pg, hs, block):
    seq, width = dh2.shape
    rows = pl.BlockSpec((block, width), lambda i: (i, 0))
    smem = pl.BlockSpec(memory_space=pltpu.SMEM)
    vec = whole((1, width))
    ovec = out_whole((1, width))
    return pl.pallas_call(
        out_back_kernel,
        grid=(seq // block,),
        in_specs=[smem, rows, rows, rows, rows, rows, whole((width, width)), vec, vec, vec],
        out_specs=[rows] * 4 + [ovec] * 5,
        out_shape=[
            sds((seq, width), F32), sds((seq, width), BF16), sds((seq, width), BF16), sds((seq, width), F32),
        ] + [sds((1, width), F32)] * 5,
        compiler_params=params(),
        cost_estimate=pl.CostEstimate(flops=2 * seq * width * width, bytes_accessed=30 * seq * width, transcendentals=0),
        name="out_backward",
    )(length, dh2, ct, x2, o, c, w, fg, pg, hs)


def weights_kernel(left_ref, right_ref, out_ref, left_s):
    @pl.when(pl.program_id(0) == 0)
    def _():
        left_s[...] = left_ref[...].T

    out_ref[...] = dot_nn(left_s[...], right_ref[...]).astype(BF16)


def weight_grad(left, right, block):
    seq, width = left.shape
    cols = right.shape[1]
    return pl.pallas_call(
        weights_kernel,
        grid=(cols // block,),
        in_specs=[whole((seq, width)), pl.BlockSpec((seq, block), lambda j: (0, j))],
        out_specs=pl.BlockSpec((width, block), lambda j: (0, j)),
        out_shape=sds((width, cols), BF16),
        scratch_shapes=[pltpu.VMEM((width, seq), BF16)],
        compiler_params=params(),
        cost_estimate=pl.CostEstimate(flops=2 * seq * width * cols, bytes_accessed=6 * seq * cols, transcendentals=0),
        name="weight_grad",
    )(left, right)


def input_kernel(
    dq_ref, dk_ref, dv_ref, wq_ref, wk_ref, wv_ref, x_ref, dx2_ref, gain_ref,
    dx_ref, gg_ref, gb_ref, gqb_ref, gvb_ref,
):
    @pl.when(pl.program_id(0) == 0)
    def _():
        for ref in (gg_ref, gb_ref, gqb_ref, gvb_ref):
            ref[...] = jnp.zeros_like(ref)

    dq, dk, dv = dq_ref[...], dk_ref[...], dv_ref[...]
    dh = dot_nt(dq, wq_ref[...]) + dot_nt(dk, wk_ref[...]) + dot_nt(dv, wv_ref[...])
    hat, inverse = norm_parts(x_ref[...].astype(F32))
    gg_ref[...] += col_sum(dh * hat)
    gb_ref[...] += col_sum(dh)
    gqb_ref[...] += col_sum(dq.astype(F32))
    gvb_ref[...] += col_sum(dv.astype(F32))
    dx_ref[...] = dx2_ref[...] + norm_back(dh * gain_ref[...], hat, inverse)


def input_grad(dq, dk, dv, wq, wk, wv, x, dx2, gain, block):
    seq, width = dq.shape
    rows = pl.BlockSpec((block, width), lambda i: (i, 0))
    mat = whole((width, width))
    ovec = out_whole((1, width))
    return pl.pallas_call(
        input_kernel,
        grid=(seq // block,),
        in_specs=[rows, rows, rows, mat, mat, mat, rows, rows, whole((1, width))],
        out_specs=[rows] + [ovec] * 4,
        out_shape=[sds((seq, width), F32)] + [sds((1, width), F32)] * 4,
        compiler_params=params(),
        cost_estimate=pl.CostEstimate(flops=6 * seq * width * width, bytes_accessed=22 * seq * width, transcendentals=0),
        name="input_grad",
    )(dq, dk, dv, wq, wk, wv, x, dx2, gain)


def gather_rows(parts):
    n = len(parts)
    width = parts[0].shape[1]
    whole_rows = lax.all_gather(jnp.concatenate(parts, axis=1), BOTH, axis=0, tiled=True)
    return [whole_rows[:, i * width : (i + 1) * width] for i in range(n)]


def gather_blocks(shard):
    over_ffn = lax.all_gather(shard, "ffn", axis=0, tiled=False)
    return lax.all_gather(over_ffn, "rows", axis=1, tiled=True)


def widen(blocks, lanes):
    nb, rows, hb = blocks.shape
    group = max(1, lanes // hb)
    if group == 1:
        return blocks
    return blocks.reshape(nb // group, group, rows, hb).transpose(0, 2, 1, 3).reshape(nb // group, rows, group * hb)


def narrow(blocks, hb):
    nb, rows, lanes = blocks.shape
    group = lanes // hb
    if group == 1:
        return blocks
    return blocks.reshape(nb, rows, group, hb).transpose(0, 2, 1, 3).reshape(nb * group, rows, hb)


def scatter_blocks(grad):
    mine = lax.psum_scatter(grad, "rows", scatter_dimension=1, tiled=True)
    return lax.psum_scatter(mine, "ffn", scatter_dimension=0, tiled=False).astype(F32)


def rows_of(vector):
    return vector.reshape(1, -1)


def shards(
    tokens, lengths, cotangent, ln_attn_gain, ln_attn_bias, w_query, query_bias, w_key, w_value, value_bias,
    head_scale, w_out, out_bias, post_gain, post_bias, ffn_gain, ffn_bias, w_up, up_bias, mid_gain, mid_bias,
    w_down, down_bias,
):
    seq, width = tokens.shape
    heads = head_scale.shape[0]
    head = width // heads
    factor = head ** (-0.5)
    block = min(seq, 256)
    wq, wk, wv, wo = gather_rows([w_query, w_key, w_value, w_out])
    own_units = w_up.shape[1]
    wup = widen(gather_blocks(w_up), 512)
    wdn = widen(gather_blocks(w_down), 512)
    nb, _, hb = wup.shape
    h, q, k, v = project_qkv(
        tokens, rows_of(ln_attn_gain), rows_of(ln_attn_bias), wq, rows_of(query_bias), wk, wv, rows_of(value_bias),
        factor, block,
    )
    c, lse = attend_forward(lengths, head_scale, q, k, v, block, head)
    o, x2, h2 = out_forward(
        c, wo, rows_of(out_bias), tokens, rows_of(post_gain), rows_of(post_bias), rows_of(ffn_gain),
        rows_of(ffn_bias), block,
    )
    units = lambda vector: vector.reshape(nb, 1, hb)
    result, dh2, m, du, g_ub, g_mg, g_mb, g_db = feed_forward(
        lengths, h2, cotangent, x2, wup, wdn, units(up_bias), units(mid_gain), units(mid_bias), rows_of(down_bias),
        block,
    )
    g_up, g_dn = ffn_weight_grads(lengths, h2, cotangent, m, du)
    scale_cols = rows_of(jnp.repeat(head_scale, head))
    dx2, dor, g, dcc, g_fg, g_fb, g_pg, g_pb, g_ob = out_backward(
        lengths, dh2, cotangent, x2, o, c, wo, rows_of(ffn_gain), rows_of(post_gain), scale_cols, block
    )
    inner = jnp.sum(dcc.reshape(seq, heads, head), axis=-1)
    g_hs = jnp.sum(inner, axis=0) / head_scale
    inner_rows = inner.T.reshape(heads // 2, 2, seq)
    lse_rows = jnp.stack([lse[:, :, 0], lse[:, :, head]], axis=1)
    dq, dk, dv = attend_backward(lengths, q, k, v, g, lse_rows, inner_rows, block, head, factor)
    g_wo = weight_grad(c, dor, 512)
    g_wq, g_wk, g_wv = (weight_grad(h, part, 512) for part in (dq, dk, dv))
    dx, g_lg, g_lb, g_qb, g_vb = input_grad(dq, dk, dv, wq, wk, wv, tokens, dx2, rows_of(ln_attn_gain), block)
    grad_up = scatter_blocks(narrow(g_up, own_units))
    grad_down = scatter_blocks(narrow(g_dn, own_units))
    stacked = narrow(jnp.concatenate([g_ub, g_mg, g_mb], axis=1), own_units)
    stacked = lax.psum(lax.psum_scatter(stacked, "ffn", scatter_dimension=0, tiled=False), "rows")
    attn = lax.psum_scatter(
        jnp.concatenate([g_wq, g_wk, g_wv, g_wo], axis=1), BOTH, scatter_dimension=0, tiled=True
    ).astype(F32)
    small = jnp.concatenate(
        [g_lg, g_lb, g_qb, g_vb, g_ob, g_pg, g_pb, g_fg, g_fb, g_db, jnp.pad(rows_of(g_hs), ((0, 0), (0, width - heads)))],
        axis=0,
    )
    small = lax.psum(small, BOTH)
    return (
        result, dx, small[0], small[1], attn[:, :width], small[2], attn[:, width : 2 * width],
        attn[:, 2 * width : 3 * width], small[3], small[10, :heads], attn[:, 3 * width :], small[4], small[5],
        small[6], small[7], small[8], grad_up, stacked[0], stacked[1], stacked[2], grad_down, small[9],
    )


def solution(mesh):
    split = P(BOTH, None)
    tiles = P("rows", "ffn")
    one = P()
    return jax.shard_map(
        shards,
        mesh=mesh,
        in_specs=(
            split, P(BOTH), split, one, one, split, one, split, split, one, one, split, one, one, one, one, one,
            tiles, one, one, one, tiles, one,
        ),
        out_specs=(
            split, split, one, one, split, one, split, split, one, one, split, one, one, one, one, one,
            tiles, P("ffn"), P("ffn"), P("ffn"), tiles, one,
        ),
        check_vma=False,
    )
```

```python
import functools
import math

import jax
import jax.numpy as jnp
from jax import lax
from jax.experimental import pallas as pl
from jax.experimental.pallas import tpu as pltpu
from jax.sharding import PartitionSpec as P

epsilon = 1e-05
masked_score = -1e30
F32 = jnp.float32
BF16 = jnp.bfloat16
MIB = 1 << 20
BOTH = ("rows", "ffn")


def dot_nn(left, right):
    return lax.dot_general(left, right, (((1,), (0,)), ((), ())), preferred_element_type=F32)


def dot_nt(left, right):
    return lax.dot_general(left, right, (((1,), (1,)), ((), ())), preferred_element_type=F32)


def dot_tn(left, right):
    return lax.dot_general(left, right, (((0,), (0,)), ((), ())), preferred_element_type=F32)


def params(limit=56 * MIB, **kw):
    return pltpu.CompilerParams(vmem_limit_bytes=limit, **kw)


def whole(shape):
    return pl.BlockSpec(shape, lambda *_: (0,) * len(shape), pipeline_mode=pl.Buffered(1))


def out_whole(shape):
    return pl.BlockSpec(shape, lambda *_: (0,) * len(shape))


def sds(shape, dtype):
    return jax.ShapeDtypeStruct(shape, dtype)


def norm_parts(values):
    center = jnp.mean(values, axis=-1, keepdims=True)
    centered = values - center
    spread = jnp.mean(centered * centered, axis=-1, keepdims=True)
    inverse = lax.rsqrt(spread + epsilon)
    return centered * inverse, inverse


def norm_back(grad_hat, hat, inverse):
    return (
        grad_hat
        - jnp.mean(grad_hat, axis=-1, keepdims=True)
        - hat * jnp.mean(grad_hat * hat, axis=-1, keepdims=True)
    ) * inverse


def col_sum(values):
    return jnp.sum(values, axis=0, keepdims=True)


def qkv_kernel(x_ref, gain_ref, bias_ref, wq_ref, qb_ref, wk_ref, wv_ref, vb_ref, h_ref, q_ref, k_ref, v_ref, *, factor):
    hat, _ = norm_parts(x_ref[...].astype(F32))
    h = (hat * gain_ref[...] + bias_ref[...]).astype(BF16)
    h_ref[...] = h
    queries = (dot_nn(h, wq_ref[...]) + qb_ref[...]).astype(BF16)
    q_ref[...] = (queries.astype(F32) * factor).astype(BF16)
    k_ref[...] = dot_nn(h, wk_ref[...]).astype(BF16)
    v_ref[...] = (dot_nn(h, wv_ref[...]) + vb_ref[...]).astype(BF16)


def project_qkv(x, gain, bias, wq, qb, wk, wv, vb, factor, block):
    seq, width = x.shape
    rows = pl.BlockSpec((block, width), lambda i: (i, 0))
    vec = whole((1, width))
    mat = whole((width, width))
    return pl.pallas_call(
        functools.partial(qkv_kernel, factor=factor),
        grid=(seq // block,),
        in_specs=[rows, vec, vec, mat, vec, mat, mat, vec],
        out_specs=[rows] * 4,
        out_shape=[sds((seq, width), BF16)] * 4,
        compiler_params=params(),
        cost_estimate=pl.CostEstimate(
            flops=6 * seq * width * width, bytes_accessed=16 * seq * width, transcendentals=0
        ),
        name="project_qkv",
    )(x, gain, bias, wq, qb, wk, wv, vb)


def attend_kernel(length_ref, scale_ref, q_ref, k_ref, v_ref, c_ref, lse_ref, *, block, head):
    pair = pl.program_id(0)
    seq, lanes = q_ref.shape
    length = length_ref[0]
    lane = lax.broadcasted_iota(jnp.int32, (block, lanes), 1)
    for i in range(seq // block):
        keys_here = (i + 1) * block
        rows = slice(i * block, (i + 1) * block)
        q = q_ref[rows, :]
        k = k_ref[:keys_here, :]
        v = v_ref[:keys_here, :]
        key_pos = lax.broadcasted_iota(jnp.int32, (block, keys_here), 1)
        row_pos = lax.broadcasted_iota(jnp.int32, (block, keys_here), 0) + i * block
        allowed = key_pos < jnp.minimum(row_pos + 1, length)
        ctx = None
        totals = []
        for n in range(2):
            mine = (lane < head) if n == 0 else (lane >= head)
            scores = dot_nt(jnp.where(mine, q, 0), k)
            scores = jnp.where(allowed, scores, masked_score)
            peak = jnp.max(scores, axis=-1, keepdims=True)
            weights = jnp.exp(scores - peak)
            total = jnp.sum(weights, axis=-1, keepdims=True)
            part = dot_nn(weights.astype(BF16), v) * (scale_ref[2 * pair + n] / total)
            ctx = part if n == 0 else jnp.where(lane < head, ctx, part)
            totals.append(peak + jnp.log(total))
        c_ref[rows, :] = ctx.astype(BF16)
        lse_ref[0, rows, :] = jnp.where(lane < head, totals[0], totals[1])


def attend_forward(length, scale, q, k, v, block, head):
    seq, width = q.shape
    lanes = 2 * head
    cols = pl.BlockSpec((seq, lanes), lambda p: (0, p))
    smem = pl.BlockSpec(memory_space=pltpu.SMEM)
    pairs = width // lanes
    return pl.pallas_call(
        functools.partial(attend_kernel, block=block, head=head),
        grid=(pairs,),
        in_specs=[smem, smem, cols, cols, cols],
        out_specs=[cols, pl.BlockSpec((1, seq, lanes), lambda p: (p, 0, 0))],
        out_shape=[sds((seq, width), BF16), sds((pairs, seq, lanes), F32)],
        compiler_params=params(),
        cost_estimate=pl.CostEstimate(
            flops=8 * seq * seq * width, bytes_accessed=12 * seq * width, transcendentals=seq * seq * 16
        ),
        name="attend_forward",
    )(length, scale, q, k, v)


def attend_back_kernel(
    length_ref, q_ref, k_ref, v_ref, g_ref, lse_ref, inner_ref, dq_ref, dk_ref, dv_ref, dq_s, *, block, head, factor
):
    seq, lanes = q_ref.shape
    length = length_ref[0]
    lane_q = lax.broadcasted_iota(jnp.int32, (seq, lanes), 1)
    dq_s[...] = jnp.zeros_like(dq_s)
    q_all = q_ref[...]
    g_all = g_ref[...]
    zero = jnp.zeros_like(q_all)
    q_heads = [jnp.where(lane_q < head, q_all, zero), jnp.where(lane_q >= head, q_all, zero)]
    g_heads = [jnp.where(lane_q < head, g_all, zero), jnp.where(lane_q >= head, g_all, zero)]
    for j in range(seq // block):
        start = j * block
        width = seq - start
        k = k_ref[start : start + block, :]
        v = v_ref[start : start + block, :]
        key_pos = lax.broadcasted_iota(jnp.int32, (block, width), 0) + start
        row_pos = lax.broadcasted_iota(jnp.int32, (block, width), 1) + start
        allowed = (key_pos <= row_pos) & (key_pos < length)
        dk = dv = None
        dqs = []
        for n in range(2):
            q = q_heads[n][start:, :]
            g = g_heads[n][start:, :]
            scores = dot_nt(k, q)
            probs = jnp.where(allowed, jnp.exp(scores - lse_ref[0, n : n + 1, start:]), 0.0)
            grad_probs = dot_nt(v, g)
            grad_scores = (probs * (grad_probs - inner_ref[0, n : n + 1, start:])).astype(BF16)
            dv_part = dot_nn(probs.astype(BF16), g)
            dk_part = dot_nn(grad_scores, q)
            dv = dv_part if n == 0 else dv + dv_part
            dk = dk_part if n == 0 else dk + dk_part
            dqs.append(dot_tn(grad_scores, k))
        dq_s[start:, :] += jnp.where(lane_q[start:, :] < head, dqs[0], dqs[1])
        dk_ref[start : start + block, :] = dk.astype(BF16)
        dv_ref[start : start + block, :] = dv.astype(BF16)
    dq_ref[...] = (dq_s[...] * factor).astype(BF16)


def attend_backward(length, q, k, v, g, lse_rows, inner_rows, block, head, factor):
    seq, width = q.shape
    lanes = 2 * head
    cols = pl.BlockSpec((seq, lanes), lambda p: (0, p))
    smem = pl.BlockSpec(memory_space=pltpu.SMEM)
    pairs = width // lanes
    rowspec = pl.BlockSpec((1, 2, seq), lambda p: (p, 0, 0))
    return pl.pallas_call(
        functools.partial(attend_back_kernel, block=block, head=head, factor=factor),
        grid=(pairs,),
        in_specs=[smem, cols, cols, cols, cols, rowspec, rowspec],
        out_specs=[cols] * 3,
        out_shape=[sds((seq, width), BF16)] * 3,
        scratch_shapes=[pltpu.VMEM((seq, lanes), F32)],
        compiler_params=params(),
        cost_estimate=pl.CostEstimate(
            flops=20 * seq * seq * width, bytes_accessed=16 * seq * width, transcendentals=seq * seq * 16
        ),
        name="attend_backward",
    )(length, q, k, v, g, lse_rows, inner_rows)


def out_kernel(c_ref, w_ref, ob_ref, x_ref, pg_ref, pb_ref, fg_ref, fb_ref, o_ref, x2_ref, h2_ref):
    o = dot_nn(c_ref[...], w_ref[...]) + ob_ref[...]
    o_ref[...] = o
    hat, _ = norm_parts(o)
    x2 = x_ref[...].astype(F32) + (hat * pg_ref[...] + pb_ref[...])
    x2_ref[...] = x2
    hat2, _ = norm_parts(x2)
    h2_ref[...] = (hat2 * fg_ref[...] + fb_ref[...]).astype(BF16)


def out_forward(c, w, ob, x, pg, pb, fg, fb, block):
    seq, width = c.shape
    rows = pl.BlockSpec((block, width), lambda i: (i, 0))
    vec = whole((1, width))
    return pl.pallas_call(
        out_kernel,
        grid=(seq // block,),
        in_specs=[rows, whole((width, width)), vec, rows, vec, vec, vec, vec],
        out_specs=[rows] * 3,
        out_shape=[sds((seq, width), F32), sds((seq, width), F32), sds((seq, width), BF16)],
        compiler_params=params(),
        cost_estimate=pl.CostEstimate(flops=2 * seq * width * width, bytes_accessed=16 * seq * width, transcendentals=0),
        name="out_forward",
    )(c, w, ob, x, pg, pb, fg, fb)


def ffn_kernel(
    length_ref, h2_ref, ct_ref, x2_ref, wup_ref, wdn_ref, ub_ref, mg_ref, mb_ref, db_ref,
    res_ref, dh2_ref, m_ref, du_ref, gub_ref, gmg_ref, gmb_ref, gdb_ref,
    e_s, gp_s, dm_s,
):
    step = pl.program_id(0)
    block, width = h2_ref.shape
    nb, _, hb = wup_ref.shape
    units = nb * hb
    row = lax.broadcasted_iota(jnp.int32, (block, width), 0) + step * block
    valid = row < length_ref[0]
    h2 = h2_ref[...]
    dfr = jnp.where(valid, ct_ref[...].astype(F32), 0.0).astype(BF16)

    @pl.when(step == 0)
    def _():
        gub_ref[...] = jnp.zeros_like(gub_ref)
        gmg_ref[...] = jnp.zeros_like(gmg_ref)
        gmb_ref[...] = jnp.zeros_like(gmb_ref)
        gdb_ref[...] = jnp.zeros_like(gdb_ref)

    gdb_ref[...] += col_sum(dfr.astype(F32))

    def first(j, sums):
        u = dot_nn(h2, wup_ref[j]) + ub_ref[j]
        dm = dot_nn(dfr, wdn_ref[j])
        cdf = 0.5 * (1.0 + lax.erf(u * math.sqrt(0.5)))
        e = u * cdf
        gp = cdf + u * (jnp.exp(u * u * -0.5) * (1.0 / math.sqrt(2.0 * math.pi)))
        dmh = dm * mg_ref[j]
        e_s[j] = e
        gp_s[j] = gp
        dm_s[j] = dm
        terms = (e, e * e, dmh, dmh * e)
        return tuple(s + jnp.sum(t, axis=-1, keepdims=True) for s, t in zip(sums, terms))

    zero = jnp.zeros((block, 1), F32)
    sum_e, sum_ee, sum_d, sum_de = lax.fori_loop(0, nb, first, (zero,) * 4)
    mu = sum_e / units
    inverse = lax.rsqrt(sum_ee / units - mu * mu + epsilon)
    mean_d = sum_d / units
    mean_dh = (sum_de - mu * sum_d) * inverse / units

    def second(j, sums):
        f, dh2 = sums
        ehat = (e_s[j] - mu) * inverse
        dm = dm_s[j]
        m = (ehat * mg_ref[j] + mb_ref[j]).astype(BF16)
        m_ref[j] = m
        f = f + dot_nt(m, wdn_ref[j])
        de = (dm * mg_ref[j] - mean_d - ehat * mean_dh) * inverse
        du = (de * gp_s[j]).astype(BF16)
        du_ref[j] = du
        dh2 = dh2 + dot_nt(du, wup_ref[j])
        gub_ref[j] += col_sum(du.astype(F32))
        gmg_ref[j] += col_sum(dm * ehat)
        gmb_ref[j] += col_sum(dm)
        return f, dh2

    zeros = jnp.zeros((block, width), F32)
    f, dh2 = lax.fori_loop(0, nb, second, (zeros, zeros))
    res_ref[...] = jnp.where(valid, x2_ref[...] + f + db_ref[...], 0.0)
    dh2_ref[...] = dh2


def feed_forward(length, h2, ct, x2, wup, wdn, ub, mg, mb, db, block):
    seq, width = h2.shape
    nb, _, hb = wup.shape
    rows = pl.BlockSpec((block, width), lambda i: (i, 0))
    smem = pl.BlockSpec(memory_space=pltpu.SMEM)
    units = whole((nb, 1, hb))
    blocks = pl.BlockSpec((nb, block, hb), lambda i: (0, i, 0))
    sums = out_whole((nb, 1, hb))
    return pl.pallas_call(
        ffn_kernel,
        grid=(seq // block,),
        in_specs=[
            smem, rows, rows, rows, whole((nb, width, hb)), whole((nb, width, hb)),
            units, units, units, whole((1, width)),
        ],
        out_specs=[rows, rows, blocks, blocks, sums, sums, sums, out_whole((1, width))],
        out_shape=[
            sds((seq, width), F32), sds((seq, width), F32), sds((nb, seq, hb), BF16), sds((nb, seq, hb), BF16),
            sds((nb, 1, hb), F32), sds((nb, 1, hb), F32), sds((nb, 1, hb), F32), sds((1, width), F32),
        ],
        scratch_shapes=[pltpu.VMEM((nb, block, hb), F32)] * 3,
        compiler_params=params(60 * MIB),
        cost_estimate=pl.CostEstimate(
            flops=16 * seq * width * nb * hb, bytes_accessed=60 * MIB, transcendentals=2 * seq * nb * hb
        ),
        name="feed_forward",
    )(length, h2, ct, x2, wup, wdn, ub, mg, mb, db)


def ffn_weights_kernel(length_ref, h2_ref, ct_ref, m_ref, du_ref, gup_ref, gdn_ref, h2t_s, dft_s):
    seq, width = h2_ref.shape

    @pl.when(pl.program_id(0) == 0)
    def _():
        row = lax.broadcasted_iota(jnp.int32, (seq, width), 0)
        dfr = jnp.where(row < length_ref[0], ct_ref[...], 0)
        h2t_s[...] = h2_ref[...].T
        dft_s[...] = dfr.T

    gdn_ref[0] = dot_nn(dft_s[...], m_ref[0]).astype(BF16)
    gup_ref[0] = dot_nn(h2t_s[...], du_ref[0]).astype(BF16)


def ffn_weight_grads(length, h2, ct, m, du):
    seq, width = h2.shape
    nb, _, hb = m.shape
    smem = pl.BlockSpec(memory_space=pltpu.SMEM)
    block = pl.BlockSpec((1, seq, hb), lambda j: (j, 0, 0))
    out = pl.BlockSpec((1, width, hb), lambda j: (j, 0, 0))
    return pl.pallas_call(
        ffn_weights_kernel,
        grid=(nb,),
        in_specs=[smem, whole((seq, width)), whole((seq, width)), block, block],
        out_specs=[out, out],
        out_shape=[sds((nb, width, hb), BF16)] * 2,
        scratch_shapes=[pltpu.VMEM((width, seq), BF16)] * 2,
        compiler_params=params(),
        cost_estimate=pl.CostEstimate(
            flops=4 * seq * width * nb * hb, bytes_accessed=36 * MIB, transcendentals=0
        ),
        name="ffn_weight_grads",
    )(length, h2, ct, m, du)


def out_back_kernel(
    length_ref, dh2_ref, ct_ref, x2_ref, o_ref, c_ref, w_ref, fg_ref, pg_ref, hs_ref,
    dx2_ref, dor_ref, g_ref, dcc_ref, gfg_ref, gfb_ref, gpg_ref, gpb_ref, gob_ref,
):
    step = pl.program_id(0)
    block, width = dh2_ref.shape
    row = lax.broadcasted_iota(jnp.int32, (block, width), 0) + step * block
    dy = jnp.where(row < length_ref[0], ct_ref[...].astype(F32), 0.0)

    @pl.when(step == 0)
    def _():
        for ref in (gfg_ref, gfb_ref, gpg_ref, gpb_ref, gob_ref):
            ref[...] = jnp.zeros_like(ref)

    dh2 = dh2_ref[...]
    hat2, inverse2 = norm_parts(x2_ref[...])
    gfg_ref[...] += col_sum(dh2 * hat2)
    gfb_ref[...] += col_sum(dh2)
    dx2 = dy + norm_back(dh2 * fg_ref[...], hat2, inverse2)
    dx2_ref[...] = dx2
    hat, inverse = norm_parts(o_ref[...])
    gpg_ref[...] += col_sum(dx2 * hat)
    gpb_ref[...] += col_sum(dx2)
    dor = norm_back(dx2 * pg_ref[...], hat, inverse).astype(BF16)
    dor_ref[...] = dor
    gob_ref[...] += col_sum(dor.astype(F32))
    dc = dot_nt(dor, w_ref[...])
    g_ref[...] = (dc * hs_ref[...]).astype(BF16)
    dcc_ref[...] = dc * c_ref[...].astype(F32)


def out_backward(length, dh2, ct, x2, o, c, w, fg, pg, hs, block):
    seq, width = dh2.shape
    rows = pl.BlockSpec((block, width), lambda i: (i, 0))
    smem = pl.BlockSpec(memory_space=pltpu.SMEM)
    vec = whole((1, width))
    ovec = out_whole((1, width))
    return pl.pallas_call(
        out_back_kernel,
        grid=(seq // block,),
        in_specs=[smem, rows, rows, rows, rows, rows, whole((width, width)), vec, vec, vec],
        out_specs=[rows] * 4 + [ovec] * 5,
        out_shape=[
            sds((seq, width), F32), sds((seq, width), BF16), sds((seq, width), BF16), sds((seq, width), F32),
        ] + [sds((1, width), F32)] * 5,
        compiler_params=params(),
        cost_estimate=pl.CostEstimate(flops=2 * seq * width * width, bytes_accessed=30 * seq * width, transcendentals=0),
        name="out_backward",
    )(length, dh2, ct, x2, o, c, w, fg, pg, hs)


def weights_kernel(left_ref, right_ref, out_ref, left_s):
    @pl.when(pl.program_id(0) == 0)
    def _():
        left_s[...] = left_ref[...].T

    out_ref[...] = dot_nn(left_s[...], right_ref[...]).astype(BF16)


def weight_grad(left, right, block):
    seq, width = left.shape
    cols = right.shape[1]
    return pl.pallas_call(
        weights_kernel,
        grid=(cols // block,),
        in_specs=[whole((seq, width)), pl.BlockSpec((seq, block), lambda j: (0, j))],
        out_specs=pl.BlockSpec((width, block), lambda j: (0, j)),
        out_shape=sds((width, cols), BF16),
        scratch_shapes=[pltpu.VMEM((width, seq), BF16)],
        compiler_params=params(),
        cost_estimate=pl.CostEstimate(flops=2 * seq * width * cols, bytes_accessed=6 * seq * cols, transcendentals=0),
        name="weight_grad",
    )(left, right)


def input_kernel(
    dq_ref, dk_ref, dv_ref, wq_ref, wk_ref, wv_ref, x_ref, dx2_ref, gain_ref,
    dx_ref, gg_ref, gb_ref, gqb_ref, gvb_ref,
):
    @pl.when(pl.program_id(0) == 0)
    def _():
        for ref in (gg_ref, gb_ref, gqb_ref, gvb_ref):
            ref[...] = jnp.zeros_like(ref)

    dq, dk, dv = dq_ref[...], dk_ref[...], dv_ref[...]
    dh = dot_nt(dq, wq_ref[...]) + dot_nt(dk, wk_ref[...]) + dot_nt(dv, wv_ref[...])
    hat, inverse = norm_parts(x_ref[...].astype(F32))
    gg_ref[...] += col_sum(dh * hat)
    gb_ref[...] += col_sum(dh)
    gqb_ref[...] += col_sum(dq.astype(F32))
    gvb_ref[...] += col_sum(dv.astype(F32))
    dx_ref[...] = dx2_ref[...] + norm_back(dh * gain_ref[...], hat, inverse)


def input_grad(dq, dk, dv, wq, wk, wv, x, dx2, gain, block):
    seq, width = dq.shape
    rows = pl.BlockSpec((block, width), lambda i: (i, 0))
    mat = whole((width, width))
    ovec = out_whole((1, width))
    return pl.pallas_call(
        input_kernel,
        grid=(seq // block,),
        in_specs=[rows, rows, rows, mat, mat, mat, rows, rows, whole((1, width))],
        out_specs=[rows] + [ovec] * 4,
        out_shape=[sds((seq, width), F32)] + [sds((1, width), F32)] * 4,
        compiler_params=params(),
        cost_estimate=pl.CostEstimate(flops=6 * seq * width * width, bytes_accessed=22 * seq * width, transcendentals=0),
        name="input_grad",
    )(dq, dk, dv, wq, wk, wv, x, dx2, gain)


class Place:
    def __init__(self, rows, ffn):
        self.rows, self.ffn, self.depth = rows, ffn, ffn // 2
        self.r = lax.axis_index("rows")
        f = lax.axis_index("ffn")
        self.z, self.c = f // 2, lax.rem(f, 2)

    def row_flip(self, r, bit):
        return r + 1 - 2 * lax.rem(r, 2) if bit == 0 else lax.rem(r + 2, 4)

    def z_at(self, d):
        return lax.rem(self.z + d + self.depth, self.depth)

    def device(self, r, z, c):
        return (r, 2 * z + c)


def remote(src, dst, send, recv, device):
    return pltpu.make_async_remote_copy(
        src_ref=src, dst_ref=dst, send_sem=send, recv_sem=recv, device_id=device, device_id_type=pl.DeviceIdType.MESH
    )


class Gather:
    def __init__(self, place, src, view, local, send, recv):
        self.place, self.src, self.view, self.local, self.send, self.recv = place, src, view, local, send, recv

    def piece(self, r, z, c):
        return self.view(r, 2 * z + c)

    def arrival(self, r, z, c):
        return self.recv.at[r, 2 * z + c]

    def copy(self, src, kind, d, r, z, c, device):
        return remote(src, self.piece(r, z, c), self.send.at[kind, d], self.arrival(r, z, c), device)

    def wait_piece(self, r, z, c):
        there = self.piece(r, z, c)
        pltpu.make_async_copy(there, there, self.arrival(r, z, c)).wait()

    def begin(self):
        p = self.place
        self.own_copy().start()
        for d in range(1, p.depth):
            self.copy(self.src, 0, d, p.r, p.z, p.c, p.device(p.r, p.z_at(d), p.c)).start()
        self.spread(0, self.src)

    def own_copy(self):
        p = self.place
        return pltpu.make_async_copy(self.src, self.piece(p.r, p.z, p.c), self.local)

    def bits(self, d):
        return (0, 1) if d % 2 == 0 else (1, 0)

    def spread(self, d, src=None):
        p = self.place
        z = p.z_at(-d)
        first, second = self.bits(d)
        src = self.piece(p.r, z, p.c) if src is None else src
        self.copy(src, 1, d, p.r, z, p.c, p.device(p.row_flip(p.r, first), p.z, p.c)).start()
        self.copy(src, 2, d, p.r, z, p.c, p.device(p.row_flip(p.r, second), p.z, p.c)).start()
        self.hand_over(4, d, p.r, z, src)

    def hand_over(self, kind, d, r, z, src=None):
        p = self.place
        src = self.piece(r, z, p.c) if src is None else src
        self.copy(src, kind, d, r, z, p.c, p.device(p.r, p.z, 1 - p.c)).start()

    def take_z(self, d):
        p = self.place
        self.wait_piece(p.r, p.z_at(-d), p.c)
        self.spread(d)

    def take_first(self, d):
        p = self.place
        z = p.z_at(-d)
        first, second = self.bits(d)
        r = p.row_flip(p.r, first)
        self.wait_piece(r, z, p.c)
        self.copy(
            self.piece(r, z, p.c), 3, d, r, z, p.c, p.device(p.row_flip(p.r, second), p.z, p.c)
        ).start()
        self.hand_over(5, d, r, z)

    def take_second(self, d):
        p = self.place
        r = p.row_flip(p.r, self.bits(d)[1])
        z = p.z_at(-d)
        self.wait_piece(r, z, p.c)
        self.hand_over(6, d, r, z)

    def take_both(self, d):
        p = self.place
        r = p.row_flip(p.row_flip(p.r, 0), 1)
        z = p.z_at(-d)
        self.wait_piece(r, z, p.c)
        self.hand_over(7, d, r, z)

    def finish(self):
        p = self.place
        self.own_copy().wait()
        for d in range(p.depth):
            for r in range(p.rows):
                self.wait_piece(r, p.z_at(-d), 1 - p.c)
        there = self.src
        for d in range(p.depth):
            for kind in range(8):
                if kind > 0 or d > 0:
                    pltpu.make_async_copy(there, there, self.send.at[kind, d]).wait()


def gather_kernel(*refs, rows, ffn, views):
    n = len(views)
    src, dst = refs[:n], refs[n : 2 * n]
    local, send, recv = refs[2 * n :]
    place = Place(rows, ffn)
    jobs = [
        Gather(place, src[i], views[i](dst[i]), local.at[i], send.at[i], recv.at[i]) for i in range(n)
    ]
    for job in jobs:
        job.begin()
    for step in ("take_z", "take_first", "take_second", "take_both"):
        for job in jobs:
            for d in range(1 if step == "take_z" else 0, place.depth):
                getattr(job, step)(d)
    for job in jobs:
        job.finish()


def by_device(ref):
    return lambda r, f: ref.at[r, f]


def by_unit(ref):
    return lambda r, f: ref.at[f, r]


def gather_all(rows, ffn, by_rows, by_units):
    src = list(by_rows) + list(by_units)
    shapes = [(rows, ffn) + a.shape for a in by_rows] + [(ffn, rows) + a.shape for a in by_units]
    views = (by_device,) * len(by_rows) + (by_unit,) * len(by_units)
    n = len(src)
    hbm = pl.BlockSpec(memory_space=pl.ANY)
    return pl.pallas_call(
        functools.partial(gather_kernel, rows=rows, ffn=ffn, views=views),
        in_specs=[hbm] * n,
        out_specs=[hbm] * n,
        out_shape=[sds(s, BF16) for s in shapes],
        scratch_shapes=[
            pltpu.SemaphoreType.DMA((n,)),
            pltpu.SemaphoreType.DMA((n, 8, ffn // 2)),
            pltpu.SemaphoreType.DMA((n, rows, ffn)),
        ],
        compiler_params=pltpu.CompilerParams(has_side_effects=True),
        name="gather_all",
    )(*src)


class Scatter:
    def __init__(self, place, view, own, half, pair, last, far, sems):
        self.place, self.view, self.own, self.half, self.pair, self.last, self.far = place, view, own, half, pair, last, far
        self.load, self.send, self.recv = sems

    def bits(self, d):
        return (0, 1) if d % 2 == 0 else (1, 0)

    def copy(self, src, dst, kind, d, device):
        return remote(src, dst, self.send.at[kind, d], self.recv.at[kind, d], device)

    def to_core(self, d, r):
        p = self.place
        z = p.z_at(d)
        return self.copy(
            self.view(r, 2 * z + 1 - p.c), self.half.at[d, r], r, d, p.device(p.r, p.z, 1 - p.c)
        )

    def fetch(self, d, r):
        p = self.place
        return pltpu.make_async_copy(self.view(r, 2 * p.z_at(d) + p.c), self.own.at[d, r], self.load.at[r, d])

    def begin(self, d):
        for r in range(4):
            self.to_core(d, r).start()
            self.fetch(d, r).start()

    def exchange_one(self, d, k):
        p = self.place
        first, second = self.bits(d)
        partner = p.row_flip(p.r, first)
        r = partner if k == 0 else p.row_flip(partner, second)
        return self.copy(self.own.at[d, r], self.pair.at[d, k], 4 + k, d, p.device(partner, p.z, p.c))

    def exchange_two(self, d):
        p = self.place
        partner = p.row_flip(p.r, self.bits(d)[1])
        return self.copy(self.own.at[d, partner], self.last.at[d], 6, d, p.device(partner, p.z, p.c))

    def along(self, d):
        p = self.place
        return self.copy(self.own.at[d, p.r], self.far.at[d], 7, d, p.device(p.r, p.z_at(d), p.c))

    def add_core(self, d, k):
        p = self.place
        first, second = self.bits(d)
        base = p.row_flip(p.r, first) if k < 2 else p.r
        r = base if k % 2 == 0 else p.row_flip(base, second)
        pltpu.make_async_copy(self.own.at[d, r], self.own.at[d, r], self.load.at[r, d]).wait()
        pltpu.make_async_copy(self.half.at[d, r], self.half.at[d, r], self.recv.at[r, d]).wait()
        self.own[d, r] = self.own[d, r] + self.half[d, r]
        if k < 2:
            self.exchange_one(d, k).start()

    def add_one(self, d, k):
        p = self.place
        r = p.r if k == 0 else p.row_flip(p.r, self.bits(d)[1])
        self.exchange_one(d, k).wait_recv()
        self.own[d, r] = self.own[d, r] + self.pair[d, k]
        if k == 1:
            self.exchange_two(d).start()

    def add_two(self, d):
        p = self.place
        self.exchange_two(d).wait_recv()
        self.own[d, p.r] = self.own[d, p.r] + self.last[d]
        if d > 0:
            self.along(d).start()

    def total(self):
        p = self.place
        out = self.own[0, p.r].astype(F32)
        for d in range(1, p.depth):
            self.along(d).wait_recv()
            out = out + self.far[d].astype(F32)
        return out

    def finish(self):
        p = self.place
        for d in range(p.depth):
            for r in range(4):
                self.to_core(d, r).wait_send()
            for k in range(2):
                self.exchange_one(d, k).wait_send()
            self.exchange_two(d).wait_send()
            if d > 0:
                self.along(d).wait_send()


def scatter_kernel(src, out, own, half, pair, last, far, load, send, recv, *, rows, ffn, view):
    place = Place(rows, ffn)
    job = Scatter(place, view(src), own, half, pair, last, far, (load, send, recv))
    order = list(range(1, place.depth)) + [0]
    for d in order:
        job.begin(d)
    for d in order:
        for k in (0, 1, 3, 2):
            job.add_core(d, k)
    for d in order:
        for k in (1, 0):
            job.add_one(d, k)
    for d in order:
        job.add_two(d)
    out[...] = job.total()
    job.finish()


def scatter_sum(rows, ffn, grad, view):
    piece = grad.shape[2:]
    depth = ffn // 2
    return pl.pallas_call(
        functools.partial(scatter_kernel, rows=rows, ffn=ffn, view=view),
        in_specs=[pl.BlockSpec(memory_space=pl.ANY)],
        out_specs=pl.BlockSpec(memory_space=pltpu.VMEM),
        out_shape=sds(piece, F32),
        scratch_shapes=[
            pltpu.VMEM((depth, rows) + piece, BF16),
            pltpu.VMEM((depth, rows) + piece, BF16),
            pltpu.VMEM((depth, 2) + piece, BF16),
            pltpu.VMEM((depth,) + piece, BF16),
            pltpu.VMEM((depth,) + piece, BF16),
            pltpu.SemaphoreType.DMA((4, depth)),
            pltpu.SemaphoreType.DMA((8, depth)),
            pltpu.SemaphoreType.DMA((8, depth)),
        ],
        compiler_params=params(has_side_effects=True),
        name="scatter_sum",
    )(grad)


def widen(blocks, lanes):
    nb, rows, hb = blocks.shape
    group = max(1, lanes // hb)
    if group == 1:
        return blocks
    return blocks.reshape(nb // group, group, rows, hb).transpose(0, 2, 1, 3).reshape(nb // group, rows, group * hb)


def narrow(blocks, hb):
    nb, rows, lanes = blocks.shape
    group = lanes // hb
    if group == 1:
        return blocks
    return blocks.reshape(nb, rows, group, hb).transpose(0, 2, 1, 3).reshape(nb * group, rows, hb)


def rows_of(vector):
    return vector.reshape(1, -1)


def shards(
    tokens, lengths, cotangent, ln_attn_gain, ln_attn_bias, w_query, query_bias, w_key, w_value, value_bias,
    head_scale, w_out, out_bias, post_gain, post_bias, ffn_gain, ffn_bias, w_up, up_bias, mid_gain, mid_bias,
    w_down, down_bias,
):
    seq, width = tokens.shape
    heads = head_scale.shape[0]
    head = width // heads
    factor = head ** (-0.5)
    block = min(seq, 256)
    rows, ffn = lax.axis_size("rows"), lax.axis_size("ffn")
    four = jnp.stack([w_query, w_key, w_value, w_out])
    attn_all, up_all, down_all = gather_all(rows, ffn, [four], [w_up, w_down])
    wq, wk, wv, wo = (attn_all[:, :, i].reshape(width, width) for i in range(4))
    own_units = w_up.shape[1]
    wup = widen(up_all.reshape(ffn, width, own_units), 512)
    wdn = widen(down_all.reshape(ffn, width, own_units), 512)
    nb, _, hb = wup.shape
    h, q, k, v = project_qkv(
        tokens, rows_of(ln_attn_gain), rows_of(ln_attn_bias), wq, rows_of(query_bias), wk, wv, rows_of(value_bias),
        factor, block,
    )
    c, lse = attend_forward(lengths, head_scale, q, k, v, block, head)
    o, x2, h2 = out_forward(
        c, wo, rows_of(out_bias), tokens, rows_of(post_gain), rows_of(post_bias), rows_of(ffn_gain),
        rows_of(ffn_bias), block,
    )
    units = lambda vector: vector.reshape(nb, 1, hb)
    result, dh2, m, du, g_ub, g_mg, g_mb, g_db = feed_forward(
        lengths, h2, cotangent, x2, wup, wdn, units(up_bias), units(mid_gain), units(mid_bias), rows_of(down_bias),
        block,
    )
    g_up, g_dn = ffn_weight_grads(lengths, h2, cotangent, m, du)
    scale_cols = rows_of(jnp.repeat(head_scale, head))
    dx2, dor, g, dcc, g_fg, g_fb, g_pg, g_pb, g_ob = out_backward(
        lengths, dh2, cotangent, x2, o, c, wo, rows_of(ffn_gain), rows_of(post_gain), scale_cols, block
    )
    inner = jnp.sum(dcc.reshape(seq, heads, head), axis=-1)
    g_hs = jnp.sum(inner, axis=0) / head_scale
    inner_rows = inner.T.reshape(heads // 2, 2, seq)
    lse_rows = jnp.stack([lse[:, :, 0], lse[:, :, head]], axis=1)
    dq, dk, dv = attend_backward(lengths, q, k, v, g, lse_rows, inner_rows, block, head, factor)
    g_wo = weight_grad(c, dor, 512)
    g_wq, g_wk, g_wv = (weight_grad(h, part, 512) for part in (dq, dk, dv))
    dx, g_lg, g_lb, g_qb, g_vb = input_grad(dq, dk, dv, wq, wk, wv, tokens, dx2, rows_of(ln_attn_gain), block)
    grad_up, grad_down = (
        scatter_sum(rows, ffn, narrow(part, own_units).reshape((ffn, rows) + w_up.shape), by_unit) for part in (g_up, g_dn)
    )
    stacked = narrow(jnp.concatenate([g_ub, g_mg, g_mb], axis=1), own_units)
    stacked = lax.psum(lax.psum_scatter(stacked, "ffn", scatter_dimension=0, tiled=False), "rows")
    attn = jnp.stack([part.reshape((rows, ffn) + w_query.shape) for part in (g_wq, g_wk, g_wv, g_wo)], axis=2)
    attn = scatter_sum(rows, ffn, attn, by_device)
    small = jnp.concatenate(
        [g_lg, g_lb, g_qb, g_vb, g_ob, g_pg, g_pb, g_fg, g_fb, g_db, jnp.pad(rows_of(g_hs), ((0, 0), (0, width - heads)))],
        axis=0,
    )
    small = lax.psum(small, BOTH)
    return (
        result, dx, small[0], small[1], attn[0], small[2], attn[1], attn[2], small[3], small[10, :heads], attn[3], small[4], small[5],
        small[6], small[7], small[8], grad_up, stacked[0], stacked[1], stacked[2], grad_down, small[9],
    )


def solution(mesh):
    split = P(BOTH, None)
    tiles = P("rows", "ffn")
    one = P()
    return jax.shard_map(
        shards,
        mesh=mesh,
        in_specs=(
            split, P(BOTH), split, one, one, split, one, split, split, one, one, split, one, one, one, one, one,
            tiles, one, one, one, tiles, one,
        ),
        out_specs=(
            split, split, one, one, split, one, split, split, one, one, split, one, one, one, one, one,
            tiles, P("ffn"), P("ffn"), P("ffn"), tiles, one,
        ),
        check_vma=False,
    )
```

```python
import functools
import math

import jax
import jax.numpy as jnp
from jax import lax
from jax.experimental import pallas as pl
from jax.experimental.pallas import tpu as pltpu
from jax.sharding import PartitionSpec as P

epsilon = 1e-05
masked_score = -1e30
F32 = jnp.float32
BF16 = jnp.bfloat16
MIB = 1 << 20
BOTH = ("rows", "ffn")


def dot_nn(left, right):
    return lax.dot_general(left, right, (((1,), (0,)), ((), ())), preferred_element_type=F32)


def dot_nt(left, right):
    return lax.dot_general(left, right, (((1,), (1,)), ((), ())), preferred_element_type=F32)


def dot_tn(left, right):
    return lax.dot_general(left, right, (((0,), (0,)), ((), ())), preferred_element_type=F32)


def params(limit=56 * MIB, **kw):
    return pltpu.CompilerParams(vmem_limit_bytes=limit, **kw)


def whole(shape):
    return pl.BlockSpec(shape, lambda *_: (0,) * len(shape), pipeline_mode=pl.Buffered(1))


def out_whole(shape):
    return pl.BlockSpec(shape, lambda *_: (0,) * len(shape))


def sds(shape, dtype):
    return jax.ShapeDtypeStruct(shape, dtype)


def norm_parts(values):
    center = jnp.mean(values, axis=-1, keepdims=True)
    centered = values - center
    spread = jnp.mean(centered * centered, axis=-1, keepdims=True)
    inverse = lax.rsqrt(spread + epsilon)
    return centered * inverse, inverse


def norm_back(grad_hat, hat, inverse):
    return (
        grad_hat
        - jnp.mean(grad_hat, axis=-1, keepdims=True)
        - hat * jnp.mean(grad_hat * hat, axis=-1, keepdims=True)
    ) * inverse


def col_sum(values):
    return jnp.sum(values, axis=0, keepdims=True)


class Place:
    def __init__(self, rows, ffn):
        self.rows, self.ffn, self.depth = rows, ffn, ffn // 2
        self.r = lax.axis_index("rows")
        f = lax.axis_index("ffn")
        self.z, self.c = f // 2, lax.rem(f, 2)

    def row_flip(self, r, bit):
        return r + 1 - 2 * lax.rem(r, 2) if bit == 0 else lax.rem(r + 2, 4)

    def z_at(self, d):
        return lax.rem(self.z + d + self.depth, self.depth)

    def device(self, r, z, c):
        return (r, 2 * z + c)


def remote(src, dst, send, recv, device):
    return pltpu.make_async_remote_copy(
        src_ref=src, dst_ref=dst, send_sem=send, recv_sem=recv, device_id=device, device_id_type=pl.DeviceIdType.MESH
    )


class Gather:
    def __init__(self, place, src, view, local, send, recv):
        self.place, self.src, self.view, self.local, self.send, self.recv = place, src, view, local, send, recv

    def piece(self, r, z, c):
        return self.view(r, 2 * z + c)

    def arrival(self, r, z, c):
        return self.recv.at[r, 2 * z + c]

    def copy(self, src, kind, d, r, z, c, device):
        return remote(src, self.piece(r, z, c), self.send.at[kind, d], self.arrival(r, z, c), device)

    def wait_piece(self, r, z, c):
        there = self.piece(r, z, c)
        pltpu.make_async_copy(there, there, self.arrival(r, z, c)).wait()

    def begin(self):
        p = self.place
        self.own_copy().start()
        for d in range(1, p.depth):
            self.copy(self.src, 0, d, p.r, p.z, p.c, p.device(p.r, p.z_at(d), p.c)).start()
        self.spread(0, self.src)

    def own_copy(self):
        p = self.place
        return pltpu.make_async_copy(self.src, self.piece(p.r, p.z, p.c), self.local)

    def bits(self, d):
        return (0, 1) if d % 2 == 0 else (1, 0)

    def spread(self, d, src=None):
        p = self.place
        z = p.z_at(-d)
        first, second = self.bits(d)
        src = self.piece(p.r, z, p.c) if src is None else src
        self.copy(src, 1, d, p.r, z, p.c, p.device(p.row_flip(p.r, first), p.z, p.c)).start()
        self.copy(src, 2, d, p.r, z, p.c, p.device(p.row_flip(p.r, second), p.z, p.c)).start()
        self.hand_over(4, d, p.r, z, src)

    def hand_over(self, kind, d, r, z, src=None):
        p = self.place
        src = self.piece(r, z, p.c) if src is None else src
        self.copy(src, kind, d, r, z, p.c, p.device(p.r, p.z, 1 - p.c)).start()

    def take_z(self, d):
        p = self.place
        self.wait_piece(p.r, p.z_at(-d), p.c)
        self.spread(d)

    def take_first(self, d):
        p = self.place
        z = p.z_at(-d)
        first, second = self.bits(d)
        r = p.row_flip(p.r, first)
        self.wait_piece(r, z, p.c)
        self.copy(
            self.piece(r, z, p.c), 3, d, r, z, p.c, p.device(p.row_flip(p.r, second), p.z, p.c)
        ).start()
        self.hand_over(5, d, r, z)

    def take_second(self, d):
        p = self.place
        r = p.row_flip(p.r, self.bits(d)[1])
        z = p.z_at(-d)
        self.wait_piece(r, z, p.c)
        self.hand_over(6, d, r, z)

    def take_both(self, d):
        p = self.place
        r = p.row_flip(p.row_flip(p.r, 0), 1)
        z = p.z_at(-d)
        self.wait_piece(r, z, p.c)
        self.hand_over(7, d, r, z)

    def finish(self):
        p = self.place
        self.own_copy().wait()
        for d in range(p.depth):
            for r in range(p.rows):
                self.wait_piece(r, p.z_at(-d), 1 - p.c)
        there = self.src
        for d in range(p.depth):
            for kind in range(8):
                if kind > 0 or d > 0:
                    pltpu.make_async_copy(there, there, self.send.at[kind, d]).wait()


def gather_kernel(*refs, rows, ffn, views):
    n = len(views)
    src, dst = refs[:n], refs[n : 2 * n]
    local, send, recv = refs[2 * n :]
    place = Place(rows, ffn)
    jobs = [
        Gather(place, src[i], views[i](dst[i]), local.at[i], send.at[i], recv.at[i]) for i in range(n)
    ]
    for job in jobs:
        job.begin()
    for step in ("take_z", "take_first", "take_second", "take_both"):
        for job in jobs:
            for d in range(1 if step == "take_z" else 0, place.depth):
                getattr(job, step)(d)
    for job in jobs:
        job.finish()


def by_device(ref):
    return lambda r, f: ref.at[r, f]


def by_unit(ref):
    return lambda r, f: ref.at[f, r]


def gather_all(rows, ffn, by_rows, by_units):
    src = list(by_rows) + list(by_units)
    shapes = [(rows, ffn) + a.shape for a in by_rows] + [(ffn, rows) + a.shape for a in by_units]
    views = (by_device,) * len(by_rows) + (by_unit,) * len(by_units)
    n = len(src)
    hbm = pl.BlockSpec(memory_space=pl.ANY)
    return pl.pallas_call(
        functools.partial(gather_kernel, rows=rows, ffn=ffn, views=views),
        in_specs=[hbm] * n,
        out_specs=[hbm] * n,
        out_shape=[sds(s, BF16) for s in shapes],
        scratch_shapes=[
            pltpu.SemaphoreType.DMA((n,)),
            pltpu.SemaphoreType.DMA((n, 8, ffn // 2)),
            pltpu.SemaphoreType.DMA((n, rows, ffn)),
        ],
        compiler_params=pltpu.CompilerParams(has_side_effects=True),
        name="gather_all",
    )(*src)


class Scatter:
    def __init__(self, place, view, own, half, pair, last, far, sems):
        self.place, self.view, self.own, self.half, self.pair, self.last, self.far = place, view, own, half, pair, last, far
        self.load, self.send, self.recv = sems

    def bits(self, d):
        return (0, 1) if d % 2 == 0 else (1, 0)

    def copy(self, src, dst, kind, d, device):
        return remote(src, dst, self.send.at[kind, d], self.recv.at[kind, d], device)

    def to_core(self, d, r):
        p = self.place
        z = p.z_at(d)
        return self.copy(
            self.view(r, 2 * z + 1 - p.c), self.half.at[d, r], r, d, p.device(p.r, p.z, 1 - p.c)
        )

    def fetch(self, d, r):
        p = self.place
        return pltpu.make_async_copy(self.view(r, 2 * p.z_at(d) + p.c), self.own.at[d, r], self.load.at[r, d])

    def begin(self, d):
        for r in range(4):
            self.to_core(d, r).start()
            self.fetch(d, r).start()

    def exchange_one(self, d, k):
        p = self.place
        first, second = self.bits(d)
        partner = p.row_flip(p.r, first)
        r = partner if k == 0 else p.row_flip(partner, second)
        return self.copy(self.own.at[d, r], self.pair.at[d, k], 4 + k, d, p.device(partner, p.z, p.c))

    def exchange_two(self, d):
        p = self.place
        partner = p.row_flip(p.r, self.bits(d)[1])
        return self.copy(self.own.at[d, partner], self.last.at[d], 6, d, p.device(partner, p.z, p.c))

    def along(self, d):
        p = self.place
        return self.copy(self.own.at[d, p.r], self.far.at[d], 7, d, p.device(p.r, p.z_at(d), p.c))

    def add_core(self, d, k):
        p = self.place
        first, second = self.bits(d)
        base = p.row_flip(p.r, first) if k < 2 else p.r
        r = base if k % 2 == 0 else p.row_flip(base, second)
        pltpu.make_async_copy(self.own.at[d, r], self.own.at[d, r], self.load.at[r, d]).wait()
        pltpu.make_async_copy(self.half.at[d, r], self.half.at[d, r], self.recv.at[r, d]).wait()
        self.own[d, r] = self.own[d, r] + self.half[d, r]
        if k < 2:
            self.exchange_one(d, k).start()

    def add_one(self, d, k):
        p = self.place
        r = p.r if k == 0 else p.row_flip(p.r, self.bits(d)[1])
        self.exchange_one(d, k).wait_recv()
        self.own[d, r] = self.own[d, r] + self.pair[d, k]
        if k == 1:
            self.exchange_two(d).start()

    def add_two(self, d):
        p = self.place
        self.exchange_two(d).wait_recv()
        self.own[d, p.r] = self.own[d, p.r] + self.last[d]
        if d > 0:
            self.along(d).start()

    def total(self):
        p = self.place
        out = self.own[0, p.r].astype(F32)
        for d in range(1, p.depth):
            self.along(d).wait_recv()
            out = out + self.far[d].astype(F32)
        return out

    def finish(self):
        p = self.place
        for d in range(p.depth):
            for r in range(4):
                self.to_core(d, r).wait_send()
            for k in range(2):
                self.exchange_one(d, k).wait_send()
            self.exchange_two(d).wait_send()
            if d > 0:
                self.along(d).wait_send()


def scatter_kernel(src, out, own, half, pair, last, far, load, send, recv, *, rows, ffn, view):
    place = Place(rows, ffn)
    job = Scatter(place, view(src), own, half, pair, last, far, (load, send, recv))
    order = list(range(1, place.depth)) + [0]
    for d in order:
        job.begin(d)
    for d in order:
        for k in (0, 1, 3, 2):
            job.add_core(d, k)
    for d in order:
        for k in (1, 0):
            job.add_one(d, k)
    for d in order:
        job.add_two(d)
    out[...] = job.total()
    job.finish()


def scatter_sum(rows, ffn, grad, view):
    piece = grad.shape[2:]
    depth = ffn // 2
    return pl.pallas_call(
        functools.partial(scatter_kernel, rows=rows, ffn=ffn, view=view),
        in_specs=[pl.BlockSpec(memory_space=pl.ANY)],
        out_specs=pl.BlockSpec(memory_space=pltpu.VMEM),
        out_shape=sds(piece, F32),
        scratch_shapes=[
            pltpu.VMEM((depth, rows) + piece, BF16),
            pltpu.VMEM((depth, rows) + piece, BF16),
            pltpu.VMEM((depth, 2) + piece, BF16),
            pltpu.VMEM((depth,) + piece, BF16),
            pltpu.VMEM((depth,) + piece, BF16),
            pltpu.SemaphoreType.DMA((4, depth)),
            pltpu.SemaphoreType.DMA((8, depth)),
            pltpu.SemaphoreType.DMA((8, depth)),
        ],
        compiler_params=params(has_side_effects=True),
        name="scatter_sum",
    )(grad)


def clip(step, low, count):
    return jnp.minimum(jnp.maximum(step - low, 0), count - 1)


def at_steps(step, plan):
    for when, actions in plan.items():

        @pl.when(step == when)
        def _(actions=actions):
            for action in actions:
                action()


def attend_pair(length, scales, q_of, k, v, seq, block, head, store):
    lanes = 2 * head
    lane = lax.broadcasted_iota(jnp.int32, (block, lanes), 1)
    for i in range(seq // block):
        keys_here = (i + 1) * block
        q = q_of(i)
        key_pos = lax.broadcasted_iota(jnp.int32, (block, keys_here), 1)
        row_pos = lax.broadcasted_iota(jnp.int32, (block, keys_here), 0) + i * block
        allowed = key_pos < jnp.minimum(row_pos + 1, length)
        ctx = None
        logs = []
        for n in range(2):
            mine = (lane < head) if n == 0 else (lane >= head)
            scores = dot_nt(jnp.where(mine, q, 0), k[:keys_here, :])
            scores = jnp.where(allowed, scores, masked_score)
            peak = jnp.max(scores, axis=-1, keepdims=True)
            weights = jnp.exp(scores - peak)
            total = jnp.sum(weights, axis=-1, keepdims=True)
            part = dot_nn(weights.astype(BF16), v[:keys_here, :]) * (scales[n] / total)
            ctx = part if n == 0 else jnp.where(lane < head, ctx, part)
            logs.append(peak + jnp.log(total))
        store(i, ctx.astype(BF16), jnp.where(lane < head, logs[0], logs[1]).T)


def front_kernel(*refs, rows, ffn, block, head, factor, fused):
    n_in = 14 if fused else 12
    (length_ref, scale_ref, x_ref, lg_ref, lb_ref, qb_ref, vb_ref, ob_ref, pg_ref, pb_ref, fg_ref) = refs[:11]
    fb_ref = refs[11]
    comm_in = refs[12 : 15 if fused else 13]
    refs = refs[15 if fused else 13 :]
    h_ref, q_ref, k_ref, v_ref, c_ref, lse_ref, o_ref, x2_ref, h2_ref = refs[:9]
    comm_out = refs[9:12] if fused else ()
    refs = refs[12 if fused else 9 :]
    w_s, q_s, k_s, v_s, c_s, load = refs[:6]
    step = pl.program_id(0)
    seq, width = q_s.shape
    nb = seq // block
    pairs = width // (2 * head)
    last = 2 * nb + pairs - 1

    def load_weights(source):
        copies = [pltpu.make_async_copy(source(i), w_s.at[i], load.at[i]) for i in range(4)]
        for copy in copies:
            copy.start()
        for copy in copies:
            copy.wait()

    late = {}
    if fused:
        local, send, recv = refs[6:9]
        place = Place(rows, ffn)
        views = (by_device, by_unit, by_unit)
        four, down, up = (
            Gather(place, comm_in[i], views[i](comm_out[i]), local.at[i], send.at[i], recv.at[i]) for i in range(3)
        )
        depth = place.depth
        every = range(depth)

        @pl.when(step == 0)
        def _():
            four.begin()
            for d in range(1, depth):
                four.take_z(d)
            down.begin()
            for d in every:
                four.take_first(d)
            for d in every:
                four.take_second(d)
            for d in every:
                four.take_both(d)
            up.begin()
            four.finish()
            load_weights(lambda i: comm_out[0].at[:, :, i])

        def do(job, name, *ds):
            return [functools.partial(getattr(job, name), d) for d in ds if d < depth]

        late = {
            1: do(down, "take_z", 1) + do(down, "take_first", 0),
            2: do(down, "take_z", 2) + do(down, "take_first", 1),
            3: do(down, "take_z", 3) + do(down, "take_second", 0),
            4: do(down, "take_first", 2) + do(up, "take_z", 1),
            5: do(down, "take_first", 3) + do(down, "take_second", 1) + do(up, "take_z", 2),
            6: do(down, "take_both", 0, 1) + do(down, "take_second", 2) + do(up, "take_z", 3),
            7: do(down, "take_second", 3) + do(up, "take_first", 0),
            8: do(down, "take_both", 2, 3) + do(up, "take_first", 1),
            9: do(up, "take_first", 2) + do(up, "take_second", 0),
            10: do(up, "take_first", 3) + do(up, "take_second", 1),
            11: do(up, "take_second", 2),
            12: do(up, "take_second", 3) + do(up, "take_both", 0),
            13: do(up, "take_both", 1),
        }
        at_steps(step, late)
    else:

        @pl.when(step == 0)
        def _():
            load_weights(lambda i: comm_in[0].at[i])

    def weight(i):
        return w_s[i].reshape(width, width)

    @pl.when(step < nb)
    def _():
        here = pl.ds(pl.multiple_of(step * block, block), block)
        hat, _ = norm_parts(x_ref[...].astype(F32))
        h = (hat * lg_ref[...] + lb_ref[...]).astype(BF16)
        h_ref[...] = h
        q = ((dot_nn(h, weight(0)) + qb_ref[...]).astype(BF16).astype(F32) * factor).astype(BF16)
        k = dot_nn(h, weight(1)).astype(BF16)
        v = (dot_nn(h, weight(2)) + vb_ref[...]).astype(BF16)
        for ref, scratch, value in ((q_ref, q_s, q), (k_ref, k_s, k), (v_ref, v_s, v)):
            ref[...] = value
            scratch[here, :] = value

    @pl.when((step >= nb) & (step < nb + pairs))
    def _():
        pair = step - nb
        cols = pl.ds(pl.multiple_of(pair * (2 * head), 2 * head), 2 * head)

        def store(i, ctx, logs):
            c_s[i * block : (i + 1) * block, cols] = ctx
            for n in range(2):
                lse_ref[0, n : n + 1, i * block : (i + 1) * block] = logs[n * head : n * head + 1, :]

        attend_pair(
            length_ref[0], [scale_ref[2 * pair + n] for n in range(2)],
            lambda i: q_s[i * block : (i + 1) * block, cols], k_s[:, cols], v_s[:, cols], seq, block, head, store,
        )

    @pl.when(step >= nb + pairs)
    def _():
        here = pl.ds(pl.multiple_of((step - nb - pairs) * block, block), block)
        c = c_s[here, :]
        c_ref[...] = c
        o = dot_nn(c, weight(3)) + ob_ref[...]
        o_ref[...] = o
        hat, _ = norm_parts(o)
        x2 = x_ref[...].astype(F32) + (hat * pg_ref[...] + pb_ref[...])
        x2_ref[...] = x2
        hat2, _ = norm_parts(x2)
        h2_ref[...] = (hat2 * fg_ref[...] + fb_ref[...]).astype(BF16)

    if fused:

        @pl.when(step == last)
        def _():
            for d in (2, 3):
                if d < depth:
                    up.take_both(d)
            down.finish()
            up.finish()


def front(length, scale, x, vectors, weights, rows, ffn, block, head, factor, fused):
    seq, width = x.shape
    nb, pairs = seq // block, width // (2 * head)
    steps = 2 * nb + pairs
    x_rows = pl.BlockSpec((block, width), lambda i: (jnp.where(i < nb + pairs, jnp.minimum(i, nb - 1), i - nb - pairs), 0))
    first = pl.BlockSpec((block, width), lambda i: (clip(i, 0, nb), 0))
    final = pl.BlockSpec((block, width), lambda i: (clip(i, nb + pairs, nb), 0))
    smem = pl.BlockSpec(memory_space=pltpu.SMEM)
    hbm = pl.BlockSpec(memory_space=pl.ANY)
    out_specs = [first] * 4 + [final, pl.BlockSpec((1, 2, seq), lambda i: (clip(i, nb, pairs), 0, 0))] + [final] * 3
    out_shape = [sds((seq, width), BF16)] * 5 + [sds((pairs, 2, seq), F32)] + [sds((seq, width), F32)] * 2
    out_shape += [sds((seq, width), BF16)]
    scratch = [pltpu.VMEM((seq, width), BF16)] * 4 + [pltpu.SemaphoreType.DMA((4,))]
    if fused:
        four, down, up = weights
        out_shape += [sds((rows, ffn) + four.shape, BF16)] + [sds((ffn, rows) + a.shape, BF16) for a in (down, up)]
        out_specs += [hbm] * 3
        scratch = [pltpu.VMEM((4, rows, ffn) + four.shape[1:], BF16)] + scratch + [
            pltpu.SemaphoreType.DMA((3,)),
            pltpu.SemaphoreType.DMA((3, 8, ffn // 2)),
            pltpu.SemaphoreType.DMA((3, rows, ffn)),
        ]
    else:
        scratch = [pltpu.VMEM((4, width, width), BF16)] + scratch
    return pl.pallas_call(
        functools.partial(front_kernel, rows=rows, ffn=ffn, block=block, head=head, factor=factor, fused=fused),
        grid=(steps,),
        in_specs=[smem, smem, x_rows] + [whole((1, width))] * 9 + [hbm] * len(weights),
        out_specs=out_specs,
        out_shape=out_shape,
        scratch_shapes=scratch,
        compiler_params=params(60 * MIB, has_side_effects=fused),
        name="forward_attention",
    )(length, scale, x, *vectors, *weights)


def ffn_kernel(
    length_ref, h2_ref, ct_ref, x2_ref, wup_ref, wdn_ref, ub_ref, mg_ref, mb_ref, db_ref,
    res_ref, dh2_ref, m_ref, du_ref, gub_ref, gmg_ref, gmb_ref, gdb_ref,
    e_s, gp_s, dm_s,
):
    step = pl.program_id(0)
    block, width = h2_ref.shape
    nb, _, hb = wup_ref.shape
    units = nb * hb
    row = lax.broadcasted_iota(jnp.int32, (block, width), 0) + step * block
    valid = row < length_ref[0]
    h2 = h2_ref[...]
    dfr = jnp.where(valid, ct_ref[...].astype(F32), 0.0).astype(BF16)

    @pl.when(step == 0)
    def _():
        gub_ref[...] = jnp.zeros_like(gub_ref)
        gmg_ref[...] = jnp.zeros_like(gmg_ref)
        gmb_ref[...] = jnp.zeros_like(gmb_ref)
        gdb_ref[...] = jnp.zeros_like(gdb_ref)

    gdb_ref[...] += col_sum(dfr.astype(F32))

    def first(j, sums):
        u = dot_nn(h2, wup_ref[j]) + ub_ref[j]
        dm = dot_nn(dfr, wdn_ref[j])
        cdf = 0.5 * (1.0 + lax.erf(u * math.sqrt(0.5)))
        e = u * cdf
        gp = cdf + u * (jnp.exp(u * u * -0.5) * (1.0 / math.sqrt(2.0 * math.pi)))
        dmh = dm * mg_ref[j]
        e_s[j] = e
        gp_s[j] = gp
        dm_s[j] = dm
        terms = (e, e * e, dmh, dmh * e)
        return tuple(s + jnp.sum(t, axis=-1, keepdims=True) for s, t in zip(sums, terms))

    zero = jnp.zeros((block, 1), F32)
    sum_e, sum_ee, sum_d, sum_de = lax.fori_loop(0, nb, first, (zero,) * 4)
    mu = sum_e / units
    inverse = lax.rsqrt(sum_ee / units - mu * mu + epsilon)
    mean_d = sum_d / units
    mean_dh = (sum_de - mu * sum_d) * inverse / units

    def second(j, sums):
        f, dh2 = sums
        ehat = (e_s[j] - mu) * inverse
        dm = dm_s[j]
        m = (ehat * mg_ref[j] + mb_ref[j]).astype(BF16)
        m_ref[j] = m
        f = f + dot_nt(m, wdn_ref[j])
        de = (dm * mg_ref[j] - mean_d - ehat * mean_dh) * inverse
        du = (de * gp_s[j]).astype(BF16)
        du_ref[j] = du
        dh2 = dh2 + dot_nt(du, wup_ref[j])
        gub_ref[j] += col_sum(du.astype(F32))
        gmg_ref[j] += col_sum(dm * ehat)
        gmb_ref[j] += col_sum(dm)
        return f, dh2

    zeros = jnp.zeros((block, width), F32)
    f, dh2 = lax.fori_loop(0, nb, second, (zeros, zeros))
    res_ref[...] = jnp.where(valid, x2_ref[...] + f + db_ref[...], 0.0)
    dh2_ref[...] = dh2


def feed_forward(length, h2, ct, x2, wup, wdn, ub, mg, mb, db, block):
    seq, width = h2.shape
    nb, _, hb = wup.shape
    rows = pl.BlockSpec((block, width), lambda i: (i, 0))
    smem = pl.BlockSpec(memory_space=pltpu.SMEM)
    units = whole((nb, 1, hb))
    blocks = pl.BlockSpec((nb, block, hb), lambda i: (0, i, 0))
    sums = out_whole((nb, 1, hb))
    return pl.pallas_call(
        ffn_kernel,
        grid=(seq // block,),
        in_specs=[
            smem, rows, rows, rows, whole((nb, width, hb)), whole((nb, width, hb)),
            units, units, units, whole((1, width)),
        ],
        out_specs=[rows, rows, blocks, blocks, sums, sums, sums, out_whole((1, width))],
        out_shape=[
            sds((seq, width), F32), sds((seq, width), F32), sds((nb, seq, hb), BF16), sds((nb, seq, hb), BF16),
            sds((nb, 1, hb), F32), sds((nb, 1, hb), F32), sds((nb, 1, hb), F32), sds((1, width), F32),
        ],
        scratch_shapes=[pltpu.VMEM((nb, block, hb), F32)] * 3,
        compiler_params=params(60 * MIB),
        cost_estimate=pl.CostEstimate(
            flops=16 * seq * width * nb * hb, bytes_accessed=60 * MIB, transcendentals=2 * seq * nb * hb
        ),
        name="feed_forward",
    )(length, h2, ct, x2, wup, wdn, ub, mg, mb, db)


def ffn_weights_kernel(length_ref, h2_ref, ct_ref, m_ref, du_ref, gup_ref, gdn_ref, h2t_s, dft_s):
    seq, width = h2_ref.shape

    @pl.when(pl.program_id(0) == 0)
    def _():
        row = lax.broadcasted_iota(jnp.int32, (seq, width), 0)
        dfr = jnp.where(row < length_ref[0], ct_ref[...], 0)
        h2t_s[...] = h2_ref[...].T
        dft_s[...] = dfr.T

    gdn_ref[0] = dot_nn(dft_s[...], m_ref[0]).astype(BF16)
    gup_ref[0] = dot_nn(h2t_s[...], du_ref[0]).astype(BF16)


def ffn_weight_grads(length, h2, ct, m, du):
    seq, width = h2.shape
    nb, _, hb = m.shape
    smem = pl.BlockSpec(memory_space=pltpu.SMEM)
    block = pl.BlockSpec((1, seq, hb), lambda j: (j, 0, 0))
    out = pl.BlockSpec((1, width, hb), lambda j: (j, 0, 0))
    return pl.pallas_call(
        ffn_weights_kernel,
        grid=(nb,),
        in_specs=[smem, whole((seq, width)), whole((seq, width)), block, block],
        out_specs=[out, out],
        out_shape=[sds((nb, width, hb), BF16)] * 2,
        scratch_shapes=[pltpu.VMEM((width, seq), BF16)] * 2,
        compiler_params=params(),
        cost_estimate=pl.CostEstimate(
            flops=4 * seq * width * nb * hb, bytes_accessed=36 * MIB, transcendentals=0
        ),
        name="ffn_weight_grads",
    )(length, h2, ct, m, du)


def attend_back_pair(length, q_all, k_of, v_of, g_all, lse_ref, inner_row, dq_s, store, seq, block, head):
    lanes = 2 * head
    lane = lax.broadcasted_iota(jnp.int32, (seq, lanes), 1)
    dq_s[...] = jnp.zeros_like(dq_s)
    zero = jnp.zeros_like(q_all)
    q_heads = [jnp.where(lane < head, q_all, zero), jnp.where(lane >= head, q_all, zero)]
    g_heads = [jnp.where(lane < head, g_all, zero), jnp.where(lane >= head, g_all, zero)]
    for j in range(seq // block):
        start = j * block
        width = seq - start
        k, v = k_of(j), v_of(j)
        key_pos = lax.broadcasted_iota(jnp.int32, (block, width), 0) + start
        row_pos = lax.broadcasted_iota(jnp.int32, (block, width), 1) + start
        allowed = (key_pos <= row_pos) & (key_pos < length)
        dk = dv = None
        dqs = []
        for n in range(2):
            q = q_heads[n][start:, :]
            g = g_heads[n][start:, :]
            scores = dot_nt(k, q)
            probs = jnp.where(allowed, jnp.exp(scores - lse_ref[0, n : n + 1, start:]), 0.0)
            grad_probs = dot_nt(v, g)
            grad_scores = (probs * (grad_probs - inner_row(n)[:, start:])).astype(BF16)
            dv_part = dot_nn(probs.astype(BF16), g)
            dk_part = dot_nn(grad_scores, q)
            dv = dv_part if n == 0 else dv + dv_part
            dk = dk_part if n == 0 else dk + dk_part
            dqs.append(dot_tn(grad_scores, k))
        dq_s[start:, :] += jnp.where(lane[start:, :] < head, dqs[0], dqs[1])
        store(j, dk.astype(BF16), dv.astype(BF16))


def back_kernel(*refs, rows, ffn, block, head, factor, fused):
    (
        length_ref, dh2_ref, ct_ref, x2_ref, o_ref, c_ref, w_ref, fg_ref, pg_ref, hs_ref, q_ref, k_ref, v_ref, lse_ref,
    ) = refs[:14]
    comm_in = refs[14:16] if fused else ()
    refs = refs[16 if fused else 14 :]
    (
        dx2_ref, dor_ref, dq_ref, dk_ref, dv_ref, ghs_ref, gfg_ref, gfb_ref, gpg_ref, gpb_ref, gob_ref,
    ) = refs[:11]
    comm_out = refs[11:13] if fused else ()
    refs = refs[13 if fused else 11 :]
    g_s, inner_s, dq_s = refs[:3]
    step = pl.program_id(0)
    seq, width = g_s.shape
    nb = seq // block
    pairs = width // (2 * head)
    heads = width // head
    last = nb + pairs - 1

    if fused:
        place = Place(rows, ffn)
        depth = place.depth
        jobs = []
        for n in range(2):
            bufs = refs[3 + 8 * n : 11 + 8 * n]
            jobs.append(Scatter(place, by_unit(comm_in[n]), *bufs[:5], bufs[5:]))
        one, two = jobs
        order = [d for d in (1, 2, 3) if d < depth] + [0]

        @pl.when(step == 0)
        def _():
            for job in jobs:
                for d in order:
                    job.begin(d)

        def core(job, *ds):
            return [functools.partial(job.add_core, d, k) for d in ds if d < depth for k in (0, 1, 3, 2)]

        def first(job, *ds):
            return [functools.partial(job.add_one, d, k) for d in ds if d < depth for k in (1, 0)]

        def second(job, *ds):
            return [functools.partial(job.add_two, d) for d in ds if d < depth]

        at_steps(step, {
            2: core(one, 1, 2),
            3: core(one, 3, 0),
            4: core(two, 1, 2),
            5: core(two, 3, 0),
            6: first(one, 1, 2),
            7: first(one, 3, 0),
            8: second(one, 1, 2, 3),
            10: first(two, 1, 2) + second(one, 0),
        })

    @pl.when(step < nb)
    def _():
        row = lax.broadcasted_iota(jnp.int32, (block, width), 0) + step * block
        dy = jnp.where(row < length_ref[0], ct_ref[...].astype(F32), 0.0)

        @pl.when(step == 0)
        def _():
            for ref in (gfg_ref, gfb_ref, gpg_ref, gpb_ref, gob_ref, ghs_ref):
                ref[...] = jnp.zeros_like(ref)

        dh2 = dh2_ref[...]
        hat2, inverse2 = norm_parts(x2_ref[...])
        gfg_ref[...] += col_sum(dh2 * hat2)
        gfb_ref[...] += col_sum(dh2)
        dx2 = dy + norm_back(dh2 * fg_ref[...], hat2, inverse2)
        dx2_ref[...] = dx2
        hat, inverse = norm_parts(o_ref[...])
        gpg_ref[...] += col_sum(dx2 * hat)
        gpb_ref[...] += col_sum(dx2)
        dor = norm_back(dx2 * pg_ref[...], hat, inverse).astype(BF16)
        dor_ref[...] = dor
        gob_ref[...] += col_sum(dor.astype(F32))
        dc = dot_nt(dor, w_ref[...].reshape(width, width))
        here = pl.ds(pl.multiple_of(step * block, block), block)
        g_s[here, :] = (dc * hs_ref[...]).astype(BF16)
        product = dc * c_ref[...].astype(F32)
        high = product.astype(BF16)
        low = (product - high.astype(F32)).astype(BF16)
        owner = lax.broadcasted_iota(jnp.int32, (heads, width), 1) // head
        pick = (owner == lax.broadcasted_iota(jnp.int32, (heads, width), 0)).astype(BF16)
        inner = dot_nt(pick, high) + dot_nt(pick, low)
        inner_s[step] = inner
        ghs_ref[...] += jnp.broadcast_to(jnp.sum(inner, axis=-1, keepdims=True), ghs_ref.shape)

    @pl.when(step >= nb)
    def _():
        pair = step - nb
        cols = pl.ds(pl.multiple_of(pair * (2 * head), 2 * head), 2 * head)
        inner_rows = [
            jnp.concatenate([inner_s[i, pl.ds(2 * pair + n, 1), :] for i in range(nb)], axis=1) for n in range(2)
        ]

        def store(j, dk, dv):
            dk_ref[j * block : (j + 1) * block, :] = dk
            dv_ref[j * block : (j + 1) * block, :] = dv

        attend_back_pair(
            length_ref[0], q_ref[...], lambda j: k_ref[j * block : (j + 1) * block, :],
            lambda j: v_ref[j * block : (j + 1) * block, :], g_s[:, cols], lse_ref, lambda n: inner_rows[n], dq_s, store,
            seq, block, head,
        )
        dq_ref[...] = (dq_s[...] * factor).astype(BF16)

    if fused:

        @pl.when(step == last)
        def _():
            for action in first(two, 3, 0) + second(two, 1, 2, 3, 0):
                action()
            for job, out in zip(jobs, comm_out):
                out[...] = job.total()
                job.finish()


def scatter_scratch(piece, rows, depth):
    return [
        pltpu.VMEM((depth, rows) + piece, BF16),
        pltpu.VMEM((depth, rows) + piece, BF16),
        pltpu.VMEM((depth, 2) + piece, BF16),
        pltpu.VMEM((depth,) + piece, BF16),
        pltpu.VMEM((depth,) + piece, BF16),
        pltpu.SemaphoreType.DMA((4, depth)),
        pltpu.SemaphoreType.DMA((8, depth)),
        pltpu.SemaphoreType.DMA((8, depth)),
    ]


def back(length, dh2, ct, x2, o, c, w, w_spec, fg, pg, hs, q, k, v, lse, grads, rows, ffn, block, head, factor, fused):
    seq, width = dh2.shape
    nb, pairs, heads = seq // block, width // (2 * head), width // head
    part = pl.BlockSpec((block, width), lambda i: (clip(i, 0, nb), 0))
    cols = pl.BlockSpec((seq, 2 * head), lambda i: (0, clip(i, nb, pairs)))
    smem = pl.BlockSpec(memory_space=pltpu.SMEM)
    hbm = pl.BlockSpec(memory_space=pl.ANY)
    vec, ovec = whole((1, width)), out_whole((1, width))
    out_specs = [part] * 2 + [cols] * 3 + [out_whole((heads, 128))] + [ovec] * 5
    out_shape = [sds((seq, width), F32), sds((seq, width), BF16)] + [sds((seq, width), BF16)] * 3
    out_shape += [sds((heads, 128), F32)] + [sds((1, width), F32)] * 5
    scratch = [
        pltpu.VMEM((seq, width), BF16), pltpu.VMEM((nb, heads, block), F32), pltpu.VMEM((seq, 2 * head), F32),
    ]
    if fused:
        piece = grads[0].shape[2:]
        out_specs += [pl.BlockSpec(memory_space=pltpu.VMEM)] * 2
        out_shape += [sds(piece, F32)] * 2
        scratch += scatter_scratch(piece, rows, ffn // 2) * 2
    else:
        grads = ()
    return pl.pallas_call(
        functools.partial(back_kernel, rows=rows, ffn=ffn, block=block, head=head, factor=factor, fused=fused),
        grid=(nb + pairs,),
        in_specs=[smem] + [part] * 5 + [w_spec] + [vec] * 3 + [cols] * 3
        + [pl.BlockSpec((1, 2, seq), lambda i: (clip(i, nb, pairs), 0, 0))] + [hbm] * len(grads),
        out_specs=out_specs,
        out_shape=out_shape,
        scratch_shapes=scratch,
        compiler_params=params(60 * MIB, has_side_effects=fused),
        name="backward_attention",
    )(length, dh2, ct, x2, o, c, w, fg, pg, hs, q, k, v, lse, *grads)


class AllSum:
    def __init__(self, place, stages, far, send, recv):
        self.place, self.stages, self.far, self.send, self.recv = place, stages, far, send, recv

    def copy(self, k):
        p = self.place
        device = (
            p.device(p.r, p.z, 1 - p.c), p.device(p.row_flip(p.r, 0), p.z, p.c), p.device(p.row_flip(p.r, 1), p.z, p.c)
        )[k]
        return remote(self.stages.at[k], self.stages.at[3 + k], self.send.at[k], self.recv.at[k], device)

    def along(self, d):
        p = self.place
        return remote(
            self.far.at[p.z], self.far.at[p.z], self.send.at[2 + d], self.recv.at[2 + d], p.device(p.r, p.z_at(d), p.c)
        )

    def begin(self):
        self.copy(0).start()

    def add(self, k):
        self.copy(k).wait_recv()
        total = self.stages[k] + self.stages[3 + k]
        if k < 2:
            self.stages[k + 1] = total
            self.copy(k + 1).start()
        else:
            self.far[self.place.z] = total
            for d in range(1, self.place.depth):
                self.along(d).start()

    def total(self):
        p = self.place
        for d in range(1, p.depth):
            there = self.far.at[p.z_at(-d)]
            pltpu.make_async_copy(there, there, self.recv.at[2 + d]).wait()
        out = self.far[0]
        for z in range(1, p.depth):
            out = out + self.far[z]
        return out

    def finish(self):
        for k in range(3):
            self.copy(k).wait_send()
        for d in range(1, self.place.depth):
            self.along(d).wait_send()


def last_kernel(*refs, rows, ffn, block, fused):
    (
        dq_ref, dk_ref, dv_ref, dor_ref, h_ref, c_ref, wq_ref, wk_ref, wv_ref, x_ref, dx2_ref, gain_ref, small_ref,
    ) = refs[:13]
    refs = refs[13:]
    dx_ref, small_out = refs[:2]
    refs = refs[2:]
    grad_refs = refs[:4]
    refs = refs[4:]
    if fused:
        grads = refs[:4]
        left_s, sums_s = refs[4:6]
        refs = refs[6:]
    else:
        grads = grad_refs
        left_s, sums_s = refs[:2]
    step = pl.program_id(0)
    seq, width = dq_ref.shape
    nb = seq // block
    last = 4 + nb - 1

    if fused:
        place = Place(rows, ffn)
        depth = place.depth
        jobs = []
        for n in range(4):
            bufs = refs[8 * n : 8 * n + 8]
            jobs.append(Scatter(place, by_device(grads[n]), *bufs[:5], bufs[5:]))
        small = AllSum(place, *refs[32:36])
        order = [d for d in (1, 2, 3) if d < depth] + [0]

        def core(job):
            for d in order:
                for k in (0, 1, 3, 2):
                    job.add_core(d, k)

        def first(job):
            for d in order:
                for k in (1, 0):
                    job.add_one(d, k)

        def second(job):
            for d in order:
                job.add_two(d)

    for n, right in enumerate((dor_ref, dv_ref, dk_ref, dq_ref)):

        @pl.when(step == n)
        def _(n=n, right=right):
            if n == 0:
                left_s[...] = c_ref[...].T
            if n == 1:
                left_s[...] = h_ref[...].T
            half = width // 2
            for part in range(2):
                cols = slice(part * half, (part + 1) * half)
                value = dot_nn(left_s[...], right[:, cols]).astype(BF16)
                if fused:
                    grads[n][..., cols] = value.reshape(grads[n].shape[:-1] + (half,))
                else:
                    grads[n][:, cols] = value
            if fused:
                for d in order:
                    jobs[n].begin(d)
                if n > 0:
                    core(jobs[n - 1])

    @pl.when(step >= 4)
    def _():
        here = pl.ds(pl.multiple_of((step - 4) * block, block), block)
        dq, dk, dv = dq_ref[here, :], dk_ref[here, :], dv_ref[here, :]

        @pl.when(step == 4)
        def _():
            sums_s[...] = jnp.zeros_like(sums_s)

        dh = (
            dot_nt(dq, wq_ref[...].reshape(width, width))
            + dot_nt(dk, wk_ref[...].reshape(width, width))
            + dot_nt(dv, wv_ref[...].reshape(width, width))
        )
        hat, inverse = norm_parts(x_ref[...].astype(F32))
        sums_s[0:1, :] += col_sum(dh * hat)
        sums_s[1:2, :] += col_sum(dh)
        sums_s[2:3, :] += col_sum(dq.astype(F32))
        sums_s[3:4, :] += col_sum(dv.astype(F32))
        dx_ref[...] = dx2_ref[...] + norm_back(dh * gain_ref[...], hat, inverse)

    if fused:
        at_steps(step, {
            4: [functools.partial(core, jobs[3]), functools.partial(first, jobs[0])],
            5: [functools.partial(first, jobs[1])],
            6: [functools.partial(first, jobs[2]), functools.partial(second, jobs[0])],
            7: [functools.partial(first, jobs[3]), functools.partial(second, jobs[1])],
        })

    @pl.when(step == last)
    def _():
        if fused:
            stages = refs[32]
            stages[0] = small_ref[...]
            stages[0, 0:4, :] = sums_s[0:4, :]
            small.begin()
            second(jobs[2])
            small.add(0)
            second(jobs[3])
            small.add(1)
            small.add(2)
            for job, out in zip(jobs, grad_refs):
                out[...] = job.total()
            small_out[...] = small.total()
            small.finish()
            for job in jobs:
                job.finish()
        else:
            small_out[...] = small_ref[...]
            small_out[0:4, :] = sums_s[0:4, :]


def last_stage(dq, dk, dv, dor, h, c, w, w_specs, x, dx2, gain, small, rows, ffn, block, fused):
    seq, width = dq.shape
    nb = seq // block
    part = pl.BlockSpec((block, width), lambda i: (clip(i, 4, nb), 0))
    full = whole((seq, width))
    piece = (width // (rows * ffn), width)
    depth = ffn // 2
    scratch = [pltpu.VMEM((width, seq), BF16), pltpu.VMEM((8, width), F32)]
    out_specs = [part, out_whole(small.shape)]
    out_shape = [sds((seq, width), F32), sds(small.shape, F32)]
    if fused:
        scratch = [pltpu.VMEM((rows, ffn) + piece, BF16)] * 4 + scratch + scatter_scratch(piece, rows, depth) * 4 + [
            pltpu.VMEM((6,) + small.shape, F32),
            pltpu.VMEM((depth,) + small.shape, F32),
            pltpu.SemaphoreType.DMA((2 + depth,)),
            pltpu.SemaphoreType.DMA((2 + depth,)),
        ]
        out_specs += [pl.BlockSpec(memory_space=pltpu.VMEM)] * 4
        out_shape += [sds(piece, F32)] * 4
    else:
        out_specs += [out_whole((width, width))] * 4
        out_shape += [sds((width, width), BF16)] * 4
    return pl.pallas_call(
        functools.partial(last_kernel, rows=rows, ffn=ffn, block=block, fused=fused),
        grid=(4 + nb,),
        in_specs=[full] * 6 + list(w_specs) + [part, part, whole((1, width)), whole(small.shape)],
        out_specs=out_specs,
        out_shape=out_shape,
        scratch_shapes=scratch,
        compiler_params=params(60 * MIB, has_side_effects=fused),
        name="input_and_weights",
    )(dq, dk, dv, dor, h, c, *[w] * 3, x, dx2, gain, small)


def widen(blocks, lanes):
    nb, rows, hb = blocks.shape
    group = max(1, lanes // hb)
    if group == 1:
        return blocks
    return blocks.reshape(nb // group, group, rows, hb).transpose(0, 2, 1, 3).reshape(nb // group, rows, group * hb)


def narrow(blocks, hb):
    nb, rows, lanes = blocks.shape
    group = lanes // hb
    if group == 1:
        return blocks
    return blocks.reshape(nb, rows, group, hb).transpose(0, 2, 1, 3).reshape(nb * group, rows, hb)


def rows_of(vector):
    return vector.reshape(1, -1)


def shards(
    tokens, lengths, cotangent, ln_attn_gain, ln_attn_bias, w_query, query_bias, w_key, w_value, value_bias,
    head_scale, w_out, out_bias, post_gain, post_bias, ffn_gain, ffn_bias, w_up, up_bias, mid_gain, mid_bias,
    w_down, down_bias,
):
    seq, width = tokens.shape
    heads = head_scale.shape[0]
    head = width // heads
    factor = head ** (-0.5)
    block = min(seq, 256)
    rows, ffn = lax.axis_size("rows"), lax.axis_size("ffn")
    own_units = w_up.shape[1]
    hidden = own_units * ffn
    fused = w_query.shape[0] % 16 == 0 and own_units % 128 == 0
    four = jnp.stack([w_query, w_key, w_value, w_out])
    vectors = [
        rows_of(v)
        for v in (
            ln_attn_gain, ln_attn_bias, query_bias, value_bias, out_bias, post_gain, post_bias, ffn_gain, ffn_bias,
        )
    ]
    if fused:
        weights = (four, w_down, w_up)
    else:
        attn, down_all, up_all = gather_all(rows, ffn, [four], [w_down, w_up])
        attn = attn.transpose(2, 0, 1, 3, 4).reshape(4, width, width)
        weights = (attn,)
    h, q, k, v, c, lse, o, x2, h2, *gathered = front(
        lengths, head_scale, tokens, vectors, weights, rows, ffn, block, head, factor, fused
    )
    if fused:
        attn, down_all, up_all = gathered

        def w_spec(i):
            return pl.BlockSpec(
                (rows, ffn, None) + four.shape[1:], lambda *_: (0, 0, i, 0, 0), pipeline_mode=pl.Buffered(1)
            )

    else:

        def w_spec(i):
            return pl.BlockSpec((None, width, width), lambda *_: (i, 0, 0), pipeline_mode=pl.Buffered(1))

    wup = widen(up_all.reshape(ffn, width, own_units), 512)
    wdn = widen(down_all.reshape(ffn, width, own_units), 512)
    nb, _, hb = wup.shape
    units = lambda vector: vector.reshape(nb, 1, hb)
    result, dh2, m, du, g_ub, g_mg, g_mb, g_db = feed_forward(
        lengths, h2, cotangent, x2, wup, wdn, units(up_bias), units(mid_gain), units(mid_bias), rows_of(down_bias),
        block,
    )
    g_up, g_dn = ffn_weight_grads(lengths, h2, cotangent, m, du)
    g_up, g_dn = (narrow(part, own_units).reshape((ffn, rows) + w_up.shape) for part in (g_up, g_dn))
    scale_cols = rows_of(jnp.repeat(head_scale, head))
    dx2, dor, dq, dk, dv, g_hs, g_fg, g_fb, g_pg, g_pb, g_ob, *summed = back(
        lengths, dh2, cotangent, x2, o, c, attn, w_spec(3), rows_of(ffn_gain), rows_of(post_gain), scale_cols, q, k, v,
        lse, (g_dn, g_up), rows, ffn, block, head, factor, fused,
    )
    if fused:
        grad_down, grad_up = summed
    else:
        grad_down, grad_up = (scatter_sum(rows, ffn, part, by_unit) for part in (g_dn, g_up))
    g_hs = jnp.pad(rows_of(g_hs[:, 0] / head_scale), ((0, 0), (0, width - heads)))
    wide = [part.reshape(-1, width) for part in (g_ub, g_mg, g_mb)]
    small = jnp.concatenate([jnp.zeros((4, width), F32), g_ob, g_pg, g_pb, g_fg, g_fb, g_db, g_hs] + wide, axis=0)
    small = jnp.pad(small, ((0, -small.shape[0] % 8), (0, 0)))
    dx, small, *attn_grads = last_stage(
        dq, dk, dv, dor, h, c, attn, [w_spec(i) for i in range(3)], tokens, dx2, rows_of(ln_attn_gain), small, rows, ffn,
        block, fused,
    )
    if not fused:
        small = lax.psum(small, BOTH)
        attn_grads = [
            scatter_sum(rows, ffn, part.reshape((rows, ffn) + w_query.shape), by_device) for part in attn_grads
        ]
    g_wo, g_wv, g_wk, g_wq = attn_grads
    n = hidden // width
    mine = lax.axis_index("ffn") * own_units
    g_ub, g_mg, g_mb = (
        lax.dynamic_slice(small[11 + i * n : 11 + (i + 1) * n].reshape(hidden), (mine,), (own_units,)) for i in range(3)
    )
    return (
        result, dx, small[0], small[1], g_wq, small[2], g_wk, g_wv, small[3], small[10, :heads], g_wo, small[4],
        small[5], small[6], small[7], small[8], grad_up, g_ub, g_mg, g_mb, grad_down, small[9],
    )


def solution(mesh):
    split = P(BOTH, None)
    tiles = P("rows", "ffn")
    one = P()
    return jax.shard_map(
        shards,
        mesh=mesh,
        in_specs=(
            split, P(BOTH), split, one, one, split, one, split, split, one, one, split, one, one, one, one, one,
            tiles, one, one, one, tiles, one,
        ),
        out_specs=(
            split, split, one, one, split, one, split, split, one, one, split, one, one, one, one, one,
            tiles, P("ffn"), P("ffn"), P("ffn"), tiles, one,
        ),
        check_vma=False,
    )
```

```python
import functools
import math

import jax
import jax.numpy as jnp
from jax import lax
from jax.experimental import pallas as pl
from jax.experimental.pallas import tpu as pltpu
from jax.sharding import PartitionSpec as P

epsilon = 1e-05
masked_score = -1e30
F32 = jnp.float32
BF16 = jnp.bfloat16
MIB = 1 << 20
BOTH = ("rows", "ffn")


def dot_nn(left, right):
    return lax.dot_general(left, right, (((1,), (0,)), ((), ())), preferred_element_type=F32)


def dot_nt(left, right):
    return lax.dot_general(left, right, (((1,), (1,)), ((), ())), preferred_element_type=F32)


def dot_tn(left, right):
    return lax.dot_general(left, right, (((0,), (0,)), ((), ())), preferred_element_type=F32)


def params(limit=56 * MIB, **kw):
    return pltpu.CompilerParams(vmem_limit_bytes=limit, **kw)


def comm_params(fused, number):
    return dict(has_side_effects=True, collective_id=number) if fused else {}


def whole(shape):
    return pl.BlockSpec(shape, lambda *_: (0,) * len(shape), pipeline_mode=pl.Buffered(1))


def out_whole(shape):
    return pl.BlockSpec(shape, lambda *_: (0,) * len(shape))


def sds(shape, dtype):
    return jax.ShapeDtypeStruct(shape, dtype)


def norm_parts(values):
    center = jnp.mean(values, axis=-1, keepdims=True)
    centered = values - center
    spread = jnp.mean(centered * centered, axis=-1, keepdims=True)
    inverse = lax.rsqrt(spread + epsilon)
    return centered * inverse, inverse


def norm_back(grad_hat, hat, inverse):
    return (
        grad_hat
        - jnp.mean(grad_hat, axis=-1, keepdims=True)
        - hat * jnp.mean(grad_hat * hat, axis=-1, keepdims=True)
    ) * inverse


def col_sum(values):
    return jnp.sum(values, axis=0, keepdims=True)


class Place:
    def __init__(self, rows, ffn):
        self.rows, self.ffn, self.depth = rows, ffn, ffn // 2
        self.r = lax.axis_index("rows")
        f = lax.axis_index("ffn")
        self.z, self.c = f // 2, lax.rem(f, 2)

    def row_flip(self, r, bit):
        return r + 1 - 2 * lax.rem(r, 2) if bit == 0 else lax.rem(r + 2, 4)

    def z_at(self, d):
        return lax.rem(self.z + d + self.depth, self.depth)

    def near(self, k):
        if self.depth != 4:
            return self.z_at(k)
        inward = 1 - 2 * (self.z // 2)
        inner = lax.rem(self.z, 3) // 1
        inner = inner - (inner // 2)
        if k == 0:
            return self.z
        if k == 1:
            return self.z + inward * (1 - 2 * inner)
        return self.z + inward * (k - inner)

    def device(self, r, z, c):
        return (r, 2 * z + c)

    def enter(self):
        barrier = pltpu.get_barrier_semaphore()
        partners = [self.device(self.r, self.z, 1 - self.c)]
        partners += [self.device(self.row_flip(self.r, bit), self.z, self.c) for bit in range(2)]
        partners += [self.device(self.r, self.z_at(d), self.c) for d in range(1, self.depth)]
        for partner in partners:
            pl.semaphore_signal(barrier, inc=1, device_id=partner, device_id_type=pl.DeviceIdType.MESH)
        pl.semaphore_wait(barrier, len(partners))


def remote(src, dst, send, recv, device):
    return pltpu.make_async_remote_copy(
        src_ref=src, dst_ref=dst, send_sem=send, recv_sem=recv, device_id=device, device_id_type=pl.DeviceIdType.MESH
    )


class Gather:
    def __init__(self, place, src, view, many, sems):
        self.place, self.src, self.view, self.many = place, src, view, many
        self.local, self.send, self.recv, self.core = sems

    def copy(self, src, kind, r, z, c, device, arrival):
        return remote(src, self.view(r, z, c), self.send.at[kind], arrival, device)

    def to_near(self, src, kind, r, z, device):
        self.copy(src, kind, r, z, self.place.c, device, self.recv.at[r, z]).start()

    def wait_piece(self, r, z):
        there = self.view(r, z, self.place.c)
        pltpu.make_async_copy(there, there, self.recv.at[r, z]).wait()

    def bits(self, d):
        return (0, 1) if d % 2 == 0 else (1, 0)

    def begin_z(self, d=0):
        p = self.place
        for k in range(1, p.depth):
            self.to_near(self.src, 0, p.r, p.z, p.device(p.r, p.near(k), p.c))

    def begin_rows(self, d=0):
        p = self.place
        pltpu.make_async_copy(self.src, self.view(p.r, p.z, p.c), self.local).start()
        self.spread(0, self.src)

    def spread(self, d, src=None):
        p = self.place
        z = p.near(d)
        src = self.view(p.r, z, p.c) if src is None else src
        for bit in self.bits(d):
            self.to_near(src, 1, p.r, z, p.device(p.row_flip(p.r, bit), p.z, p.c))
        self.hand_over(p.r, z, src)

    def hand_over(self, r, z, src=None):
        p = self.place
        src = self.view(r, z, p.c) if src is None else src
        self.copy(src, 2, r, z, p.c, p.device(p.r, p.z, 1 - p.c), self.core).start()

    def take_z(self, d):
        p = self.place
        self.wait_piece(p.r, p.near(d))
        self.spread(d)

    def take_first(self, d):
        p = self.place
        z = p.near(d)
        first, second = self.bits(d)
        r = p.row_flip(p.r, first)
        self.wait_piece(r, z)
        self.to_near(self.view(r, z, p.c), 1, r, z, p.device(p.row_flip(p.r, second), p.z, p.c))
        self.hand_over(r, z)

    def take_rest(self, d):
        p = self.place
        z = p.near(d)
        for r in (p.row_flip(p.r, self.bits(d)[1]), p.row_flip(p.row_flip(p.r, 0), 1)):
            self.wait_piece(r, z)
            self.hand_over(r, z)

    def finish(self):
        p = self.place
        pltpu.make_async_copy(self.src, self.view(p.r, p.z, p.c), self.local).wait()
        half = self.many(slice(None), slice(None), p.c)
        pltpu.make_async_copy(half, half, self.core).wait()
        pltpu.make_async_copy(half, half, self.send.at[2]).wait()
        part = self.many(slice(0, 3), slice(None), p.c)
        pltpu.make_async_copy(part, part, self.send.at[1]).wait()
        part = self.many(0, slice(0, p.depth - 1), p.c)
        pltpu.make_async_copy(part, part, self.send.at[0]).wait()


def gather_sems(jobs, rows, depth):
    dma = pltpu.SemaphoreType.DMA
    return [dma((jobs,)), dma((jobs, 3)), dma((jobs, rows, depth)), dma((jobs,))]


def gather_jobs(place, four, four_all, down, down_all, up, up_all, sems):
    local, send, recv, core = sems
    jobs = []

    def add(src, many):
        n = len(jobs)
        jobs.append(Gather(place, src, many, many, (local.at[n], send.at[n], recv.at[n], core.at[n])))

    for i in range(4):
        add(four.at[i], lambda r, z, c, i=i: four_all.at[r, z, c, i])
    half = down.shape[0] // 2
    for src, out in ((down, down_all), (up, up_all)):
        for i in range(2):
            part = pl.ds(i * half, half)
            add(src.at[part], lambda r, z, c, out=out, part=part: out.at[z, c, r, part])
    return jobs


def gather_kernel(four, down, up, four_all, down_all, up_all, *sems, rows, ffn):
    place = Place(rows, ffn)
    jobs = gather_jobs(place, four, four_all, down, down_all, up, up_all, sems)
    place.enter()
    for job in jobs:
        job.begin_z()
        job.begin_rows()
    for job in jobs:
        for d in range(1, place.depth):
            job.take_z(d)
    for job in jobs:
        for d in range(place.depth):
            job.take_first(d)
    for job in jobs:
        for d in range(place.depth):
            job.take_rest(d)
        job.finish()


def gathered_shapes(rows, ffn, four, down, up):
    depth = ffn // 2
    return [sds((rows, depth, 2) + four.shape, BF16)] + [sds((depth, 2, rows) + a.shape, BF16) for a in (down, up)]


def gather_all(rows, ffn, four, down, up):
    hbm = pl.BlockSpec(memory_space=pl.ANY)
    return pl.pallas_call(
        functools.partial(gather_kernel, rows=rows, ffn=ffn),
        in_specs=[hbm] * 3,
        out_specs=[hbm] * 3,
        out_shape=gathered_shapes(rows, ffn, four, down, up),
        scratch_shapes=gather_sems(8, rows, ffn // 2),
        compiler_params=pltpu.CompilerParams(has_side_effects=True, collective_id=3),
        name="gather_all",
    )(four, down, up)


ROWS_FIRST = 8
STRIDE = 6
BACK_FROM = 0
BACK_STRIDE = 4
LAST_ONE = 2
LAST_TWO = 4
LAST_ORDER = ("leave", "add_one", "add_two", "stay")


def gather_rounds(jobs, depth, rows_first):
    rounds = [[(n, "begin_rows", 0) for n in range(rows_first)]]
    for t in range(jobs + 2):
        todo = []
        if t < jobs:
            todo += [(t, "begin_rows", 0)] if t >= rows_first else []
            todo += [(t, "take_z", d) for d in range(1, depth)]
        rounds.append(todo)
        rounds.append([(t - 1, "take_first", d) for d in range(depth)] if 0 <= t - 1 < jobs else [])
        rounds.append([(t - 2, "take_rest", d) for d in range(depth)] if 0 <= t - 2 < jobs else [])
    return rounds


def by_device(ref):
    return lambda r, z, c: ref.at[r, z, c]


def by_unit(ref, part=slice(None)):
    return lambda r, z, c: ref.at[z, c, r, part]


class Scatter:
    def __init__(self, place, view, own, half, pair, last, far, sems):
        self.place, self.view, self.own, self.half, self.pair, self.last, self.far = place, view, own, half, pair, last, far
        self.load, self.send, self.recv = sems

    def bits(self, d):
        return (0, 1) if d % 2 == 0 else (1, 0)

    def sum_at(self, d, r):
        if self.own is None:
            return self.view(r, self.place.z_at(d), self.place.c)
        return self.own.at[d, r]

    def copy(self, src, dst, kind, arrival, d, device):
        return remote(src, dst, self.send.at[kind], self.recv.at[arrival, d], device)

    def fetch(self, d, r):
        p = self.place
        return pltpu.make_async_copy(self.view(r, p.z_at(d), p.c), self.own.at[d, r], self.load.at[r, d])

    def begin(self, d):
        p = self.place
        first, _ = self.bits(d)
        leaving = p.row_flip(p.r, first)
        for base in (leaving, p.r):
            for r in (base, p.row_flip(base, 1 - first)):
                self.copy(
                    self.view(r, p.z_at(d), 1 - p.c), self.half.at[d, r], 0, r, d, p.device(p.r, p.z, 1 - p.c)
                ).start()
                if self.own is not None:
                    self.fetch(d, r).start()

    def arrived(self, ref, arrival, d):
        pltpu.make_async_copy(ref, ref, self.recv.at[arrival, d]).wait()

    def add(self, d, r, ref):
        here = self.sum_at(d, r)
        here[...] = here[...] + ref[...]

    def add_half(self, d, r):
        if self.own is not None:
            self.fetch(d, r).wait()
        self.arrived(self.half.at[d, r], r, d)
        self.add(d, r, self.half.at[d, r])

    def leave(self, d):
        p = self.place
        first, second = self.bits(d)
        partner = p.row_flip(p.r, first)
        for k, r in enumerate((partner, p.row_flip(partner, second))):
            self.add_half(d, r)
            self.copy(self.sum_at(d, r), self.pair.at[d, k], 1, 4 + k, d, p.device(partner, p.z, p.c)).start()

    def stay(self, d):
        p = self.place
        for r in (p.row_flip(p.r, self.bits(d)[1]), p.r):
            self.add_half(d, r)

    def add_one(self, d):
        p = self.place
        partner = p.row_flip(p.r, self.bits(d)[1])
        for k, r in ((1, partner), (0, p.r)):
            self.arrived(self.pair.at[d, k], 4 + k, d)
            self.add(d, r, self.pair.at[d, k])
            if k == 1:
                self.copy(self.sum_at(d, r), self.last.at[d], 2, 6, d, p.device(partner, p.z, p.c)).start()

    def add_two(self, d):
        p = self.place
        self.arrived(self.last.at[d], 6, d)
        self.add(d, p.r, self.last.at[d])
        if d > 0:
            self.copy(self.sum_at(d, p.r), self.far.at[d], 3, 7, d, p.device(p.r, p.z_at(d), p.c)).start()

    def total(self):
        p = self.place
        out = self.sum_at(0, p.r)[...].astype(F32)
        for d in range(1, p.depth):
            self.arrived(self.far.at[d], 7, d)
            out = out + self.far[d].astype(F32)
        return out

    def finish(self):
        for kind, ref in enumerate((self.half, self.pair, self.last, self.far.at[pl.ds(1, self.place.depth - 1)])):
            pltpu.make_async_copy(ref, ref, self.send.at[kind]).wait()


def scatter_rounds(jobs, depth):
    order = list(range(1, depth)) + [0]
    rounds = []
    for t in range(jobs + 2):
        rounds.append([(t, "leave", d) for d in order] if t < jobs else [])
        rounds.append([(t - 1, "add_one", d) for d in order] if 0 <= t - 1 < jobs else [])
        rounds.append([(t - 2, "add_two", d) for d in order] if 0 <= t - 2 < jobs else [])
        rounds.append([(t, "stay", d) for d in order] if t < jobs else [])
    return rounds


def scatter_kernel(src, out, own, half, pair, last, far, load, send, recv, *, rows, ffn, view):
    place = Place(rows, ffn)
    job = Scatter(place, view(src), own, half, pair, last, far, (load, send, recv))
    order = list(range(1, place.depth)) + [0]
    place.enter()
    for name in ("begin", "leave", "stay", "add_one", "add_two"):
        for d in order:
            getattr(job, name)(d)
    out[...] = job.total()
    job.finish()


def scatter_scratch(piece, rows, depth, own):
    return ([pltpu.VMEM((depth, rows) + piece, BF16)] if own else []) + [
        pltpu.VMEM((depth, rows) + piece, BF16),
        pltpu.VMEM((depth, 2) + piece, BF16),
        pltpu.VMEM((depth,) + piece, BF16),
        pltpu.VMEM((depth,) + piece, BF16),
        pltpu.SemaphoreType.DMA((4, depth)),
        pltpu.SemaphoreType.DMA((4,)),
        pltpu.SemaphoreType.DMA((8, depth)),
    ]


def scatter_sum(rows, ffn, grad, view):
    piece = grad.shape[3:]
    return pl.pallas_call(
        functools.partial(scatter_kernel, rows=rows, ffn=ffn, view=view),
        in_specs=[pl.BlockSpec(memory_space=pl.ANY)],
        out_specs=pl.BlockSpec(memory_space=pltpu.VMEM),
        out_shape=sds(piece, F32),
        scratch_shapes=scatter_scratch(piece, rows, ffn // 2, True),
        compiler_params=params(has_side_effects=True, collective_id=4),
        name="scatter_sum",
    )(grad)


def clip(step, low, count):
    return jnp.minimum(jnp.maximum(step - low, 0), count - 1)


def at_steps(step, plan):
    for when, actions in sorted(plan.items()):

        @pl.when(step == when)
        def _(actions=actions):
            for action in actions:
                action()


def attend_pair(length, scales, q_of, k, v, seq, block, head, store):
    lanes = 2 * head
    lane = lax.broadcasted_iota(jnp.int32, (block, lanes), 1)
    for i in range(seq // block):
        keys_here = (i + 1) * block
        q = q_of(i)
        key_pos = lax.broadcasted_iota(jnp.int32, (block, keys_here), 1)
        row_pos = lax.broadcasted_iota(jnp.int32, (block, keys_here), 0) + i * block
        allowed = key_pos < jnp.minimum(row_pos + 1, length)
        ctx = None
        logs = []
        for n in range(2):
            mine = (lane < head) if n == 0 else (lane >= head)
            scores = dot_nt(jnp.where(mine, q, 0), k[:keys_here, :])
            scores = jnp.where(allowed, scores, masked_score)
            peak = jnp.max(scores, axis=-1, keepdims=True)
            weights = jnp.exp(scores - peak)
            total = jnp.sum(weights, axis=-1, keepdims=True)
            part = dot_nn(weights.astype(BF16), v[:keys_here, :]) * (scales[n] / total)
            ctx = part if n == 0 else jnp.where(lane < head, ctx, part)
            logs.append(peak + jnp.log(total))
        store(i, ctx.astype(BF16), jnp.where(lane < head, logs[0], logs[1]).T)


def front_kernel(*refs, rows, ffn, block, head, factor, fused):
    n_in = 14 if fused else 12
    (length_ref, scale_ref, x_ref, lg_ref, lb_ref, qb_ref, vb_ref, ob_ref, pg_ref, pb_ref, fg_ref) = refs[:11]
    fb_ref = refs[11]
    comm_in = refs[12 : 15 if fused else 13]
    refs = refs[15 if fused else 13 :]
    h_ref, q_ref, k_ref, v_ref, c_ref, lse_ref, o_ref, x2_ref, h2_ref = refs[:9]
    comm_out = refs[9:12] if fused else ()
    refs = refs[12 if fused else 9 :]
    w_s, q_s, k_s, v_s, c_s, load = refs[:6]
    step = pl.program_id(0)
    seq, width = q_s.shape
    nb = seq // block
    pairs = width // (2 * head)
    last = 2 * nb + pairs - 1

    def load_weights(source):
        copies = [pltpu.make_async_copy(source(i), w_s.at[i], load.at[i]) for i in range(4)]
        for copy in copies:
            copy.start()
        for copy in copies:
            copy.wait()

    late = {}
    if fused:
        place = Place(rows, ffn)
        jobs = gather_jobs(
            place, comm_in[0], comm_out[0], comm_in[1], comm_out[1], comm_in[2], comm_out[2], refs[6:10]
        )
        rounds = gather_rounds(len(jobs), place.depth, ROWS_FIRST)
        cut = 1 + 3 * 6
        opening = sum(rounds[:cut], [])
        table = {}
        for k, keys in enumerate(rounds[cut:]):
            table.setdefault(min(1 + k * STRIDE // 4, last), []).extend(keys)

        def actions(keys):
            return [functools.partial(getattr(jobs[n], name), d) for n, name, d in keys]

        @pl.when(step == 0)
        def _():
            place.enter()
            for job in jobs:
                job.begin_z()
            for action in actions(opening):
                action()
            copies = [pltpu.make_async_copy(comm_out[0].at[:, :, :, i], w_s.at[i], load.at[i]) for i in range(4)]
            for job, copy in zip(jobs, copies):
                job.finish()
                copy.start()
            for copy in copies:
                copy.wait()

        late = {i: actions(keys) for i, keys in table.items() if keys and i < last}
        at_steps(step, late)
    else:

        @pl.when(step == 0)
        def _():
            load_weights(lambda i: comm_in[0].at[i])

    def weight(i):
        return w_s[i].reshape(width, width)

    @pl.when(step < nb)
    def _():
        here = pl.ds(pl.multiple_of(step * block, block), block)
        hat, _ = norm_parts(x_ref[...].astype(F32))
        h = (hat * lg_ref[...] + lb_ref[...]).astype(BF16)
        h_ref[...] = h
        q = ((dot_nn(h, weight(0)) + qb_ref[...]).astype(BF16).astype(F32) * factor).astype(BF16)
        k = dot_nn(h, weight(1)).astype(BF16)
        v = (dot_nn(h, weight(2)) + vb_ref[...]).astype(BF16)
        for ref, scratch, value in ((q_ref, q_s, q), (k_ref, k_s, k), (v_ref, v_s, v)):
            ref[...] = value
            scratch[here, :] = value

    @pl.when((step >= nb) & (step < nb + pairs))
    def _():
        pair = step - nb
        cols = pl.ds(pl.multiple_of(pair * (2 * head), 2 * head), 2 * head)

        def store(i, ctx, logs):
            c_s[i * block : (i + 1) * block, cols] = ctx
            for n in range(2):
                lse_ref[0, n : n + 1, i * block : (i + 1) * block] = logs[n * head : n * head + 1, :]

        attend_pair(
            length_ref[0], [scale_ref[2 * pair + n] for n in range(2)],
            lambda i: q_s[i * block : (i + 1) * block, cols], k_s[:, cols], v_s[:, cols], seq, block, head, store,
        )

    @pl.when(step >= nb + pairs)
    def _():
        here = pl.ds(pl.multiple_of((step - nb - pairs) * block, block), block)
        c = c_s[here, :]
        c_ref[...] = c
        o = dot_nn(c, weight(3)) + ob_ref[...]
        o_ref[...] = o
        hat, _ = norm_parts(o)
        x2 = x_ref[...].astype(F32) + (hat * pg_ref[...] + pb_ref[...])
        x2_ref[...] = x2
        hat2, _ = norm_parts(x2)
        h2_ref[...] = (hat2 * fg_ref[...] + fb_ref[...]).astype(BF16)

    if fused:

        @pl.when(step == last)
        def _():
            for action in actions(table.get(last, [])):
                action()
            for job in jobs[4:]:
                job.finish()


def front(length, scale, x, vectors, weights, rows, ffn, block, head, factor, fused):
    seq, width = x.shape
    nb, pairs = seq // block, width // (2 * head)
    steps = 2 * nb + pairs
    x_rows = pl.BlockSpec((block, width), lambda i: (jnp.where(i < nb + pairs, jnp.minimum(i, nb - 1), i - nb - pairs), 0))
    first = pl.BlockSpec((block, width), lambda i: (clip(i, 0, nb), 0))
    final = pl.BlockSpec((block, width), lambda i: (clip(i, nb + pairs, nb), 0))
    smem = pl.BlockSpec(memory_space=pltpu.SMEM)
    hbm = pl.BlockSpec(memory_space=pl.ANY)
    out_specs = [first] * 4 + [final, pl.BlockSpec((1, 2, seq), lambda i: (clip(i, nb, pairs), 0, 0))] + [final] * 3
    out_shape = [sds((seq, width), BF16)] * 5 + [sds((pairs, 2, seq), F32)] + [sds((seq, width), F32)] * 2
    out_shape += [sds((seq, width), BF16)]
    scratch = [pltpu.VMEM((seq, width), BF16)] * 4 + [pltpu.SemaphoreType.DMA((4,))]
    if fused:
        four, down, up = weights
        out_shape += gathered_shapes(rows, ffn, four, down, up)
        out_specs += [hbm] * 3
        scratch = [pltpu.VMEM((4, rows, ffn // 2, 2) + four.shape[1:], BF16)] + scratch
        scratch += gather_sems(8, rows, ffn // 2)
    else:
        scratch = [pltpu.VMEM((4, width, width), BF16)] + scratch
    return pl.pallas_call(
        functools.partial(front_kernel, rows=rows, ffn=ffn, block=block, head=head, factor=factor, fused=fused),
        grid=(steps,),
        in_specs=[smem, smem, x_rows] + [whole((1, width))] * 9 + [hbm] * len(weights),
        out_specs=out_specs,
        out_shape=out_shape,
        scratch_shapes=scratch,
        compiler_params=params(60 * MIB, **comm_params(fused, 0)),
        name="forward_attention",
    )(length, scale, x, *vectors, *weights)


def ffn_kernel(
    length_ref, h2_ref, ct_ref, x2_ref, wup_ref, wdn_ref, ub_ref, mg_ref, mb_ref, db_ref,
    res_ref, dh2_ref, m_ref, du_ref, gub_ref, gmg_ref, gmb_ref, gdb_ref,
    e_s, gp_s, dm_s,
):
    step = pl.program_id(0)
    block, width = h2_ref.shape
    nb, _, hb = wup_ref.shape
    units = nb * hb
    row = lax.broadcasted_iota(jnp.int32, (block, width), 0) + step * block
    valid = row < length_ref[0]
    h2 = h2_ref[...]
    dfr = jnp.where(valid, ct_ref[...].astype(F32), 0.0).astype(BF16)

    @pl.when(step == 0)
    def _():
        gub_ref[...] = jnp.zeros_like(gub_ref)
        gmg_ref[...] = jnp.zeros_like(gmg_ref)
        gmb_ref[...] = jnp.zeros_like(gmb_ref)
        gdb_ref[...] = jnp.zeros_like(gdb_ref)

    gdb_ref[...] += col_sum(dfr.astype(F32))

    def first(j, sums):
        u = dot_nn(h2, wup_ref[j]) + ub_ref[j]
        dm = dot_nn(dfr, wdn_ref[j])
        cdf = 0.5 * (1.0 + lax.erf(u * math.sqrt(0.5)))
        e = u * cdf
        gp = cdf + u * (jnp.exp(u * u * -0.5) * (1.0 / math.sqrt(2.0 * math.pi)))
        dmh = dm * mg_ref[j]
        e_s[j] = e
        gp_s[j] = gp
        dm_s[j] = dm
        terms = (e, e * e, dmh, dmh * e)
        return tuple(s + jnp.sum(t, axis=-1, keepdims=True) for s, t in zip(sums, terms))

    zero = jnp.zeros((block, 1), F32)
    sum_e, sum_ee, sum_d, sum_de = lax.fori_loop(0, nb, first, (zero,) * 4, unroll=2)
    mu = sum_e / units
    inverse = lax.rsqrt(sum_ee / units - mu * mu + epsilon)
    mean_d = sum_d / units
    mean_dh = (sum_de - mu * sum_d) * inverse / units

    def second(j, sums):
        f, dh2 = sums
        ehat = (e_s[j] - mu) * inverse
        dm = dm_s[j]
        m = (ehat * mg_ref[j] + mb_ref[j]).astype(BF16)
        m_ref[j] = m
        f = f + dot_nt(m, wdn_ref[j])
        de = (dm * mg_ref[j] - mean_d - ehat * mean_dh) * inverse
        du = (de * gp_s[j]).astype(BF16)
        du_ref[j] = du
        dh2 = dh2 + dot_nt(du, wup_ref[j])
        gub_ref[j] += col_sum(du.astype(F32))
        gmg_ref[j] += col_sum(dm * ehat)
        gmb_ref[j] += col_sum(dm)
        return f, dh2

    zeros = jnp.zeros((block, width), F32)
    f, dh2 = lax.fori_loop(0, nb, second, (zeros, zeros), unroll=2)
    res_ref[...] = jnp.where(valid, x2_ref[...] + f + db_ref[...], 0.0)
    dh2_ref[...] = dh2


def feed_forward(length, h2, ct, x2, wup, wdn, ub, mg, mb, db, block):
    seq, width = h2.shape
    nb, _, hb = wup.shape
    rows = pl.BlockSpec((block, width), lambda i: (i, 0))
    smem = pl.BlockSpec(memory_space=pltpu.SMEM)
    units = whole((nb, 1, hb))
    blocks = pl.BlockSpec((nb, block, hb), lambda i: (0, i, 0))
    sums = out_whole((nb, 1, hb))
    return pl.pallas_call(
        ffn_kernel,
        grid=(seq // block,),
        in_specs=[
            smem, rows, rows, rows, whole((nb, width, hb)), whole((nb, width, hb)),
            units, units, units, whole((1, width)),
        ],
        out_specs=[rows, rows, blocks, blocks, sums, sums, sums, out_whole((1, width))],
        out_shape=[
            sds((seq, width), F32), sds((seq, width), F32), sds((nb, seq, hb), BF16), sds((nb, seq, hb), BF16),
            sds((nb, 1, hb), F32), sds((nb, 1, hb), F32), sds((nb, 1, hb), F32), sds((1, width), F32),
        ],
        scratch_shapes=[pltpu.VMEM((nb, block, hb), F32)] * 3,
        compiler_params=params(60 * MIB),
        cost_estimate=pl.CostEstimate(
            flops=16 * seq * width * nb * hb, bytes_accessed=60 * MIB, transcendentals=2 * seq * nb * hb
        ),
        name="feed_forward",
    )(length, h2, ct, x2, wup, wdn, ub, mg, mb, db)


def ffn_weights_kernel(length_ref, h2_ref, ct_ref, m_ref, du_ref, gup_ref, gdn_ref, h2t_s, dft_s):
    seq, width = h2_ref.shape

    @pl.when(pl.program_id(0) == 0)
    def _():
        row = lax.broadcasted_iota(jnp.int32, (seq, width), 0)
        dfr = jnp.where(row < length_ref[0], ct_ref[...], 0)
        h2t_s[...] = h2_ref[...].T
        dft_s[...] = dfr.T

    gdn_ref[0] = dot_nn(dft_s[...], m_ref[0]).astype(BF16)
    gup_ref[0] = dot_nn(h2t_s[...], du_ref[0]).astype(BF16)


def ffn_weight_grads(length, h2, ct, m, du):
    seq, width = h2.shape
    nb, _, hb = m.shape
    smem = pl.BlockSpec(memory_space=pltpu.SMEM)
    block = pl.BlockSpec((1, seq, hb), lambda j: (j, 0, 0))
    out = pl.BlockSpec((1, width, hb), lambda j: (j, 0, 0))
    return pl.pallas_call(
        ffn_weights_kernel,
        grid=(nb,),
        in_specs=[smem, whole((seq, width)), whole((seq, width)), block, block],
        out_specs=[out, out],
        out_shape=[sds((nb, width, hb), BF16)] * 2,
        scratch_shapes=[pltpu.VMEM((width, seq), BF16)] * 2,
        compiler_params=params(),
        cost_estimate=pl.CostEstimate(
            flops=4 * seq * width * nb * hb, bytes_accessed=36 * MIB, transcendentals=0
        ),
        name="ffn_weight_grads",
    )(length, h2, ct, m, du)


def attend_back_pair(length, q_all, k_of, v_of, g_all, lse_ref, inner_row, dq_s, store, seq, block, head):
    lanes = 2 * head
    lane = lax.broadcasted_iota(jnp.int32, (seq, lanes), 1)
    dq_s[...] = jnp.zeros_like(dq_s)
    zero = jnp.zeros_like(q_all)
    q_heads = [jnp.where(lane < head, q_all, zero), jnp.where(lane >= head, q_all, zero)]
    g_heads = [jnp.where(lane < head, g_all, zero), jnp.where(lane >= head, g_all, zero)]
    for j in range(seq // block):
        start = j * block
        width = seq - start
        k, v = k_of(j), v_of(j)
        key_pos = lax.broadcasted_iota(jnp.int32, (block, width), 0) + start
        row_pos = lax.broadcasted_iota(jnp.int32, (block, width), 1) + start
        allowed = (key_pos <= row_pos) & (key_pos < length)
        dk = dv = None
        dqs = []
        for n in range(2):
            q = q_heads[n][start:, :]
            g = g_heads[n][start:, :]
            scores = dot_nt(k, q)
            probs = jnp.where(allowed, jnp.exp(scores - lse_ref[0, n : n + 1, start:]), 0.0)
            grad_probs = dot_nt(v, g)
            grad_scores = (probs * (grad_probs - inner_row(n)[:, start:])).astype(BF16)
            dv_part = dot_nn(probs.astype(BF16), g)
            dk_part = dot_nn(grad_scores, q)
            dv = dv_part if n == 0 else dv + dv_part
            dk = dk_part if n == 0 else dk + dk_part
            dqs.append(dot_tn(grad_scores, k))
        dq_s[start:, :] += jnp.where(lane[start:, :] < head, dqs[0], dqs[1])
        store(j, dk.astype(BF16), dv.astype(BF16))


def back_kernel(*refs, rows, ffn, block, head, factor, fused):
    (
        length_ref, dh2_ref, ct_ref, x2_ref, o_ref, c_ref, w_ref, fg_ref, pg_ref, hs_ref, q_ref, k_ref, v_ref, lse_ref,
    ) = refs[:14]
    comm_in = refs[14:16] if fused else ()
    refs = refs[16 if fused else 14 :]
    (
        dx2_ref, dor_ref, dq_ref, dk_ref, dv_ref, ghs_ref, gfg_ref, gfb_ref, gpg_ref, gpb_ref, gob_ref,
    ) = refs[:11]
    comm_out = refs[11:13] if fused else ()
    refs = refs[13 if fused else 11 :]
    g_s, inner_s, dq_s = refs[:3]
    step = pl.program_id(0)
    seq, width = g_s.shape
    nb = seq // block
    pairs = width // (2 * head)
    heads = width // head
    last = nb + pairs - 1

    if fused:
        place = Place(rows, ffn)
        depth = place.depth
        jobs = []
        half = comm_out[0].shape[0] // 2
        for n in range(4):
            bufs = refs[3 + 8 * n : 11 + 8 * n]
            part = pl.ds(n % 2 * half, half)
            jobs.append(Scatter(place, by_unit(comm_in[n // 2], part), *bufs[:5], bufs[5:]))
        rounds = scatter_rounds(4, depth)
        table = {}
        for k, keys in enumerate(rounds):
            table.setdefault(min(max(0, k - BACK_FROM) * BACK_STRIDE // 8, last), []).extend(keys)

        def actions(keys):
            return [functools.partial(getattr(jobs[n], name), d) for n, name, d in keys]

        order = list(range(1, depth)) + [0]
        begin = [functools.partial(job.begin, d) for job in jobs for d in order]
        plan = {i: actions(keys) for i, keys in table.items() if i < last}
        plan[0] = [place.enter] + begin + plan[0]
        at_steps(step, {i: todo for i, todo in plan.items() if todo})

    @pl.when(step < nb)
    def _():
        row = lax.broadcasted_iota(jnp.int32, (block, width), 0) + step * block
        dy = jnp.where(row < length_ref[0], ct_ref[...].astype(F32), 0.0)

        @pl.when(step == 0)
        def _():
            for ref in (gfg_ref, gfb_ref, gpg_ref, gpb_ref, gob_ref, ghs_ref):
                ref[...] = jnp.zeros_like(ref)

        dh2 = dh2_ref[...]
        hat2, inverse2 = norm_parts(x2_ref[...])
        gfg_ref[...] += col_sum(dh2 * hat2)
        gfb_ref[...] += col_sum(dh2)
        dx2 = dy + norm_back(dh2 * fg_ref[...], hat2, inverse2)
        dx2_ref[...] = dx2
        hat, inverse = norm_parts(o_ref[...])
        gpg_ref[...] += col_sum(dx2 * hat)
        gpb_ref[...] += col_sum(dx2)
        dor = norm_back(dx2 * pg_ref[...], hat, inverse).astype(BF16)
        dor_ref[...] = dor
        gob_ref[...] += col_sum(dor.astype(F32))
        dc = dot_nt(dor, w_ref[...].reshape(width, width))
        here = pl.ds(pl.multiple_of(step * block, block), block)
        g_s[here, :] = (dc * hs_ref[...]).astype(BF16)
        product = dc * c_ref[...].astype(F32)
        high = product.astype(BF16)
        low = (product - high.astype(F32)).astype(BF16)
        owner = lax.broadcasted_iota(jnp.int32, (heads, width), 1) // head
        pick = (owner == lax.broadcasted_iota(jnp.int32, (heads, width), 0)).astype(BF16)
        inner = dot_nt(pick, high) + dot_nt(pick, low)
        inner_s[step] = inner
        ghs_ref[...] += jnp.broadcast_to(jnp.sum(inner, axis=-1, keepdims=True), ghs_ref.shape)

    @pl.when(step >= nb)
    def _():
        pair = step - nb
        cols = pl.ds(pl.multiple_of(pair * (2 * head), 2 * head), 2 * head)
        inner_rows = [
            jnp.concatenate([inner_s[i, pl.ds(2 * pair + n, 1), :] for i in range(nb)], axis=1) for n in range(2)
        ]

        def store(j, dk, dv):
            dk_ref[j * block : (j + 1) * block, :] = dk
            dv_ref[j * block : (j + 1) * block, :] = dv

        attend_back_pair(
            length_ref[0], q_ref[...], lambda j: k_ref[j * block : (j + 1) * block, :],
            lambda j: v_ref[j * block : (j + 1) * block, :], g_s[:, cols], lse_ref, lambda n: inner_rows[n], dq_s, store,
            seq, block, head,
        )
        dq_ref[...] = (dq_s[...] * factor).astype(BF16)

    if fused:

        @pl.when(step == last)
        def _():
            for action in actions(table.get(last, [])):
                action()
            for n, job in enumerate(jobs):
                comm_out[n // 2][n % 2 * half : (n % 2 + 1) * half, :] = job.total()
                job.finish()


def back(length, dh2, ct, x2, o, c, w, w_spec, fg, pg, hs, q, k, v, lse, grads, rows, ffn, block, head, factor, fused):
    seq, width = dh2.shape
    nb, pairs, heads = seq // block, width // (2 * head), width // head
    part = pl.BlockSpec((block, width), lambda i: (clip(i, 0, nb), 0))
    cols = pl.BlockSpec((seq, 2 * head), lambda i: (0, clip(i, nb, pairs)))
    smem = pl.BlockSpec(memory_space=pltpu.SMEM)
    hbm = pl.BlockSpec(memory_space=pl.ANY)
    vec, ovec = whole((1, width)), out_whole((1, width))
    out_specs = [part] * 2 + [cols] * 3 + [out_whole((heads, 128))] + [ovec] * 5
    out_shape = [sds((seq, width), F32), sds((seq, width), BF16)] + [sds((seq, width), BF16)] * 3
    out_shape += [sds((heads, 128), F32)] + [sds((1, width), F32)] * 5
    scratch = [
        pltpu.VMEM((seq, width), BF16), pltpu.VMEM((nb, heads, block), F32), pltpu.VMEM((seq, 2 * head), F32),
    ]
    if fused:
        piece = grads[0].shape[3:]
        out_specs += [pl.BlockSpec(memory_space=pltpu.VMEM)] * 2
        out_shape += [sds(piece, F32)] * 2
        scratch += scatter_scratch((piece[0] // 2, piece[1]), rows, ffn // 2, True) * 4
    else:
        grads = ()
    return pl.pallas_call(
        functools.partial(back_kernel, rows=rows, ffn=ffn, block=block, head=head, factor=factor, fused=fused),
        grid=(nb + pairs,),
        in_specs=[smem] + [part] * 5 + [w_spec] + [vec] * 3 + [cols] * 3
        + [pl.BlockSpec((1, 2, seq), lambda i: (clip(i, nb, pairs), 0, 0))] + [hbm] * len(grads),
        out_specs=out_specs,
        out_shape=out_shape,
        scratch_shapes=scratch,
        compiler_params=params(60 * MIB, **comm_params(fused, 1)),
        name="backward_attention",
    )(length, dh2, ct, x2, o, c, w, fg, pg, hs, q, k, v, lse, *grads)


class AllSum:
    def __init__(self, place, stages, far, send, recv):
        self.place, self.stages, self.far, self.send, self.recv = place, stages, far, send, recv

    def copy(self, k):
        p = self.place
        device = (
            p.device(p.r, p.z, 1 - p.c), p.device(p.row_flip(p.r, 0), p.z, p.c), p.device(p.row_flip(p.r, 1), p.z, p.c)
        )[k]
        return remote(self.stages.at[k], self.stages.at[3 + k], self.send.at[k], self.recv.at[k], device)

    def along(self, d):
        p = self.place
        return remote(
            self.far.at[p.z], self.far.at[p.z], self.send.at[2 + d], self.recv.at[2 + d], p.device(p.r, p.z_at(d), p.c)
        )

    def begin(self):
        self.copy(0).start()

    def add(self, k):
        self.copy(k).wait_recv()
        total = self.stages[k] + self.stages[3 + k]
        if k < 2:
            self.stages[k + 1] = total
            self.copy(k + 1).start()
        else:
            self.far[self.place.z] = total
            for d in range(1, self.place.depth):
                self.along(d).start()

    def total(self):
        p = self.place
        for d in range(1, p.depth):
            there = self.far.at[p.z_at(-d)]
            pltpu.make_async_copy(there, there, self.recv.at[2 + d]).wait()
        out = self.far[0]
        for z in range(1, p.depth):
            out = out + self.far[z]
        return out

    def finish(self):
        for k in range(3):
            self.copy(k).wait_send()
        for d in range(1, self.place.depth):
            self.along(d).wait_send()


def last_kernel(*refs, rows, ffn, block, fused):
    (
        dq_ref, dk_ref, dv_ref, dor_ref, h_ref, c_ref, wq_ref, wk_ref, wv_ref, x_ref, dx2_ref, gain_ref, small_ref,
    ) = refs[:13]
    refs = refs[13:]
    dx_ref, small_out = refs[:2]
    refs = refs[2:]
    grad_refs = refs[:4]
    refs = refs[4:]
    if fused:
        grads = refs[:4]
        left_s, sums_s = refs[4:6]
        refs = refs[6:]
    else:
        grads = grad_refs
        left_s, sums_s = refs[:2]
    step = pl.program_id(0)
    seq, width = dq_ref.shape
    nb = seq // block
    last = 4 + nb - 1

    if fused:
        place = Place(rows, ffn)
        depth = place.depth
        jobs = []
        for n in range(4):
            bufs = refs[7 * n : 7 * n + 7]
            jobs.append(Scatter(place, by_device(grads[n]), None, *bufs[:4], bufs[4:]))
        small = AllSum(place, *refs[28:32])
        table = {}
        for n in range(4):
            for k, (name, when) in enumerate((("leave", 1), ("stay", 1), ("add_one", 1 + LAST_ONE), ("add_two", 1 + LAST_TWO))):
                table.setdefault(min(n + when, last + 1), []).extend((n, name, d) for d in list(range(1, depth)) + [0])

        def actions(keys):
            return [functools.partial(getattr(jobs[n], name), d) for n, name, d in keys]

        order = list(range(1, depth)) + [0]
        plan = {i: actions(sorted(keys, key=lambda key: LAST_ORDER.index(key[1]))) for i, keys in table.items() if i <= last}
        rest = table.get(last + 1, [])
        plan[0] = []
        plan[0] = [place.enter] + plan[0]
        at_steps(step, {i: todo for i, todo in plan.items() if todo})

    for n, right in enumerate((dor_ref, dv_ref, dk_ref, dq_ref)):

        @pl.when(step == n)
        def _(n=n, right=right):
            if n == 0:
                left_s[...] = c_ref[...].T
            if n == 1:
                left_s[...] = h_ref[...].T
            half = width // 2
            for part in range(2):
                cols = slice(part * half, (part + 1) * half)
                value = dot_nn(left_s[...], right[:, cols]).astype(BF16)
                if fused:
                    grads[n][..., cols] = value.reshape(grads[n].shape[:-1] + (half,))
                else:
                    grads[n][:, cols] = value
            if fused:
                for d in order:
                    jobs[n].begin(d)

    @pl.when(step >= 4)
    def _():
        here = pl.ds(pl.multiple_of((step - 4) * block, block), block)
        dq, dk, dv = dq_ref[here, :], dk_ref[here, :], dv_ref[here, :]

        @pl.when(step == 4)
        def _():
            sums_s[...] = jnp.zeros_like(sums_s)

        dh = (
            dot_nt(dq, wq_ref[...].reshape(width, width))
            + dot_nt(dk, wk_ref[...].reshape(width, width))
            + dot_nt(dv, wv_ref[...].reshape(width, width))
        )
        hat, inverse = norm_parts(x_ref[...].astype(F32))
        sums_s[0:1, :] += col_sum(dh * hat)
        sums_s[1:2, :] += col_sum(dh)
        sums_s[2:3, :] += col_sum(dq.astype(F32))
        sums_s[3:4, :] += col_sum(dv.astype(F32))
        dx_ref[...] = dx2_ref[...] + norm_back(dh * gain_ref[...], hat, inverse)

    @pl.when(step == last)
    def _():
        if fused:
            stages = refs[28]
            stages[0] = small_ref[...]
            stages[0, 0:4, :] = sums_s[0:4, :]
            small.begin()
            half = len(rest) // 2
            for action in actions(rest[:half]):
                action()
            small.add(0)
            for action in actions(rest[half:]):
                action()
            small.add(1)
            small.add(2)
            for job, out in zip(jobs, grad_refs):
                out[...] = job.total()
            small_out[...] = small.total()
            small.finish()
            for job in jobs:
                job.finish()
        else:
            small_out[...] = small_ref[...]
            small_out[0:4, :] = sums_s[0:4, :]


def last_stage(dq, dk, dv, dor, h, c, w, w_specs, x, dx2, gain, small, rows, ffn, block, fused):
    seq, width = dq.shape
    nb = seq // block
    part = pl.BlockSpec((block, width), lambda i: (clip(i, 4, nb), 0))
    full = whole((seq, width))
    piece = (width // (rows * ffn), width)
    depth = ffn // 2
    scratch = [pltpu.VMEM((width, seq), BF16), pltpu.VMEM((8, width), F32)]
    out_specs = [part, out_whole(small.shape)]
    out_shape = [sds((seq, width), F32), sds(small.shape, F32)]
    if fused:
        scratch = [pltpu.VMEM((rows, depth, 2) + piece, BF16)] * 4 + scratch
        scratch += scatter_scratch(piece, rows, depth, False) * 4 + [
            pltpu.VMEM((6,) + small.shape, F32),
            pltpu.VMEM((depth,) + small.shape, F32),
            pltpu.SemaphoreType.DMA((2 + depth,)),
            pltpu.SemaphoreType.DMA((2 + depth,)),
        ]
        out_specs += [pl.BlockSpec(memory_space=pltpu.VMEM)] * 4
        out_shape += [sds(piece, F32)] * 4
    else:
        out_specs += [out_whole((width, width))] * 4
        out_shape += [sds((width, width), BF16)] * 4
    return pl.pallas_call(
        functools.partial(last_kernel, rows=rows, ffn=ffn, block=block, fused=fused),
        grid=(4 + nb,),
        in_specs=[full] * 6 + list(w_specs) + [part, part, whole((1, width)), whole(small.shape)],
        out_specs=out_specs,
        out_shape=out_shape,
        scratch_shapes=scratch,
        compiler_params=params(60 * MIB, **comm_params(fused, 2)),
        name="input_and_weights",
    )(dq, dk, dv, dor, h, c, *[w] * 3, x, dx2, gain, small)


def widen(blocks, lanes):
    nb, rows, hb = blocks.shape
    group = max(1, lanes // hb)
    if group == 1:
        return blocks
    return blocks.reshape(nb // group, group, rows, hb).transpose(0, 2, 1, 3).reshape(nb // group, rows, group * hb)


def narrow(blocks, hb):
    nb, rows, lanes = blocks.shape
    group = lanes // hb
    if group == 1:
        return blocks
    return blocks.reshape(nb, rows, group, hb).transpose(0, 2, 1, 3).reshape(nb * group, rows, hb)


def rows_of(vector):
    return vector.reshape(1, -1)


def shards(
    tokens, lengths, cotangent, ln_attn_gain, ln_attn_bias, w_query, query_bias, w_key, w_value, value_bias,
    head_scale, w_out, out_bias, post_gain, post_bias, ffn_gain, ffn_bias, w_up, up_bias, mid_gain, mid_bias,
    w_down, down_bias,
):
    seq, width = tokens.shape
    heads = head_scale.shape[0]
    head = width // heads
    factor = head ** (-0.5)
    block = min(seq, 256)
    rows, ffn = lax.axis_size("rows"), lax.axis_size("ffn")
    own_units = w_up.shape[1]
    hidden = own_units * ffn
    fused = w_query.shape[0] % 16 == 0 and own_units % 128 == 0
    four = jnp.stack([w_query, w_key, w_value, w_out])
    vectors = [
        rows_of(v)
        for v in (
            ln_attn_gain, ln_attn_bias, query_bias, value_bias, out_bias, post_gain, post_bias, ffn_gain, ffn_bias,
        )
    ]
    if fused:
        weights = (four, w_down, w_up)
    else:
        attn, down_all, up_all = gather_all(rows, ffn, four, w_down, w_up)
        attn = attn.transpose(3, 0, 1, 2, 4, 5).reshape(4, width, width)
        weights = (attn,)
    h, q, k, v, c, lse, o, x2, h2, *gathered = front(
        lengths, head_scale, tokens, vectors, weights, rows, ffn, block, head, factor, fused
    )
    if fused:
        attn, down_all, up_all = gathered

        def w_spec(i):
            return pl.BlockSpec(
                (rows, ffn // 2, 2, None) + four.shape[1:], lambda *_: (0, 0, 0, i, 0, 0), pipeline_mode=pl.Buffered(1)
            )

    else:

        def w_spec(i):
            return pl.BlockSpec((None, width, width), lambda *_: (i, 0, 0), pipeline_mode=pl.Buffered(1))

    wup = widen(up_all.reshape(ffn, width, own_units), 512)
    wdn = widen(down_all.reshape(ffn, width, own_units), 512)
    nb, _, hb = wup.shape
    units = lambda vector: vector.reshape(nb, 1, hb)
    result, dh2, m, du, g_ub, g_mg, g_mb, g_db = feed_forward(
        lengths, h2, cotangent, x2, wup, wdn, units(up_bias), units(mid_gain), units(mid_bias), rows_of(down_bias),
        block,
    )
    g_up, g_dn = ffn_weight_grads(lengths, h2, cotangent, m, du)
    g_up, g_dn = (narrow(part, own_units).reshape((ffn // 2, 2, rows) + w_up.shape) for part in (g_up, g_dn))
    scale_cols = rows_of(jnp.repeat(head_scale, head))
    dx2, dor, dq, dk, dv, g_hs, g_fg, g_fb, g_pg, g_pb, g_ob, *summed = back(
        lengths, dh2, cotangent, x2, o, c, attn, w_spec(3), rows_of(ffn_gain), rows_of(post_gain), scale_cols, q, k, v,
        lse, (g_dn, g_up), rows, ffn, block, head, factor, fused,
    )
    if fused:
        grad_down, grad_up = summed
    else:
        grad_down, grad_up = (scatter_sum(rows, ffn, part, by_unit) for part in (g_dn, g_up))
    g_hs = jnp.pad(rows_of(g_hs[:, 0] / head_scale), ((0, 0), (0, width - heads)))
    wide = [part.reshape(-1, width) for part in (g_ub, g_mg, g_mb)]
    small = jnp.concatenate([jnp.zeros((4, width), F32), g_ob, g_pg, g_pb, g_fg, g_fb, g_db, g_hs] + wide, axis=0)
    small = jnp.pad(small, ((0, -small.shape[0] % 8), (0, 0)))
    dx, small, *attn_grads = last_stage(
        dq, dk, dv, dor, h, c, attn, [w_spec(i) for i in range(3)], tokens, dx2, rows_of(ln_attn_gain), small, rows, ffn,
        block, fused,
    )
    if not fused:
        small = lax.psum(small, BOTH)
        attn_grads = [
            scatter_sum(rows, ffn, part.reshape((rows, ffn // 2, 2) + w_query.shape), by_device) for part in attn_grads
        ]
    g_wo, g_wv, g_wk, g_wq = attn_grads
    n = hidden // width
    mine = lax.axis_index("ffn") * own_units
    g_ub, g_mg, g_mb = (
        lax.dynamic_slice(small[11 + i * n : 11 + (i + 1) * n].reshape(hidden), (mine,), (own_units,)) for i in range(3)
    )
    return (
        result, dx, small[0], small[1], g_wq, small[2], g_wk, g_wv, small[3], small[10, :heads], g_wo, small[4],
        small[5], small[6], small[7], small[8], grad_up, g_ub, g_mg, g_mb, grad_down, small[9],
    )


def solution(mesh):
    split = P(BOTH, None)
    tiles = P("rows", "ffn")
    one = P()
    return jax.shard_map(
        shards,
        mesh=mesh,
        in_specs=(
            split, P(BOTH), split, one, one, split, one, split, split, one, one, split, one, one, one, one, one,
            tiles, one, one, one, tiles, one,
        ),
        out_specs=(
            split, split, one, one, split, one, split, split, one, one, split, one, one, one, one, one,
            tiles, P("ffn"), P("ffn"), P("ffn"), tiles, one,
        ),
        check_vma=False,
    )
```

```python
import functools
import math

import jax
import jax.numpy as jnp
from jax import lax
from jax.experimental import pallas as pl
from jax.experimental.pallas import tpu as pltpu
from jax.sharding import PartitionSpec as P

epsilon = 1e-05
masked_score = -1e30
F32 = jnp.float32
BF16 = jnp.bfloat16
MIB = 1 << 20
BOTH = ("rows", "ffn")


def dot_nn(left, right):
    return lax.dot_general(left, right, (((1,), (0,)), ((), ())), preferred_element_type=F32)


def dot_nt(left, right):
    return lax.dot_general(left, right, (((1,), (1,)), ((), ())), preferred_element_type=F32)


def dot_tn(left, right):
    return lax.dot_general(left, right, (((0,), (0,)), ((), ())), preferred_element_type=F32)


def params(limit=56 * MIB, **kw):
    return pltpu.CompilerParams(vmem_limit_bytes=limit, **kw)


def comm_params(fused, number):
    return dict(has_side_effects=True, collective_id=number) if fused else {}


def whole(shape):
    return pl.BlockSpec(shape, lambda *_: (0,) * len(shape), pipeline_mode=pl.Buffered(1))


def out_whole(shape):
    return pl.BlockSpec(shape, lambda *_: (0,) * len(shape))


def sds(shape, dtype):
    return jax.ShapeDtypeStruct(shape, dtype)


def norm_parts(values):
    center = jnp.mean(values, axis=-1, keepdims=True)
    centered = values - center
    spread = jnp.mean(centered * centered, axis=-1, keepdims=True)
    inverse = lax.rsqrt(spread + epsilon)
    return centered * inverse, inverse


def norm_back(grad_hat, hat, inverse):
    return (
        grad_hat
        - jnp.mean(grad_hat, axis=-1, keepdims=True)
        - hat * jnp.mean(grad_hat * hat, axis=-1, keepdims=True)
    ) * inverse


def col_sum(values):
    return jnp.sum(values, axis=0, keepdims=True)


class Place:
    def __init__(self, rows, ffn):
        self.rows, self.ffn, self.depth = rows, ffn, ffn // 2
        self.r = lax.axis_index("rows")
        f = lax.axis_index("ffn")
        self.z, self.c = f // 2, lax.rem(f, 2)

    def row_flip(self, r, bit):
        return r + 1 - 2 * lax.rem(r, 2) if bit == 0 else lax.rem(r + 2, 4)

    def z_at(self, d):
        return lax.rem(self.z + d + self.depth, self.depth)

    def near(self, k):
        if self.depth != 4:
            return self.z_at(k)
        inward = 1 - 2 * (self.z // 2)
        inner = lax.rem(self.z, 3) // 1
        inner = inner - (inner // 2)
        if k == 0:
            return self.z
        if k == 1:
            return self.z + inward * (1 - 2 * inner)
        return self.z + inward * (k - inner)

    def device(self, r, z, c):
        return (r, 2 * z + c)

    def enter(self, near=True):
        barrier = pltpu.get_barrier_semaphore()
        partners = [self.device(self.r, self.z, 1 - self.c)]
        if near:
            partners += [self.device(self.row_flip(self.r, bit), self.z, self.c) for bit in range(2)]
            partners += [self.device(self.r, self.z_at(d), self.c) for d in range(1, self.depth)]
        for partner in partners:
            pl.semaphore_signal(barrier, inc=1, device_id=partner, device_id_type=pl.DeviceIdType.MESH)
        pl.semaphore_wait(barrier, len(partners))


def remote(src, dst, send, recv, device):
    return pltpu.make_async_remote_copy(
        src_ref=src, dst_ref=dst, send_sem=send, recv_sem=recv, device_id=device, device_id_type=pl.DeviceIdType.MESH
    )


class Gather:
    def __init__(self, place, src, view, many, sems):
        self.place, self.src, self.view, self.many = place, src, view, many
        self.local, self.send, self.recv, self.core = sems

    def copy(self, src, kind, r, z, c, device, arrival):
        return remote(src, self.view(r, z, c), self.send.at[kind], arrival, device)

    def to_near(self, src, kind, r, z, device):
        self.copy(src, kind, r, z, self.place.c, device, self.recv.at[r, z]).start()

    def wait_piece(self, r, z):
        there = self.view(r, z, self.place.c)
        pltpu.make_async_copy(there, there, self.recv.at[r, z]).wait()

    def bits(self, d):
        return (0, 1) if d % 2 == 0 else (1, 0)

    def begin_z(self, d=0):
        p = self.place
        for k in range(1, p.depth):
            self.to_near(self.src, 0, p.r, p.z, p.device(p.r, p.near(k), p.c))

    def begin_rows(self, d=0):
        p = self.place
        pltpu.make_async_copy(self.src, self.view(p.r, p.z, p.c), self.local).start()
        self.spread(0, self.src)

    def spread(self, d, src=None):
        p = self.place
        z = p.near(d)
        src = self.view(p.r, z, p.c) if src is None else src
        for bit in self.bits(d):
            self.to_near(src, 1, p.r, z, p.device(p.row_flip(p.r, bit), p.z, p.c))
        self.hand_over(p.r, z, src)

    def hand_over(self, r, z, src=None):
        p = self.place
        src = self.view(r, z, p.c) if src is None else src
        self.copy(src, 2, r, z, p.c, p.device(p.r, p.z, 1 - p.c), self.core).start()

    def take_z(self, d):
        p = self.place
        self.wait_piece(p.r, p.near(d))
        self.spread(d)

    def take_first(self, d):
        p = self.place
        z = p.near(d)
        first, second = self.bits(d)
        r = p.row_flip(p.r, first)
        self.wait_piece(r, z)
        self.to_near(self.view(r, z, p.c), 1, r, z, p.device(p.row_flip(p.r, second), p.z, p.c))
        self.hand_over(r, z)

    def take_rest(self, d):
        p = self.place
        z = p.near(d)
        for r in (p.row_flip(p.r, self.bits(d)[1]), p.row_flip(p.row_flip(p.r, 0), 1)):
            self.wait_piece(r, z)
            self.hand_over(r, z)

    def finish(self):
        p = self.place
        pltpu.make_async_copy(self.src, self.view(p.r, p.z, p.c), self.local).wait()
        half = self.many(slice(None), slice(None), p.c)
        pltpu.make_async_copy(half, half, self.core).wait()
        pltpu.make_async_copy(half, half, self.send.at[2]).wait()
        part = self.many(slice(0, 3), slice(None), p.c)
        pltpu.make_async_copy(part, part, self.send.at[1]).wait()
        part = self.many(0, slice(0, p.depth - 1), p.c)
        pltpu.make_async_copy(part, part, self.send.at[0]).wait()


def gather_sems(jobs, rows, depth):
    dma = pltpu.SemaphoreType.DMA
    return [dma((jobs,)), dma((jobs, 3)), dma((jobs, rows, depth)), dma((jobs,))]


def gather_jobs(place, shards, four_all, down_all, up_all, sems):
    local, send, recv, core = sems
    jobs = []

    def add(src, many):
        n = len(jobs)
        jobs.append(Gather(place, src, many, many, (local.at[n], send.at[n], recv.at[n], core.at[n])))

    for i in range(4):
        add(shards[i], lambda r, z, c, i=i: four_all.at[r, z, c, i])
    half = shards[4].shape[0] // 2
    for src, out in ((shards[4], down_all), (shards[5], up_all)):
        for i in range(2):
            part = pl.ds(i * half, half)
            add(src.at[part], lambda r, z, c, out=out, part=part: out.at[z, c, r, part])
    return jobs


def gather_kernel(*refs, rows, ffn):
    place = Place(rows, ffn)
    jobs = gather_jobs(place, refs[:6], *refs[6:9], refs[9:])
    place.enter()
    for job in jobs:
        job.begin_z()
        job.begin_rows()
    for job in jobs:
        for d in range(1, place.depth):
            job.take_z(d)
    for job in jobs:
        for d in range(place.depth):
            job.take_first(d)
    for job in jobs:
        for d in range(place.depth):
            job.take_rest(d)
        job.finish()


def gathered_shapes(rows, ffn, shards):
    depth = ffn // 2
    return [sds((rows, depth, 2, 4) + shards[0].shape, BF16)] + [sds((depth, 2, rows) + a.shape, BF16) for a in shards[4:]]


def gather_all(rows, ffn, shards):
    hbm = pl.BlockSpec(memory_space=pl.ANY)
    return pl.pallas_call(
        functools.partial(gather_kernel, rows=rows, ffn=ffn),
        in_specs=[hbm] * 6,
        out_specs=[hbm] * 3,
        out_shape=gathered_shapes(rows, ffn, shards),
        scratch_shapes=gather_sems(8, rows, ffn // 2),
        compiler_params=pltpu.CompilerParams(has_side_effects=True, collective_id=3),
        name="gather_all",
    )(*shards)


ROWS_FIRST = 8
STRIDE = 6


def gather_rounds(jobs, depth, rows_first):
    rounds = [[(n, "begin_rows", 0) for n in range(rows_first)]]
    for t in range(jobs + 2):
        todo = []
        if t < jobs:
            todo += [(t, "begin_rows", 0)] if t >= rows_first else []
            todo += [(t, "take_z", d) for d in range(1, depth)]
        rounds.append(todo)
        rounds.append([(t - 1, "take_first", d) for d in range(depth)] if 0 <= t - 1 < jobs else [])
        rounds.append([(t - 2, "take_rest", d) for d in range(depth)] if 0 <= t - 2 < jobs else [])
    return rounds


def by_device(ref):
    return lambda r, z, c: ref.at[r, z, c]


def by_unit(ref, part=slice(None)):
    return lambda r, z, c: ref.at[z, c, r, part]


class Scatter:
    def __init__(self, place, view, own, half, pair, last, far, sems):
        self.place, self.view, self.own, self.half, self.pair, self.last, self.far = place, view, own, half, pair, last, far
        self.load, self.send, self.recv = sems

    def bits(self, d):
        return (0, 1) if d % 2 == 0 else (1, 0)

    def sum_at(self, d, r):
        if self.own is None:
            return self.view(r, self.place.z_at(d), self.place.c)
        return self.own.at[d, r]

    def copy(self, src, dst, kind, arrival, d, device):
        return remote(src, dst, self.send.at[kind], self.recv.at[arrival, d], device)

    def fetch(self, d, r):
        p = self.place
        return pltpu.make_async_copy(self.view(r, p.z_at(d), p.c), self.own.at[d, r], self.load.at[r, d])

    def begin(self, d):
        p = self.place
        first, _ = self.bits(d)
        leaving = p.row_flip(p.r, first)
        for base in (leaving, p.r):
            for r in (base, p.row_flip(base, 1 - first)):
                self.copy(
                    self.view(r, p.z_at(d), 1 - p.c), self.half.at[d, r], 0, r, d, p.device(p.r, p.z, 1 - p.c)
                ).start()
                if self.own is not None:
                    self.fetch(d, r).start()

    def arrived(self, ref, arrival, d):
        pltpu.make_async_copy(ref, ref, self.recv.at[arrival, d]).wait()

    def add(self, d, r, ref):
        here = self.sum_at(d, r)
        here[...] = here[...] + ref[...]

    def add_half(self, d, r):
        if self.own is not None:
            self.fetch(d, r).wait()
        self.arrived(self.half.at[d, r], r, d)
        self.add(d, r, self.half.at[d, r])

    def leave(self, d):
        p = self.place
        first, second = self.bits(d)
        partner = p.row_flip(p.r, first)
        for k, r in enumerate((partner, p.row_flip(partner, second))):
            self.add_half(d, r)
            self.copy(self.sum_at(d, r), self.pair.at[d, k], 1, 4 + k, d, p.device(partner, p.z, p.c)).start()

    def stay(self, d):
        p = self.place
        for r in (p.row_flip(p.r, self.bits(d)[1]), p.r):
            self.add_half(d, r)

    def add_one(self, d):
        p = self.place
        partner = p.row_flip(p.r, self.bits(d)[1])
        for k, r in ((1, partner), (0, p.r)):
            self.arrived(self.pair.at[d, k], 4 + k, d)
            self.add(d, r, self.pair.at[d, k])
            if k == 1:
                self.copy(self.sum_at(d, r), self.last.at[d], 2, 6, d, p.device(partner, p.z, p.c)).start()

    def add_two(self, d):
        p = self.place
        self.arrived(self.last.at[d], 6, d)
        self.add(d, p.r, self.last.at[d])
        if d > 0:
            self.copy(self.sum_at(d, p.r), self.far.at[d], 3, 7, d, p.device(p.r, p.z_at(d), p.c)).start()

    def total(self):
        p = self.place
        out = self.sum_at(0, p.r)[...].astype(F32)
        for d in range(1, p.depth):
            self.arrived(self.far.at[d], 7, d)
            out = out + self.far[d].astype(F32)
        return out

    def finish(self):
        for kind, ref in enumerate((self.half, self.pair, self.last, self.far.at[pl.ds(1, self.place.depth - 1)])):
            pltpu.make_async_copy(ref, ref, self.send.at[kind]).wait()


class Exchange:
    def __init__(self, place):
        self.place = place
        self.order = list(range(1, place.depth)) + [0]

    def bits(self, d):
        return (0, 1) if d % 2 == 0 else (1, 0)

    def arrived(self, ref, arrival):
        pltpu.make_async_copy(ref, ref, arrival).wait()

    def rows_of_pair(self, d, leaving):
        p = self.place
        first, second = self.bits(d)
        base = p.row_flip(p.r, first) if leaving else p.r
        return base, p.row_flip(base, second)

    def first_exchange(self, d, k, src):
        p = self.place
        partner = p.row_flip(p.r, self.bits(d)[0])
        remote(
            src, self.pair.at[d, k], self.send.at[1], self.recv.at[k, d], p.device(partner, p.z, p.c)
        ).start()

    def one(self):
        p = self.place
        for d in self.order:
            partner = p.row_flip(p.r, self.bits(d)[1])
            for k in (1, 0):
                self.arrived(self.pair.at[d, k], self.recv.at[k, d])
                here = self.kept(d, k)
                here[...] = here[...] + self.other(d, k)[...]
                if k == 1:
                    remote(
                        here, self.last.at[d], self.send.at[2], self.recv.at[2, d], p.device(partner, p.z, p.c)
                    ).start()

    def two(self):
        p = self.place
        for d in self.order:
            self.arrived(self.last.at[d], self.recv.at[2, d])
            here = self.kept(d, 0)
            here[...] = here[...] + self.last[d]
            if d > 0:
                remote(
                    here, self.far.at[d], self.send.at[3], self.recv.at[3, d], p.device(p.r, p.z_at(d), p.c)
                ).start()

    def total(self):
        out = self.kept(0, 0)[...].astype(F32)
        for d in range(1, self.place.depth):
            self.arrived(self.far.at[d], self.recv.at[3, d])
            out = out + self.far[d].astype(F32)
        for kind, ref in ((1, self.pair), (2, self.last), (3, self.far.at[pl.ds(1, self.place.depth - 1)])):
            self.arrived(ref, self.send.at[kind])
        return out


class PairExchange(Exchange):
    def __init__(self, place, view, stage, load, pair, last, far, send, recv):
        super().__init__(place)
        self.view, self.stage, self.load = view, stage, load
        self.pair, self.last, self.far, self.send, self.recv = pair, last, far, send, recv

    def kept(self, d, k):
        return self.pair.at[d, k]

    def other(self, d, k):
        self.fetch(d, k).wait()
        return self.stage.at[d, k]

    def fetch(self, d, k):
        r = self.rows_of_pair(d, False)[k]
        return pltpu.make_async_copy(self.view(r, self.place.z_at(d)), self.stage.at[d, k], self.load.at[d, k])

    def leave(self):
        for d in self.order:
            z = self.place.z_at(d)
            for k, r in enumerate(self.rows_of_pair(d, True)):
                self.first_exchange(d, k, self.view(r, z))
            for k in range(2):
                self.fetch(d, k).start()


class CoreExchange(Exchange):
    def __init__(self, place, view, whole, half, pair, last, far, send, recv):
        super().__init__(place)
        self.view, self.whole, self.half = view, whole, half
        self.pair, self.last, self.far, self.send, self.recv = pair, last, far, send, recv

    def kept(self, d, k):
        return self.half.at[d, self.rows_of_pair(d, False)[k]]

    def other(self, d, k):
        return self.pair.at[d, k]

    def begin(self):
        p = self.place
        for d in self.order:
            for leaving in (True, False):
                for r in self.rows_of_pair(d, leaving):
                    remote(
                        self.view(r, p.z_at(d), 1 - p.c), self.half.at[d, r], self.send.at[0], self.recv.at[4 + r, d],
                        p.device(p.r, p.z, 1 - p.c),
                    ).start()

    def add_core(self, d, r):
        p = self.place
        here = self.half.at[d, r]
        self.arrived(here, self.recv.at[4 + r, d])
        here[...] = here[...] + self.view(r, p.z_at(d), p.c)[...]

    def leave(self):
        for d in self.order:
            for k, r in enumerate(self.rows_of_pair(d, True)):
                self.add_core(d, r)
                self.first_exchange(d, k, self.half.at[d, r])
        for d in self.order:
            for r in self.rows_of_pair(d, False):
                self.add_core(d, r)
        self.arrived(self.half, self.send.at[0])


def scatter_kernel(src, out, own, half, pair, last, far, load, send, recv, *, rows, ffn, view):
    place = Place(rows, ffn)
    job = Scatter(place, view(src), own, half, pair, last, far, (load, send, recv))
    order = list(range(1, place.depth)) + [0]
    place.enter()
    for name in ("begin", "leave", "stay", "add_one", "add_two"):
        for d in order:
            getattr(job, name)(d)
    out[...] = job.total()
    job.finish()


def scatter_scratch(piece, rows, depth, own):
    return ([pltpu.VMEM((depth, rows) + piece, BF16)] if own else []) + [
        pltpu.VMEM((depth, rows) + piece, BF16),
        pltpu.VMEM((depth, 2) + piece, BF16),
        pltpu.VMEM((depth,) + piece, BF16),
        pltpu.VMEM((depth,) + piece, BF16),
        pltpu.SemaphoreType.DMA((4, depth)),
        pltpu.SemaphoreType.DMA((4,)),
        pltpu.SemaphoreType.DMA((8, depth)),
    ]


def scatter_sum(rows, ffn, grad, view):
    piece = grad.shape[3:]
    return pl.pallas_call(
        functools.partial(scatter_kernel, rows=rows, ffn=ffn, view=view),
        in_specs=[pl.BlockSpec(memory_space=pl.ANY)],
        out_specs=pl.BlockSpec(memory_space=pltpu.VMEM),
        out_shape=sds(piece, F32),
        scratch_shapes=scatter_scratch(piece, rows, ffn // 2, True),
        compiler_params=params(has_side_effects=True, collective_id=4),
        name="scatter_sum",
    )(grad)


def clip(step, low, count):
    return jnp.minimum(jnp.maximum(step - low, 0), count - 1)


def at_steps(step, plan):
    for when, actions in sorted(plan.items()):

        @pl.when(step == when)
        def _(actions=actions):
            for action in actions:
                action()


def attend_pair(length, scales, q_of, k, v, seq, block, head, store):
    lanes = 2 * head
    lane = lax.broadcasted_iota(jnp.int32, (block, lanes), 1)
    for i in range(seq // block):
        keys_here = (i + 1) * block
        q = q_of(i)
        key_pos = lax.broadcasted_iota(jnp.int32, (block, keys_here), 1)
        row_pos = lax.broadcasted_iota(jnp.int32, (block, keys_here), 0) + i * block
        allowed = key_pos < jnp.minimum(row_pos + 1, length)
        ctx = None
        logs = []
        for n in range(2):
            mine = (lane < head) if n == 0 else (lane >= head)
            scores = dot_nt(jnp.where(mine, q, 0), k[:keys_here, :])
            scores = jnp.where(allowed, scores, masked_score)
            peak = jnp.max(scores, axis=-1, keepdims=True)
            weights = jnp.exp(scores - peak)
            total = jnp.sum(weights, axis=-1, keepdims=True)
            part = dot_nn(weights.astype(BF16), v[:keys_here, :]) * (scales[n] / total)
            ctx = part if n == 0 else jnp.where(lane < head, ctx, part)
            logs.append(peak + jnp.log(total))
        store(i, ctx.astype(BF16), jnp.where(lane < head, logs[0], logs[1]).T)


def front_kernel(*refs, rows, ffn, block, head, factor, fused):
    (length_ref, scale_ref, x_ref, lg_ref, lb_ref, qb_ref, vb_ref, ob_ref, pg_ref, pb_ref, fg_ref) = refs[:11]
    fb_ref = refs[11]
    comm_in = refs[12 : 18 if fused else 13]
    refs = refs[18 if fused else 13 :]
    h_ref, q_ref, k_ref, v_ref, c_ref, lse_ref, o_ref, x2_ref, h2_ref = refs[:9]
    comm_out = refs[9:12] if fused else ()
    refs = refs[12 if fused else 9 :]
    w_s, q_s, k_s, v_s, c_s, load = refs[:6]
    step = pl.program_id(0)
    seq, width = q_s.shape
    nb = seq // block
    pairs = width // (2 * head)
    last = 2 * nb + pairs - 1

    def load_weights(source):
        copies = [pltpu.make_async_copy(source(i), w_s.at[i], load.at[i]) for i in range(4)]
        for copy in copies:
            copy.start()
        for copy in copies:
            copy.wait()

    late = {}
    if fused:
        place = Place(rows, ffn)
        jobs = gather_jobs(place, comm_in, *comm_out, refs[6:10])
        rounds = gather_rounds(len(jobs), place.depth, ROWS_FIRST)
        cut = 1 + 3 * 6
        opening = sum(rounds[:cut], [])
        table = {}
        for k, keys in enumerate(rounds[cut:]):
            table.setdefault(min(1 + k * STRIDE // 4, last), []).extend(keys)

        def actions(keys):
            return [functools.partial(getattr(jobs[n], name), d) for n, name, d in keys]

        @pl.when(step == 0)
        def _():
            place.enter()
            for job in jobs:
                job.begin_z()
            for action in actions(opening):
                action()
            copies = [pltpu.make_async_copy(comm_out[0].at[:, :, :, i], w_s.at[i], load.at[i]) for i in range(4)]
            for job, copy in zip(jobs, copies):
                job.finish()
                copy.start()
            for copy in copies:
                copy.wait()

        late = {i: actions(keys) for i, keys in table.items() if keys and i < last}
        at_steps(step, late)
    else:

        @pl.when(step == 0)
        def _():
            load_weights(lambda i: comm_in[0].at[i])

    def weight(i):
        return w_s[i].reshape(width, width)

    @pl.when(step < nb)
    def _():
        here = pl.ds(pl.multiple_of(step * block, block), block)
        hat, _ = norm_parts(x_ref[...].astype(F32))
        h = (hat * lg_ref[...] + lb_ref[...]).astype(BF16)
        h_ref[...] = h
        q = ((dot_nn(h, weight(0)) + qb_ref[...]).astype(BF16).astype(F32) * factor).astype(BF16)
        k = dot_nn(h, weight(1)).astype(BF16)
        v = (dot_nn(h, weight(2)) + vb_ref[...]).astype(BF16)
        for scratch, value in ((q_s, q), (k_s, k), (v_s, v)):
            scratch[here, :] = value

    @pl.when((step >= nb) & (step < nb + pairs))
    def _():
        pair = step - nb
        cols = pl.ds(pl.multiple_of(pair * (2 * head), 2 * head), 2 * head)

        def store(i, ctx, logs):
            c_s[i * block : (i + 1) * block, cols] = ctx
            for n in range(2):
                lse_ref[0, n : n + 1, i * block : (i + 1) * block] = logs[n * head : n * head + 1, :]

        for ref, scratch in ((q_ref, q_s), (k_ref, k_s), (v_ref, v_s)):
            ref[...] = scratch[:, cols]
        attend_pair(
            length_ref[0], [scale_ref[2 * pair + n] for n in range(2)],
            lambda i: q_s[i * block : (i + 1) * block, cols], k_s[:, cols], v_s[:, cols], seq, block, head, store,
        )

    @pl.when(step >= nb + pairs)
    def _():
        here = pl.ds(pl.multiple_of((step - nb - pairs) * block, block), block)
        c = c_s[here, :]
        c_ref[...] = c
        o = dot_nn(c, weight(3)) + ob_ref[...]
        o_ref[...] = o
        hat, _ = norm_parts(o)
        x2 = x_ref[...].astype(F32) + (hat * pg_ref[...] + pb_ref[...])
        x2_ref[...] = x2
        hat2, _ = norm_parts(x2)
        h2_ref[...] = (hat2 * fg_ref[...] + fb_ref[...]).astype(BF16)

    if fused:

        @pl.when(step == last)
        def _():
            for action in actions(table.get(last, [])):
                action()
            for job in jobs[4:]:
                job.finish()


def front(length, scale, x, vectors, weights, rows, ffn, block, head, factor, fused):
    seq, width = x.shape
    nb, pairs = seq // block, width // (2 * head)
    steps = 2 * nb + pairs
    x_rows = pl.BlockSpec((block, width), lambda i: (jnp.where(i < nb + pairs, jnp.minimum(i, nb - 1), i - nb - pairs), 0))
    first = pl.BlockSpec((block, width), lambda i: (clip(i, 0, nb), 0))
    final = pl.BlockSpec((block, width), lambda i: (clip(i, nb + pairs, nb), 0))
    smem = pl.BlockSpec(memory_space=pltpu.SMEM)
    hbm = pl.BlockSpec(memory_space=pl.ANY)
    out_specs = [first] + [pl.BlockSpec((None, seq, 2 * head), lambda i: (clip(i, nb, pairs), 0, 0))] * 3
    out_specs += [final, pl.BlockSpec((1, 2, seq), lambda i: (clip(i, nb, pairs), 0, 0))] + [final] * 3
    out_shape = [sds((seq, width), BF16)] + [sds((pairs, seq, 2 * head), BF16)] * 3 + [sds((seq, width), BF16)]
    out_shape += [sds((pairs, 2, seq), F32)] + [sds((seq, width), F32)] * 2
    out_shape += [sds((seq, width), BF16)]
    scratch = [pltpu.VMEM((seq, width), BF16)] * 4 + [pltpu.SemaphoreType.DMA((4,))]
    if fused:
        out_shape += gathered_shapes(rows, ffn, weights)
        out_specs += [hbm] * 3
        scratch = [pltpu.VMEM((4, rows, ffn // 2, 2) + weights[0].shape, BF16)] + scratch
        scratch += gather_sems(8, rows, ffn // 2)
    else:
        scratch = [pltpu.VMEM((4, width, width), BF16)] + scratch
    return pl.pallas_call(
        functools.partial(front_kernel, rows=rows, ffn=ffn, block=block, head=head, factor=factor, fused=fused),
        grid=(steps,),
        in_specs=[smem, smem, x_rows] + [whole((1, width))] * 9 + [hbm] * len(weights),
        out_specs=out_specs,
        out_shape=out_shape,
        scratch_shapes=scratch,
        compiler_params=params(60 * MIB, **comm_params(fused, 0)),
        name="forward_attention",
    )(length, scale, x, *vectors, *weights)


def ffn_kernel(
    length_ref, h2_ref, ct_ref, x2_ref, up_ref, dn_ref, ub_ref, mg_ref, mb_ref, db_ref,
    res_ref, dh2_ref, m_ref, du_ref, gub_ref, gmg_ref, gmb_ref, gdb_ref,
    e_s, gp_s, dm_s, wup_ref, wdn_ref, load,
):
    step = pl.program_id(0)
    block, width = h2_ref.shape
    nb, _, hb = wup_ref.shape

    def loads(j):
        return [
            pltpu.make_async_copy(src.at[j], dst.at[j], load.at[n, j])
            for n, (src, dst) in enumerate(((up_ref, wup_ref), (dn_ref, wdn_ref)))
        ]

    @pl.when(step == 0)
    def _():
        for j in range(nb):
            for copy in loads(j):
                copy.start()
    units = nb * hb
    row = lax.broadcasted_iota(jnp.int32, (block, width), 0) + step * block
    valid = row < length_ref[0]
    h2 = h2_ref[...]
    dfr = jnp.where(valid, ct_ref[...].astype(F32), 0.0).astype(BF16)

    @pl.when(step == 0)
    def _():
        gub_ref[...] = jnp.zeros_like(gub_ref)
        gmg_ref[...] = jnp.zeros_like(gmg_ref)
        gmb_ref[...] = jnp.zeros_like(gmb_ref)
        gdb_ref[...] = jnp.zeros_like(gdb_ref)

    gdb_ref[...] += col_sum(dfr.astype(F32))

    def first(j, sums, wait):
        if wait:
            for copy in loads(j):
                copy.wait()
        u = dot_nn(h2, wup_ref[j]) + ub_ref[j]
        dm = dot_nn(dfr, wdn_ref[j])
        cdf = 0.5 * (1.0 + lax.erf(u * math.sqrt(0.5)))
        e = u * cdf
        gp = cdf + u * (jnp.exp(u * u * -0.5) * (1.0 / math.sqrt(2.0 * math.pi)))
        dmh = dm * mg_ref[j]
        e_s[j] = e
        gp_s[j] = gp
        dm_s[j] = dm
        terms = (e, e * e, dmh, dmh * e)
        return tuple(s + jnp.sum(t, axis=-1, keepdims=True) for s, t in zip(sums, terms))

    def rows(wait):
        zero = jnp.zeros((block, 1), F32)
        sums = (zero,) * 4
        for j in range(nb):
            sums = first(j, sums, wait)
        sum_e, sum_ee, sum_d, sum_de = sums
        mu = sum_e / units
        inverse = lax.rsqrt(sum_ee / units - mu * mu + epsilon)
        mean_d = sum_d / units
        mean_dh = (sum_de - mu * sum_d) * inverse / units

        def second(j, sums):
            f, dh2 = sums
            ehat = (e_s[j] - mu) * inverse
            dm = dm_s[j]
            m = (ehat * mg_ref[j] + mb_ref[j]).astype(BF16)
            m_ref[j] = m
            f = f + dot_nt(m, wdn_ref[j])
            de = (dm * mg_ref[j] - mean_d - ehat * mean_dh) * inverse
            du = (de * gp_s[j]).astype(BF16)
            du_ref[j] = du
            dh2 = dh2 + dot_nt(du, wup_ref[j])
            gub_ref[j] += col_sum(du.astype(F32))
            gmg_ref[j] += col_sum(dm * ehat)
            gmb_ref[j] += col_sum(dm)
            return f, dh2

        sums = (jnp.zeros((block, width), F32),) * 2
        for j in range(nb):
            sums = second(j, sums)
        f, dh2 = sums
        res_ref[...] = jnp.where(valid, x2_ref[...] + f + db_ref[...], 0.0)
        dh2_ref[...] = dh2

    @pl.when(step == 0)
    def _():
        rows(True)

    @pl.when(step > 0)
    def _():
        rows(False)


def feed_forward(length, h2, ct, x2, wup, wdn, ub, mg, mb, db, block):
    seq, width = h2.shape
    nb, _, hb = wup.shape
    rows = pl.BlockSpec((block, width), lambda i: (i, 0))
    smem = pl.BlockSpec(memory_space=pltpu.SMEM)
    hbm = pl.BlockSpec(memory_space=pl.ANY)
    units = whole((nb, 1, hb))
    blocks = pl.BlockSpec((nb, block, hb), lambda i: (0, i, 0))
    sums = out_whole((nb, 1, hb))
    return pl.pallas_call(
        ffn_kernel,
        grid=(seq // block,),
        in_specs=[
            smem, rows, rows, rows, hbm, hbm,
            units, units, units, whole((1, width)),
        ],
        out_specs=[rows, rows, blocks, blocks, sums, sums, sums, out_whole((1, width))],
        out_shape=[
            sds((seq, width), F32), sds((seq, width), F32), sds((nb, seq, hb), BF16), sds((nb, seq, hb), BF16),
            sds((nb, 1, hb), F32), sds((nb, 1, hb), F32), sds((nb, 1, hb), F32), sds((1, width), F32),
        ],
        scratch_shapes=[pltpu.VMEM((nb, block, hb), F32)] * 3 + [pltpu.VMEM((nb, width, hb), BF16)] * 2
        + [pltpu.SemaphoreType.DMA((2, nb))],
        compiler_params=params(60 * MIB),
        cost_estimate=pl.CostEstimate(
            flops=16 * seq * width * nb * hb, bytes_accessed=60 * MIB, transcendentals=2 * seq * nb * hb
        ),
        name="feed_forward",
    )(length, h2, ct, x2, wup, wdn, ub, mg, mb, db)


def ffn_weights_kernel(length_ref, h2_ref, ct_ref, m_ref, du_ref, gup_ref, gdn_ref, h2t_s, dft_s):
    seq, width = h2_ref.shape

    @pl.when(pl.program_id(0) == 0)
    def _():
        row = lax.broadcasted_iota(jnp.int32, (seq, width), 0)
        dfr = jnp.where(row < length_ref[0], ct_ref[...], 0)
        h2t_s[...] = h2_ref[...].T
        dft_s[...] = dfr.T

    gdn_ref[0] = dot_nn(dft_s[...], m_ref[0]).astype(BF16)
    gup_ref[0] = dot_nn(h2t_s[...], du_ref[0]).astype(BF16)


def ffn_weights_pair_kernel(
    length_ref, h2_ref, ct_ref, m_ref, du_ref, gdn_ref, gup_ref, h2t_s, dft_s, grads_s, half_s, send, recv, *, rows, ffn,
):
    step = pl.program_id(0)
    place = Place(rows, ffn)
    seq, width = h2_ref.shape
    depth = place.depth

    def give(a, z):
        return remote(
            grads_s.at[a, z, 1 - place.c], half_s.at[a, z], send.at[a, z], recv.at[a, z],
            place.device(place.r, place.z, 1 - place.c),
        )

    @pl.when(step == 0)
    def _():
        place.enter(near=False)
        row = lax.broadcasted_iota(jnp.int32, (seq, width), 0)
        dfr = jnp.where(row < length_ref[0], ct_ref[...], 0)
        h2t_s[...] = h2_ref[...].T
        dft_s[...] = dfr.T

    @pl.when(step < depth)
    def _():
        for c in range(2):
            grads_s[0, step, c] = dot_nn(dft_s[...], m_ref[c]).astype(BF16)
            grads_s[1, step, c] = dot_nn(h2t_s[...], du_ref[c]).astype(BF16)
        for a in range(2):
            give(a, step).start()

    @pl.when(step > 0)
    def _():
        z = step - 1
        for a, out in enumerate((gdn_ref, gup_ref)):
            give(a, z).wait()
            out[0] = grads_s[a, z, place.c] + half_s[a, z]


def ffn_weight_pair_sums(length, h2, ct, m, du, rows, ffn):
    seq, width = h2.shape
    nb, _, hb = m.shape
    depth = nb // 2
    smem = pl.BlockSpec(memory_space=pltpu.SMEM)
    block = pl.BlockSpec((2, seq, hb), lambda j: (clip(j, 0, depth), 0, 0))
    out = pl.BlockSpec((1, width, hb), lambda j: (clip(j, 1, depth), 0, 0))
    return pl.pallas_call(
        functools.partial(ffn_weights_pair_kernel, rows=rows, ffn=ffn),
        grid=(depth + 1,),
        in_specs=[smem, whole((seq, width)), whole((seq, width)), block, block],
        out_specs=[out, out],
        out_shape=[sds((depth, width, hb), BF16)] * 2,
        scratch_shapes=[pltpu.VMEM((width, seq), BF16)] * 2 + [
            pltpu.VMEM((2, depth, 2, width, hb), BF16),
            pltpu.VMEM((2, depth, width, hb), BF16),
            pltpu.SemaphoreType.DMA((2, depth)),
            pltpu.SemaphoreType.DMA((2, depth)),
        ],
        compiler_params=params(60 * MIB, **comm_params(True, 1)),
        name="ffn_weight_pair_sums",
    )(length, h2, ct, m, du)


def ffn_weight_grads(length, h2, ct, m, du):
    seq, width = h2.shape
    nb, _, hb = m.shape
    smem = pl.BlockSpec(memory_space=pltpu.SMEM)
    block = pl.BlockSpec((1, seq, hb), lambda j: (j, 0, 0))
    out = pl.BlockSpec((1, width, hb), lambda j: (j, 0, 0))
    return pl.pallas_call(
        ffn_weights_kernel,
        grid=(nb,),
        in_specs=[smem, whole((seq, width)), whole((seq, width)), block, block],
        out_specs=[out, out],
        out_shape=[sds((nb, width, hb), BF16)] * 2,
        scratch_shapes=[pltpu.VMEM((width, seq), BF16)] * 2,
        compiler_params=params(),
        cost_estimate=pl.CostEstimate(
            flops=4 * seq * width * nb * hb, bytes_accessed=36 * MIB, transcendentals=0
        ),
        name="ffn_weight_grads",
    )(length, h2, ct, m, du)


def attend_back_pair(length, q_all, k_of, v_of, g_all, lse_ref, inner_row, dq_s, store, seq, block, head):
    lanes = 2 * head
    lane = lax.broadcasted_iota(jnp.int32, (seq, lanes), 1)
    dq_s[...] = jnp.zeros_like(dq_s)
    zero = jnp.zeros_like(q_all)
    q_heads = [jnp.where(lane < head, q_all, zero), jnp.where(lane >= head, q_all, zero)]
    g_heads = [jnp.where(lane < head, g_all, zero), jnp.where(lane >= head, g_all, zero)]
    for j in range(seq // block):
        start = j * block
        width = seq - start
        k, v = k_of(j), v_of(j)
        key_pos = lax.broadcasted_iota(jnp.int32, (block, width), 0) + start
        row_pos = lax.broadcasted_iota(jnp.int32, (block, width), 1) + start
        allowed = (key_pos <= row_pos) & (key_pos < length)
        dk = dv = None
        dqs = []
        for n in range(2):
            q = q_heads[n][start:, :]
            g = g_heads[n][start:, :]
            scores = dot_nt(k, q)
            probs = jnp.where(allowed, jnp.exp(scores - lse_ref[0, n : n + 1, start:]), 0.0)
            grad_probs = dot_nt(v, g)
            grad_scores = (probs * (grad_probs - inner_row(n)[:, start:])).astype(BF16)
            dv_part = dot_nn(probs.astype(BF16), g)
            dk_part = dot_nn(grad_scores, q)
            dv = dv_part if n == 0 else dv + dv_part
            dk = dk_part if n == 0 else dk + dk_part
            dqs.append(dot_tn(grad_scores, k))
        dq_s[start:, :] += jnp.where(lane[start:, :] < head, dqs[0], dqs[1])
        store(j, dk.astype(BF16), dv.astype(BF16))


def norms_back(dh2, x2, o, c, dy, w, fg, pg, hs, head, sums, g_store, dx2_store, dor_store):
    block, width = dh2.shape
    heads = width // head
    hat2, inverse2 = norm_parts(x2)
    dx2 = dy + norm_back(dh2 * fg, hat2, inverse2)
    dx2_store(dx2)
    hat, inverse = norm_parts(o)
    dor = norm_back(dx2 * pg, hat, inverse).astype(BF16)
    dor_store(dor)
    sums(
        col_sum(dor.astype(F32)), col_sum(dx2 * hat), col_sum(dx2), col_sum(dh2 * hat2), col_sum(dh2),
    )
    dc = dot_nt(dor, w)
    g_store((dc * hs).astype(BF16))
    product = dc * c.astype(F32)
    high = product.astype(BF16)
    low = (product - high.astype(F32)).astype(BF16)
    owner = lax.broadcasted_iota(jnp.int32, (heads, width), 1) // head
    pick = (owner == lax.broadcasted_iota(jnp.int32, (heads, width), 0)).astype(BF16)
    return dot_nt(pick, high) + dot_nt(pick, low)


def valid_grad(ct, length, first):
    row = lax.broadcasted_iota(jnp.int32, ct.shape, 0) + first
    return jnp.where(row < length, ct.astype(F32), 0.0)


def back_kernel(
    length_ref, dh2_ref, ct_ref, x2_ref, o_ref, c_ref, w_ref, fg_ref, pg_ref, hs_ref, q_ref, k_ref, v_ref, lse_ref,
    dx2_ref, dor_ref, dq_ref, dk_ref, dv_ref, ghs_ref, sums_ref, g_s, inner_s, dq_s, *, block, head, factor,
):
    step = pl.program_id(0)
    seq, width = g_s.shape
    nb = seq // block

    @pl.when(step == 0)
    def _():
        ghs_ref[...] = jnp.zeros_like(ghs_ref)
        sums_ref[...] = jnp.zeros_like(sums_ref)

    @pl.when(step < nb)
    def _():
        here = pl.ds(pl.multiple_of(step * block, block), block)

        def sums(*parts):
            for n, part in enumerate(parts):
                sums_ref[n : n + 1, :] += part

        def put(ref, *index):
            def store(value):
                ref[index if index else ...] = value

            return store

        inner = norms_back(
            dh2_ref[...], x2_ref[...], o_ref[...], c_ref[...], valid_grad(ct_ref[...], length_ref[0], step * block),
            w_ref[...], fg_ref[...], pg_ref[...], hs_ref[...], head, sums, put(g_s, here, slice(None)), put(dx2_ref),
            put(dor_ref),
        )
        inner_s[step] = inner
        ghs_ref[...] += jnp.broadcast_to(jnp.sum(inner, axis=-1, keepdims=True), ghs_ref.shape)

    @pl.when(step >= nb)
    def _():
        pair = step - nb
        cols = pl.ds(pl.multiple_of(pair * (2 * head), 2 * head), 2 * head)
        inner_rows = [
            jnp.concatenate([inner_s[i, pl.ds(2 * pair + n, 1), :] for i in range(nb)], axis=1) for n in range(2)
        ]

        def store(j, dk, dv):
            dk_ref[j * block : (j + 1) * block, :] = dk
            dv_ref[j * block : (j + 1) * block, :] = dv

        attend_back_pair(
            length_ref[0], q_ref[...], lambda j: k_ref[j * block : (j + 1) * block, :],
            lambda j: v_ref[j * block : (j + 1) * block, :], g_s[:, cols], lse_ref, lambda n: inner_rows[n], dq_s, store,
            seq, block, head,
        )
        dq_ref[...] = (dq_s[...] * factor).astype(BF16)


def back(length, dh2, ct, x2, o, c, w, fg, pg, hs, q, k, v, lse, block, head, factor):
    seq, width = dh2.shape
    nb, pairs, heads = seq // block, width // (2 * head), width // head
    part = pl.BlockSpec((block, width), lambda i: (clip(i, 0, nb), 0))
    cols = pl.BlockSpec((seq, 2 * head), lambda i: (0, clip(i, nb, pairs)))
    heads_in = pl.BlockSpec((None, seq, 2 * head), lambda i: (clip(i, nb, pairs), 0, 0))
    smem = pl.BlockSpec(memory_space=pltpu.SMEM)
    vec = whole((1, width))
    return pl.pallas_call(
        functools.partial(back_kernel, block=block, head=head, factor=factor),
        grid=(nb + pairs,),
        in_specs=[smem] + [part] * 5 + [whole((width, width))] + [vec] * 3 + [heads_in] * 3
        + [pl.BlockSpec((1, 2, seq), lambda i: (clip(i, nb, pairs), 0, 0))],
        out_specs=[part] * 2 + [cols] * 3 + [out_whole((heads, 128)), out_whole((8, width))],
        out_shape=[sds((seq, width), F32)] + [sds((seq, width), BF16)] * 4
        + [sds((heads, 128), F32), sds((8, width), F32)],
        scratch_shapes=[
            pltpu.VMEM((seq, width), BF16), pltpu.VMEM((nb, heads, block), F32), pltpu.VMEM((seq, 2 * head), F32),
        ],
        compiler_params=params(60 * MIB),
        name="backward_attention",
    )(length, dh2, ct, x2, o, c, w, fg, pg, hs, q, k, v, lse)


def weights_kernel(left_ref, right_ref, out_ref, left_s):
    @pl.when(pl.program_id(0) == 0)
    def _():
        left_s[...] = left_ref[...].T

    out_ref[...] = dot_nn(left_s[...], right_ref[...]).astype(BF16)


def weight_grad(left, right, block):
    seq, width = left.shape
    cols = right.shape[1]
    return pl.pallas_call(
        weights_kernel,
        grid=(cols // block,),
        in_specs=[whole((seq, width)), pl.BlockSpec((seq, block), lambda j: (0, j))],
        out_specs=pl.BlockSpec((width, block), lambda j: (0, j)),
        out_shape=sds((width, cols), BF16),
        scratch_shapes=[pltpu.VMEM((width, seq), BF16)],
        compiler_params=params(),
        name="weight_grad",
    )(left, right)


def input_back(dq, dk, dv, w, x, dx2, gain, sums):
    dh = dot_nt(dq, w(0)) + dot_nt(dk, w(1)) + dot_nt(dv, w(2))
    hat, inverse = norm_parts(x.astype(F32))
    sums(col_sum(dh * hat), col_sum(dh), col_sum(dq.astype(F32)), col_sum(dv.astype(F32)))
    return dx2 + norm_back(dh * gain, hat, inverse)


def input_kernel(dq_ref, dk_ref, dv_ref, w_ref, x_ref, dx2_ref, gain_ref, dx_ref, sums_ref):
    @pl.when(pl.program_id(0) == 0)
    def _():
        sums_ref[...] = jnp.zeros_like(sums_ref)

    def sums(*parts):
        for n, part in enumerate(parts):
            sums_ref[n : n + 1, :] += part

    dx_ref[...] = input_back(
        dq_ref[...], dk_ref[...], dv_ref[...], lambda i: w_ref[i], x_ref[...], dx2_ref[...], gain_ref[...], sums
    )


def input_grad(dq, dk, dv, w, x, dx2, gain, block):
    seq, width = dq.shape
    rows = pl.BlockSpec((block, width), lambda i: (i, 0))
    return pl.pallas_call(
        input_kernel,
        grid=(seq // block,),
        in_specs=[rows, rows, rows, whole((3, width, width)), rows, rows, whole((1, width))],
        out_specs=[rows, out_whole((8, width))],
        out_shape=[sds((seq, width), F32), sds((8, width), F32)],
        compiler_params=params(),
        name="input_grad",
    )(dq, dk, dv, w, x, dx2, gain)


class AllSum:
    def __init__(self, place, stages, far, send, recv):
        self.place, self.stages, self.far, self.send, self.recv = place, stages, far, send, recv

    def copy(self, k):
        p = self.place
        device = (
            p.device(p.r, p.z, 1 - p.c), p.device(p.row_flip(p.r, 0), p.z, p.c), p.device(p.row_flip(p.r, 1), p.z, p.c)
        )[k]
        return remote(self.stages.at[k], self.stages.at[3 + k], self.send.at[k], self.recv.at[k], device)

    def along(self, d):
        p = self.place
        return remote(
            self.far.at[p.z], self.far.at[p.z], self.send.at[2 + d], self.recv.at[2 + d], p.device(p.r, p.z_at(d), p.c)
        )

    def begin(self):
        self.copy(0).start()

    def add(self, k):
        self.copy(k).wait_recv()
        total = self.stages[k] + self.stages[3 + k]
        if k < 2:
            self.stages[k + 1] = total
            self.copy(k + 1).start()
        else:
            self.far[self.place.z] = total
            for d in range(1, self.place.depth):
                self.along(d).start()

    def total(self):
        p = self.place
        for d in range(1, p.depth):
            there = self.far.at[p.z_at(-d)]
            pltpu.make_async_copy(there, there, self.recv.at[2 + d]).wait()
        out = self.far[0]
        for z in range(1, p.depth):
            out = out + self.far[z]
        return out

    def finish(self):
        for k in range(3):
            self.copy(k).wait_send()
        for d in range(1, self.place.depth):
            self.along(d).wait_send()


def tail_kernel(
    length_ref, dh2_ref, ct_ref, x2_ref, o_ref, c_ref, x_ref, fg_ref, pg_ref, hs_ref, gain_ref, small_ref,
    q_ref, k_ref, v_ref, lse_ref, h_ref, w_ref, down_ref, up_ref,
    dx_ref, small_out, down_out, up_out, wo_out, wv_out, wk_out, wq_out,
    w_s, g_s, dq_s, dk_s, dv_s, left_s, dx2_s, inner_s, dqa_s, acc_s, ghs_s, load,
    stage, stage_load, grads, *bufs, rows, ffn, block, head, factor,
):
    step = pl.program_id(0)
    seq, width = g_s.shape
    nb = seq // block
    fine = block // 2
    nf = seq // fine
    pairs = width // (2 * head)
    place = Place(rows, ffn)
    depth = place.depth
    weight_at = nf
    attend_at = weight_at + 1
    input_at = attend_at + pairs
    others_at = input_at + nb
    last = others_at + 2

    take = iter(bufs)
    half_rows = down_out.shape[0] // 2
    ffn_jobs = []
    for n in range(4):
        part = pl.ds(n % 2 * half_rows, half_rows)
        ref = (down_ref, up_ref)[n // 2]
        ffn_jobs.append(
            PairExchange(
                place, lambda r, z, ref=ref, part=part: ref.at[z, r, part], stage.at[n % 2], stage_load.at[n],
                *(next(take) for _ in range(5)),
            )
        )
    proj_jobs = []
    for n in range(4):
        held = grads.at[n % 2]
        proj_jobs.append(
            CoreExchange(place, lambda r, z, c, held=held: held.at[r, z, c], held, *(next(take) for _ in range(6)))
        )
    small, late = (AllSum(place, *(next(take) for _ in range(4))) for _ in range(2))
    outs = (wo_out, wv_out, wk_out, wq_out)

    def matrix(slot, i):
        return pltpu.make_async_copy(w_ref.at[:, :, :, i], w_s.at[slot], load.at[slot])

    h_copy = pltpu.make_async_copy(h_ref, g_s, load.at[3])

    def start():
        place.enter()
        matrix(0, 3).start()
        matrix(1, 1).start()
        matrix(2, 2).start()
        ffn_jobs[0].leave()
        ffn_jobs[1].leave()
        acc_s[...] = jnp.zeros_like(acc_s)
        ghs_s[...] = jnp.zeros_like(ghs_s)
        matrix(0, 3).wait()

    def start_small():
        small.stages[0] = small_ref[...]
        small.stages[0, 0:5, :] = acc_s[4:9, :]
        small.stages[0, 6:7, 0 : ghs_s.shape[0]] = ghs_s[...].T[0:1, :]
        small.begin()

    def start_late():
        late.stages[0] = acc_s[0:8, :]
        late.begin()

    def take_h():
        h_copy.wait()
        left_s[...] = g_s[...].T

    at_steps(step, {
        0: [start],
        weight_at: [start_small],
        attend_at: [matrix(0, 0).start, ffn_jobs[0].one, functools.partial(small.add, 0), ffn_jobs[2].leave],
        attend_at + 2: [ffn_jobs[1].one, functools.partial(small.add, 1)],
        attend_at + 3: [ffn_jobs[0].two, proj_jobs[0].leave, ffn_jobs[3].leave],
        attend_at + 6: [ffn_jobs[2].one, functools.partial(small.add, 2)],
        attend_at + 7: [ffn_jobs[1].two, proj_jobs[0].one],
        input_at: [h_copy.start, matrix(0, 0).wait, matrix(1, 1).wait, matrix(2, 2).wait],
        input_at + 2: [ffn_jobs[3].one, ffn_jobs[2].two, proj_jobs[0].two],
        others_at: [start_late, take_h, ffn_jobs[3].two],
        others_at + 1: [proj_jobs[1].leave, functools.partial(late.add, 0)],
        others_at + 2: [proj_jobs[2].leave, proj_jobs[1].one, functools.partial(late.add, 1)],
    })

    def sums_from(first):
        def sums(*parts):
            for n, part in enumerate(parts):
                acc_s[first + n : first + n + 1, :] += part

        return sums

    @pl.when(step < nf)
    def _():
        here = pl.ds(pl.multiple_of(step * fine, fine), fine)

        def put(ref):
            def store(value):
                ref[here, :] = value

            return store

        c = c_ref[...]
        left_s[:, here] = c.T
        inner = norms_back(
            dh2_ref[...], x2_ref[...], o_ref[...], c, valid_grad(ct_ref[...], length_ref[0], step * fine),
            w_s[0].reshape(width, width), fg_ref[...], pg_ref[...], hs_ref[...], head, sums_from(4), put(g_s), put(dx2_s),
            put(dq_s),
        )
        inner_s[step] = inner
        ghs_s[...] += jnp.broadcast_to(jnp.sum(inner, axis=-1, keepdims=True), ghs_s.shape)

    def project(n, right_s):
        cut = width // 2
        for i in range(2):
            cols = slice(i * cut, (i + 1) * cut)
            value = dot_nn(left_s[...], right_s[:, cols]).astype(BF16)
            grads[n % 2, ..., cols] = value.reshape(grads.shape[1:-1] + (cut,))
        proj_jobs[n].begin()

    @pl.when(step == weight_at)
    def _():
        project(0, dq_s)

    @pl.when((step >= attend_at) & (step < input_at))
    def _():
        pair = step - attend_at
        cols = pl.ds(pl.multiple_of(pair * (2 * head), 2 * head), 2 * head)
        inner_rows = [
            jnp.concatenate([inner_s[i, pl.ds(2 * pair + n, 1), :] for i in range(nf)], axis=1) for n in range(2)
        ]

        def store(j, dk, dv):
            dk_s[j * block : (j + 1) * block, cols] = dk
            dv_s[j * block : (j + 1) * block, cols] = dv

        attend_back_pair(
            length_ref[0], q_ref[...], lambda j: k_ref[j * block : (j + 1) * block, :],
            lambda j: v_ref[j * block : (j + 1) * block, :], g_s[:, cols], lse_ref, lambda n: inner_rows[n], dqa_s, store,
            seq, block, head,
        )
        dq_s[:, cols] = (dqa_s[...] * factor).astype(BF16)

    @pl.when((step >= input_at) & (step < others_at))
    def _():
        here = pl.ds(pl.multiple_of((step - input_at) * block, block), block)
        dx_ref[...] = input_back(
            dq_s[here, :], dk_s[here, :], dv_s[here, :], lambda i: w_s[i].reshape(width, width), x_ref[...], dx2_s[here, :],
            gain_ref[...], sums_from(0),
        )

    for n, right_s in ((1, dv_s), (2, dk_s), (3, dq_s)):

        @pl.when(step == others_at + n - 1)
        def _(n=n, right_s=right_s):
            project(n, right_s)

    @pl.when(step == last)
    def _():
        _, wv, wk, wq = proj_jobs
        for action in (
            wq.leave, functools.partial(late.add, 2), wk.one, wv.two, wq.one, wk.two, wq.two,
        ):
            action()
        for n, job in enumerate(ffn_jobs):
            (down_out, up_out)[n // 2][n % 2 * half_rows : (n % 2 + 1) * half_rows, :] = job.total()
        small_out[0:8, :] = late.total()
        small_out[8:, :] = small.total()
        for job in (small, late):
            job.finish()
        for job, out in zip(proj_jobs, outs):
            out[...] = job.total()


def tail(
    length, dh2, ct, x2, o, c, x, fg, pg, hs, gain, small, q, k, v, lse, h, w, down, up, rows, ffn, block, head, factor
):
    seq, width = dh2.shape
    nb, pairs, heads = seq // block, width // (2 * head), width // head
    depth = ffn // 2
    fine = block // 2
    nf = seq // fine
    input_at = nf + 1 + pairs
    first = pl.BlockSpec((fine, width), lambda i: (clip(i, 0, nf), 0))
    final = pl.BlockSpec((block, width), lambda i: (clip(i, input_at, nb), 0))
    cols = pl.BlockSpec((None, seq, 2 * head), lambda i: (clip(i, nf + 1, pairs), 0, 0))
    smem = pl.BlockSpec(memory_space=pltpu.SMEM)
    hbm = pl.BlockSpec(memory_space=pl.ANY)
    vmem = pl.BlockSpec(memory_space=pltpu.VMEM)
    vec = whole((1, width))
    unit = down.shape[2:]
    piece = (unit[0] // 2, unit[1])
    proj = (width // (rows * ffn), width)
    dma = pltpu.SemaphoreType.DMA

    def arrivals(shape):
        return [pltpu.VMEM((depth, 2) + shape, BF16), pltpu.VMEM((depth,) + shape, BF16), pltpu.VMEM((depth,) + shape, BF16)]

    scratch = [
        pltpu.VMEM((3, rows, depth, 2) + proj, BF16),
        pltpu.VMEM((seq, width), BF16), pltpu.VMEM((seq, width), BF16), pltpu.VMEM((seq, width), BF16),
        pltpu.VMEM((seq, width), BF16), pltpu.VMEM((width, seq), BF16), pltpu.VMEM((seq, width), F32),
        pltpu.VMEM((nf, heads, fine), F32), pltpu.VMEM((seq, 2 * head), F32), pltpu.VMEM((16, width), F32),
        pltpu.VMEM((heads, 128), F32), dma((4,)),
        pltpu.VMEM((2, depth, 2) + piece, BF16), dma((4, depth, 2)), pltpu.VMEM((2, rows, depth, 2) + proj, BF16),
    ]
    for _ in range(4):
        scratch += arrivals(piece) + [dma((4,)), dma((4, depth))]
    for _ in range(4):
        scratch += [pltpu.VMEM((depth, rows) + proj, BF16)] + arrivals(proj) + [dma((4,)), dma((8, depth))]
    late = (8, width)
    for shape in (small.shape, late):
        scratch += [pltpu.VMEM((6,) + shape, F32), pltpu.VMEM((depth,) + shape, F32), dma((2 + depth,)), dma((2 + depth,))]
    return pl.pallas_call(
        functools.partial(tail_kernel, rows=rows, ffn=ffn, block=block, head=head, factor=factor),
        grid=(input_at + nb + 3,),
        in_specs=[smem] + [first] * 5 + [final] + [vec] * 4 + [whole(small.shape)] + [cols] * 3
        + [pl.BlockSpec((1, 2, seq), lambda i: (clip(i, nf + 1, pairs), 0, 0))] + [hbm] * 4,
        out_specs=[final] + [vmem] * 7,
        out_shape=[sds((seq, width), F32), sds((8 + small.shape[0], width), F32), sds(unit, F32), sds(unit, F32)] + [sds(proj, F32)] * 4,
        scratch_shapes=scratch,
        compiler_params=params(62 * MIB, **comm_params(True, 2)),
        name="backward_and_sums",
    )(length, dh2, ct, x2, o, c, x, fg, pg, hs, gain, small, q, k, v, lse, h, w, down, up)


def widen(blocks, lanes):
    nb, rows, hb = blocks.shape
    group = max(1, lanes // hb)
    if group == 1:
        return blocks
    return blocks.reshape(nb // group, group, rows, hb).transpose(0, 2, 1, 3).reshape(nb // group, rows, group * hb)


def narrow(blocks, hb):
    nb, rows, lanes = blocks.shape
    group = lanes // hb
    if group == 1:
        return blocks
    return blocks.reshape(nb, rows, group, hb).transpose(0, 2, 1, 3).reshape(nb * group, rows, hb)


def rows_of(vector):
    return vector.reshape(1, -1)


def shards(
    tokens, lengths, cotangent, ln_attn_gain, ln_attn_bias, w_query, query_bias, w_key, w_value, value_bias,
    head_scale, w_out, out_bias, post_gain, post_bias, ffn_gain, ffn_bias, w_up, up_bias, mid_gain, mid_bias,
    w_down, down_bias,
):
    seq, width = tokens.shape
    heads = head_scale.shape[0]
    head = width // heads
    factor = head ** (-0.5)
    block = min(seq, 256)
    rows, ffn = lax.axis_size("rows"), lax.axis_size("ffn")
    own_units = w_up.shape[1]
    hidden = own_units * ffn
    fused = ffn == 8 and w_query.shape[0] % 16 == 0 and own_units % 512 == 0
    weights = (w_query, w_key, w_value, w_out, w_down, w_up)
    vectors = [
        rows_of(v)
        for v in (
            ln_attn_gain, ln_attn_bias, query_bias, value_bias, out_bias, post_gain, post_bias, ffn_gain, ffn_bias,
        )
    ]
    if not fused:
        attn, down_all, up_all = gather_all(rows, ffn, weights)
        attn = attn.transpose(3, 0, 1, 2, 4, 5).reshape(4, width, width)
        weights = (attn,)
    h, q, k, v, c, lse, o, x2, h2, *gathered = front(
        lengths, head_scale, tokens, vectors, weights, rows, ffn, block, head, factor, fused
    )
    if fused:
        attn, down_all, up_all = gathered
    wup = widen(up_all.reshape(ffn, width, own_units), 512)
    wdn = widen(down_all.reshape(ffn, width, own_units), 512)
    nb, _, hb = wup.shape
    units = lambda vector: vector.reshape(nb, 1, hb)
    result, dh2, m, du, g_ub, g_mg, g_mb, g_db = feed_forward(
        lengths, h2, cotangent, x2, wup, wdn, units(up_bias), units(mid_gain), units(mid_bias), rows_of(down_bias),
        block,
    )
    scale_cols = rows_of(jnp.repeat(head_scale, head))
    wide = [part.reshape(-1, width) for part in (g_ub, g_mg, g_mb)]
    above = jnp.concatenate([g_db, jnp.zeros((1, width), F32)] + wide, axis=0)
    above = jnp.pad(above, ((5, -(5 + above.shape[0]) % 8), (0, 0)))
    if fused:
        g_dn, g_up = (
            part.reshape((ffn // 2, rows) + w_up.shape)
            for part in ffn_weight_pair_sums(lengths, h2, cotangent, m, du, rows, ffn)
        )
        dx, small, grad_down, grad_up, g_wo, g_wv, g_wk, g_wq = tail(
            lengths, dh2, cotangent, x2, o, c, tokens, rows_of(ffn_gain), rows_of(post_gain), scale_cols,
            rows_of(ln_attn_gain), above, q, k, v, lse, h, attn, g_dn, g_up, rows, ffn, block, head, factor,
        )
    else:
        g_up, g_dn = ffn_weight_grads(lengths, h2, cotangent, m, du)
        dx2, dor, dq, dk, dv, g_hs, late = back(
            lengths, dh2, cotangent, x2, o, c, attn[3], rows_of(ffn_gain), rows_of(post_gain), scale_cols, q, k, v, lse,
            block, head, factor,
        )
        dx, early = input_grad(dq, dk, dv, attn[:3], tokens, dx2, rows_of(ln_attn_gain), block)
        g_hs = jnp.pad(g_hs[:, :1].T, ((0, 0), (0, width - heads)))
        small = jnp.concatenate([early, late[:5], above[5:6], g_hs, above[7:]], axis=0)
        small = lax.psum(small, BOTH)
        grad_down, grad_up = (
            scatter_sum(rows, ffn, narrow(part, own_units).reshape((ffn // 2, 2, rows) + w_up.shape), by_unit)
            for part in (g_dn, g_up)
        )
        g_wo, g_wv, g_wk, g_wq = (
            scatter_sum(
                rows, ffn, weight_grad(left, right, 512).reshape((rows, ffn // 2, 2) + w_query.shape), by_device
            )
            for left, right in ((c, dor), (h, dv), (h, dk), (h, dq))
        )
    n = hidden // width
    vectors = jnp.concatenate([small[:4], small[8:14]], axis=0)
    owned = small[15 : 15 + 3 * n].reshape(3, ffn, own_units)
    if fused:
        (
            dx, grad_up, grad_down, g_wq, g_wk, g_wv, g_wo, g_lg, g_lb, g_qb, g_vb, g_ob, g_pg, g_pb, g_fg, g_fb, g_db,
        ) = hand_on(dx, grad_up, grad_down, g_wq, g_wk, g_wv, g_wo, vectors)
    else:
        g_lg, g_lb, g_qb, g_vb, g_ob, g_pg, g_pb, g_fg, g_fb, g_db = vectors
    g_hs = small[14, :heads] / head_scale
    mine = lax.dynamic_index_in_dim(owned, lax.axis_index("ffn"), axis=1, keepdims=False)
    return (
        result, dx, g_lg, g_lb, g_wq, g_qb, g_wk, g_wv, g_vb, g_hs, g_wo, g_ob, g_pg, g_pb, g_fg, g_fb, grad_up, mine[0],
        mine[1], mine[2], grad_down, g_db,
    )


def hand_on_kernel(*refs):
    ins, vectors, outs, lines = refs[:7], refs[7], refs[8:15], refs[15:]
    outs[0][...] = ins[0][...]

    @pl.when(pl.program_id(0) == 0)
    def _():
        for src, out in zip(ins[1:], outs[1:]):
            out[...] = src[...]
        for n, line in enumerate(lines):
            line[...] = vectors[n, :]


def hand_on(dx, *rest):
    *grads, vectors = rest
    seq, width = dx.shape
    n = vectors.shape[0]
    block = seq // 4
    rows = pl.BlockSpec((block, width), lambda i: (i, 0))
    return pl.pallas_call(
        hand_on_kernel,
        grid=(4,),
        in_specs=[rows] + [whole(a.shape) for a in grads] + [whole(vectors.shape)],
        out_specs=[rows] + [out_whole(a.shape) for a in grads] + [out_whole((width,))] * n,
        out_shape=[sds(a.shape, F32) for a in (dx, *grads)] + [sds((width,), F32)] * n,
        compiler_params=params(),
        name="hand_on",
    )(dx, *grads, vectors)


def solution(mesh):
    split = P(BOTH, None)
    tiles = P("rows", "ffn")
    one = P()
    return jax.shard_map(
        shards,
        mesh=mesh,
        in_specs=(
            split, P(BOTH), split, one, one, split, one, split, split, one, one, split, one, one, one, one, one,
            tiles, one, one, one, tiles, one,
        ),
        out_specs=(
            split, split, one, one, split, one, split, split, one, one, split, one, one, one, one, one,
            tiles, P("ffn"), P("ffn"), P("ffn"), tiles, one,
        ),
        check_vma=False,
    )
```

```python
import functools
import math

import jax
import jax.numpy as jnp
from jax import lax
from jax.experimental import pallas as pl
from jax.experimental.pallas import tpu as pltpu
from jax.sharding import PartitionSpec as P

epsilon = 1e-05
masked_score = -1e30
F32 = jnp.float32
BF16 = jnp.bfloat16
MIB = 1 << 20
BOTH = ("rows", "ffn")


def dot_nn(left, right):
    return lax.dot_general(left, right, (((1,), (0,)), ((), ())), preferred_element_type=F32)


def dot_nt(left, right):
    return lax.dot_general(left, right, (((1,), (1,)), ((), ())), preferred_element_type=F32)


def dot_tn(left, right):
    return lax.dot_general(left, right, (((0,), (0,)), ((), ())), preferred_element_type=F32)


def params(limit=56 * MIB, **kw):
    return pltpu.CompilerParams(vmem_limit_bytes=limit, **kw)


def comm_params(fused, number):
    return dict(has_side_effects=True, collective_id=number) if fused else {}


def whole(shape):
    return pl.BlockSpec(shape, lambda *_: (0,) * len(shape), pipeline_mode=pl.Buffered(1))


def out_whole(shape):
    return pl.BlockSpec(shape, lambda *_: (0,) * len(shape))


def sds(shape, dtype):
    return jax.ShapeDtypeStruct(shape, dtype)


def norm_parts(values):
    center = jnp.mean(values, axis=-1, keepdims=True)
    centered = values - center
    spread = jnp.mean(centered * centered, axis=-1, keepdims=True)
    inverse = lax.rsqrt(spread + epsilon)
    return centered * inverse, inverse


def norm_back(grad_hat, hat, inverse):
    return (
        grad_hat
        - jnp.mean(grad_hat, axis=-1, keepdims=True)
        - hat * jnp.mean(grad_hat * hat, axis=-1, keepdims=True)
    ) * inverse


def col_sum(values):
    return jnp.sum(values, axis=0, keepdims=True)


class Place:
    def __init__(self, rows, ffn):
        self.rows, self.ffn, self.depth = rows, ffn, ffn // 2
        self.r = lax.axis_index("rows")
        f = lax.axis_index("ffn")
        self.z, self.c = f // 2, lax.rem(f, 2)

    def row_flip(self, r, bit):
        return r + 1 - 2 * lax.rem(r, 2) if bit == 0 else lax.rem(r + 2, 4)

    def z_at(self, d):
        return lax.rem(self.z + d + self.depth, self.depth)

    def near(self, k):
        if self.depth != 4:
            return self.z_at(k)
        inward = 1 - 2 * (self.z // 2)
        inner = lax.rem(self.z, 3) // 1
        inner = inner - (inner // 2)
        if k == 0:
            return self.z
        if k == 1:
            return self.z + inward * (1 - 2 * inner)
        return self.z + inward * (k - inner)

    def device(self, r, z, c):
        return (r, 2 * z + c)

    def enter(self, near=True):
        barrier = pltpu.get_barrier_semaphore()
        partners = [self.device(self.r, self.z, 1 - self.c)]
        if near:
            partners += [self.device(self.row_flip(self.r, bit), self.z, self.c) for bit in range(2)]
            partners += [self.device(self.r, self.z_at(d), self.c) for d in range(1, self.depth)]
        for partner in partners:
            pl.semaphore_signal(barrier, inc=1, device_id=partner, device_id_type=pl.DeviceIdType.MESH)
        pl.semaphore_wait(barrier, len(partners))


def remote(src, dst, send, recv, device):
    return pltpu.make_async_remote_copy(
        src_ref=src, dst_ref=dst, send_sem=send, recv_sem=recv, device_id=device, device_id_type=pl.DeviceIdType.MESH
    )


class Gather:
    def __init__(self, place, src, view, many, sems):
        self.place, self.src, self.view, self.many = place, src, view, many
        self.local, self.send, self.recv, self.core = sems

    def copy(self, src, kind, r, z, c, device, arrival):
        return remote(src, self.view(r, z, c), self.send.at[kind], arrival, device)

    def to_near(self, src, kind, r, z, device):
        self.copy(src, kind, r, z, self.place.c, device, self.recv.at[r, z]).start()

    def wait_piece(self, r, z):
        there = self.view(r, z, self.place.c)
        pltpu.make_async_copy(there, there, self.recv.at[r, z]).wait()

    def bits(self, d):
        return (0, 1) if d % 2 == 0 else (1, 0)

    def begin_z(self, d=0):
        p = self.place
        for k in range(1, p.depth):
            self.to_near(self.src, 0, p.r, p.z, p.device(p.r, p.near(k), p.c))

    def begin_rows(self, d=0):
        p = self.place
        pltpu.make_async_copy(self.src, self.view(p.r, p.z, p.c), self.local).start()
        self.spread(0, self.src)

    def spread(self, d, src=None):
        p = self.place
        z = p.near(d)
        src = self.view(p.r, z, p.c) if src is None else src
        for bit in self.bits(d):
            self.to_near(src, 1, p.r, z, p.device(p.row_flip(p.r, bit), p.z, p.c))
        self.hand_over(p.r, z, src)

    def hand_over(self, r, z, src=None):
        p = self.place
        src = self.view(r, z, p.c) if src is None else src
        self.copy(src, 2, r, z, p.c, p.device(p.r, p.z, 1 - p.c), self.core).start()

    def take_z(self, d):
        p = self.place
        self.wait_piece(p.r, p.near(d))
        self.spread(d)

    def take_first(self, d):
        p = self.place
        z = p.near(d)
        first, second = self.bits(d)
        r = p.row_flip(p.r, first)
        self.wait_piece(r, z)
        self.to_near(self.view(r, z, p.c), 1, r, z, p.device(p.row_flip(p.r, second), p.z, p.c))
        self.hand_over(r, z)

    def take_rest(self, d):
        p = self.place
        z = p.near(d)
        for r in (p.row_flip(p.r, self.bits(d)[1]), p.row_flip(p.row_flip(p.r, 0), 1)):
            self.wait_piece(r, z)
            self.hand_over(r, z)

    def finish(self):
        p = self.place
        pltpu.make_async_copy(self.src, self.view(p.r, p.z, p.c), self.local).wait()
        half = self.many(slice(None), slice(None), p.c)
        pltpu.make_async_copy(half, half, self.core).wait()
        pltpu.make_async_copy(half, half, self.send.at[2]).wait()
        part = self.many(slice(0, 3), slice(None), p.c)
        pltpu.make_async_copy(part, part, self.send.at[1]).wait()
        part = self.many(0, slice(0, p.depth - 1), p.c)
        pltpu.make_async_copy(part, part, self.send.at[0]).wait()


def gather_sems(jobs, rows, depth):
    dma = pltpu.SemaphoreType.DMA
    return [dma((jobs,)), dma((jobs, 3)), dma((jobs, rows, depth)), dma((jobs,))]


def gather_jobs(place, shards, four_all, down_all, up_all, sems):
    local, send, recv, core = sems
    jobs = []

    def add(src, many):
        n = len(jobs)
        jobs.append(Gather(place, src, many, many, (local.at[n], send.at[n], recv.at[n], core.at[n])))

    for i in range(4):
        add(shards[i], lambda r, z, c, i=i: four_all.at[r, z, c, i])
    half = shards[4].shape[0] // 2
    for src, out in ((shards[4], down_all), (shards[5], up_all)):
        for i in range(2):
            part = pl.ds(i * half, half)
            add(src.at[part], lambda r, z, c, out=out, part=part: out.at[z, c, r, part])
    return jobs


def gather_kernel(*refs, rows, ffn):
    place = Place(rows, ffn)
    jobs = gather_jobs(place, refs[:6], *refs[6:9], refs[9:])
    place.enter()
    for job in jobs:
        job.begin_z()
        job.begin_rows()
    for job in jobs:
        for d in range(1, place.depth):
            job.take_z(d)
    for job in jobs:
        for d in range(place.depth):
            job.take_first(d)
    for job in jobs:
        for d in range(place.depth):
            job.take_rest(d)
        job.finish()


def gathered_shapes(rows, ffn, shards):
    depth = ffn // 2
    return [sds((rows, depth, 2, 4) + shards[0].shape, BF16)] + [sds((depth, 2, rows) + a.shape, BF16) for a in shards[4:]]


def gather_all(rows, ffn, shards):
    hbm = pl.BlockSpec(memory_space=pl.ANY)
    return pl.pallas_call(
        functools.partial(gather_kernel, rows=rows, ffn=ffn),
        in_specs=[hbm] * 6,
        out_specs=[hbm] * 3,
        out_shape=gathered_shapes(rows, ffn, shards),
        scratch_shapes=gather_sems(8, rows, ffn // 2),
        compiler_params=pltpu.CompilerParams(has_side_effects=True, collective_id=3),
        name="gather_all",
    )(*shards)


ROWS_FIRST = 8
STRIDE = 6


def gather_rounds(jobs, depth, rows_first):
    rounds = [[(n, "begin_rows", 0) for n in range(rows_first)]]
    for t in range(jobs + 2):
        todo = []
        if t < jobs:
            todo += [(t, "begin_rows", 0)] if t >= rows_first else []
            todo += [(t, "take_z", d) for d in range(1, depth)]
        rounds.append(todo)
        rounds.append([(t - 1, "take_first", d) for d in range(depth)] if 0 <= t - 1 < jobs else [])
        rounds.append([(t - 2, "take_rest", d) for d in range(depth)] if 0 <= t - 2 < jobs else [])
    return rounds


def by_device(ref):
    return lambda r, z, c: ref.at[r, z, c]


def by_unit(ref, part=slice(None)):
    return lambda r, z, c: ref.at[z, c, r, part]


class Scatter:
    def __init__(self, place, view, own, half, pair, last, far, sems):
        self.place, self.view, self.own, self.half, self.pair, self.last, self.far = place, view, own, half, pair, last, far
        self.load, self.send, self.recv = sems

    def bits(self, d):
        return (0, 1) if d % 2 == 0 else (1, 0)

    def sum_at(self, d, r):
        if self.own is None:
            return self.view(r, self.place.z_at(d), self.place.c)
        return self.own.at[d, r]

    def copy(self, src, dst, kind, arrival, d, device):
        return remote(src, dst, self.send.at[kind], self.recv.at[arrival, d], device)

    def fetch(self, d, r):
        p = self.place
        return pltpu.make_async_copy(self.view(r, p.z_at(d), p.c), self.own.at[d, r], self.load.at[r, d])

    def begin(self, d):
        p = self.place
        first, _ = self.bits(d)
        leaving = p.row_flip(p.r, first)
        for base in (leaving, p.r):
            for r in (base, p.row_flip(base, 1 - first)):
                self.copy(
                    self.view(r, p.z_at(d), 1 - p.c), self.half.at[d, r], 0, r, d, p.device(p.r, p.z, 1 - p.c)
                ).start()
                if self.own is not None:
                    self.fetch(d, r).start()

    def arrived(self, ref, arrival, d):
        pltpu.make_async_copy(ref, ref, self.recv.at[arrival, d]).wait()

    def add(self, d, r, ref):
        here = self.sum_at(d, r)
        here[...] = here[...] + ref[...]

    def add_half(self, d, r):
        if self.own is not None:
            self.fetch(d, r).wait()
        self.arrived(self.half.at[d, r], r, d)
        self.add(d, r, self.half.at[d, r])

    def leave(self, d):
        p = self.place
        first, second = self.bits(d)
        partner = p.row_flip(p.r, first)
        for k, r in enumerate((partner, p.row_flip(partner, second))):
            self.add_half(d, r)
            self.copy(self.sum_at(d, r), self.pair.at[d, k], 1, 4 + k, d, p.device(partner, p.z, p.c)).start()

    def stay(self, d):
        p = self.place
        for r in (p.row_flip(p.r, self.bits(d)[1]), p.r):
            self.add_half(d, r)

    def add_one(self, d):
        p = self.place
        partner = p.row_flip(p.r, self.bits(d)[1])
        for k, r in ((1, partner), (0, p.r)):
            self.arrived(self.pair.at[d, k], 4 + k, d)
            self.add(d, r, self.pair.at[d, k])
            if k == 1:
                self.copy(self.sum_at(d, r), self.last.at[d], 2, 6, d, p.device(partner, p.z, p.c)).start()

    def add_two(self, d):
        p = self.place
        self.arrived(self.last.at[d], 6, d)
        self.add(d, p.r, self.last.at[d])
        if d > 0:
            self.copy(self.sum_at(d, p.r), self.far.at[d], 3, 7, d, p.device(p.r, p.z_at(d), p.c)).start()

    def total(self):
        p = self.place
        out = self.sum_at(0, p.r)[...].astype(F32)
        for d in range(1, p.depth):
            self.arrived(self.far.at[d], 7, d)
            out = out + self.far[d].astype(F32)
        return out

    def finish(self):
        for kind, ref in enumerate((self.half, self.pair, self.last, self.far.at[pl.ds(1, self.place.depth - 1)])):
            pltpu.make_async_copy(ref, ref, self.send.at[kind]).wait()


class Exchange:
    def __init__(self, place):
        self.place = place
        self.order = list(range(1, place.depth)) + [0]

    def bits(self, d):
        return (0, 1) if d % 2 == 0 else (1, 0)

    def arrived(self, ref, arrival):
        pltpu.make_async_copy(ref, ref, arrival).wait()

    def rows_of_pair(self, d, leaving):
        p = self.place
        first, second = self.bits(d)
        base = p.row_flip(p.r, first) if leaving else p.r
        return base, p.row_flip(base, second)

    def first_exchange(self, d, k, src):
        p = self.place
        partner = p.row_flip(p.r, self.bits(d)[0])
        remote(
            src, self.pair.at[d, k], self.send.at[1], self.recv.at[k, d], p.device(partner, p.z, p.c)
        ).start()

    def one(self):
        p = self.place
        for d in self.order:
            partner = p.row_flip(p.r, self.bits(d)[1])
            for k in (1, 0):
                self.arrived(self.pair.at[d, k], self.recv.at[k, d])
                here = self.kept(d, k)
                here[...] = here[...] + self.other(d, k)[...]
                if k == 1:
                    remote(
                        here, self.last.at[d], self.send.at[2], self.recv.at[2, d], p.device(partner, p.z, p.c)
                    ).start()

    def two(self):
        p = self.place
        for d in self.order:
            self.arrived(self.last.at[d], self.recv.at[2, d])
            here = self.kept(d, 0)
            here[...] = here[...] + self.last[d]
            if d > 0:
                remote(
                    here, self.far.at[d], self.send.at[3], self.recv.at[3, d], p.device(p.r, p.z_at(d), p.c)
                ).start()

    def total(self):
        out = self.kept(0, 0)[...].astype(F32)
        for d in range(1, self.place.depth):
            self.arrived(self.far.at[d], self.recv.at[3, d])
            out = out + self.far[d].astype(F32)
        for kind, ref in ((1, self.pair), (2, self.last), (3, self.far.at[pl.ds(1, self.place.depth - 1)])):
            self.arrived(ref, self.send.at[kind])
        return out


class PairExchange(Exchange):
    def __init__(self, place, view, stage, load, pair, last, far, send, recv):
        super().__init__(place)
        self.view, self.stage, self.load = view, stage, load
        self.pair, self.last, self.far, self.send, self.recv = pair, last, far, send, recv

    def kept(self, d, k):
        return self.pair.at[d, k]

    def other(self, d, k):
        self.fetch(d, k).wait()
        return self.stage.at[d, k]

    def fetch(self, d, k):
        r = self.rows_of_pair(d, False)[k]
        return pltpu.make_async_copy(self.view(r, self.place.z_at(d)), self.stage.at[d, k], self.load.at[d, k])

    def leave(self):
        for d in self.order:
            z = self.place.z_at(d)
            for k, r in enumerate(self.rows_of_pair(d, True)):
                self.first_exchange(d, k, self.view(r, z))
            for k in range(2):
                self.fetch(d, k).start()


class CoreExchange(Exchange):
    def __init__(self, place, view, whole, half, pair, last, far, send, recv):
        super().__init__(place)
        self.view, self.whole, self.half = view, whole, half
        self.pair, self.last, self.far, self.send, self.recv = pair, last, far, send, recv

    def kept(self, d, k):
        return self.half.at[d, self.rows_of_pair(d, False)[k]]

    def other(self, d, k):
        return self.pair.at[d, k]

    def begin(self):
        p = self.place
        for d in self.order:
            for leaving in (True, False):
                for r in self.rows_of_pair(d, leaving):
                    remote(
                        self.view(r, p.z_at(d), 1 - p.c), self.half.at[d, r], self.send.at[0], self.recv.at[4 + r, d],
                        p.device(p.r, p.z, 1 - p.c),
                    ).start()

    def add_core(self, d, r):
        p = self.place
        here = self.half.at[d, r]
        self.arrived(here, self.recv.at[4 + r, d])
        here[...] = here[...] + self.view(r, p.z_at(d), p.c)[...]

    def leave(self):
        for d in self.order:
            for k, r in enumerate(self.rows_of_pair(d, True)):
                self.add_core(d, r)
                self.first_exchange(d, k, self.half.at[d, r])
        for d in self.order:
            for r in self.rows_of_pair(d, False):
                self.add_core(d, r)
        self.arrived(self.half, self.send.at[0])


def scatter_kernel(src, out, own, half, pair, last, far, load, send, recv, *, rows, ffn, view):
    place = Place(rows, ffn)
    job = Scatter(place, view(src), own, half, pair, last, far, (load, send, recv))
    order = list(range(1, place.depth)) + [0]
    place.enter()
    for name in ("begin", "leave", "stay", "add_one", "add_two"):
        for d in order:
            getattr(job, name)(d)
    out[...] = job.total()
    job.finish()


def scatter_scratch(piece, rows, depth, own):
    return ([pltpu.VMEM((depth, rows) + piece, BF16)] if own else []) + [
        pltpu.VMEM((depth, rows) + piece, BF16),
        pltpu.VMEM((depth, 2) + piece, BF16),
        pltpu.VMEM((depth,) + piece, BF16),
        pltpu.VMEM((depth,) + piece, BF16),
        pltpu.SemaphoreType.DMA((4, depth)),
        pltpu.SemaphoreType.DMA((4,)),
        pltpu.SemaphoreType.DMA((8, depth)),
    ]


def scatter_sum(rows, ffn, grad, view):
    piece = grad.shape[3:]
    return pl.pallas_call(
        functools.partial(scatter_kernel, rows=rows, ffn=ffn, view=view),
        in_specs=[pl.BlockSpec(memory_space=pl.ANY)],
        out_specs=pl.BlockSpec(memory_space=pltpu.VMEM),
        out_shape=sds(piece, F32),
        scratch_shapes=scatter_scratch(piece, rows, ffn // 2, True),
        compiler_params=params(has_side_effects=True, collective_id=4),
        name="scatter_sum",
    )(grad)


def clip(step, low, count):
    return jnp.minimum(jnp.maximum(step - low, 0), count - 1)


def at_steps(step, plan):
    for when, actions in sorted(plan.items()):

        @pl.when(step == when)
        def _(actions=actions):
            for action in actions:
                action()


def attend_pair(length, scales, q_of, k, v, seq, block, head, store):
    lanes = 2 * head
    lane = lax.broadcasted_iota(jnp.int32, (block, lanes), 1)
    for i in range(seq // block):
        keys_here = (i + 1) * block
        q = q_of(i)
        key_pos = lax.broadcasted_iota(jnp.int32, (block, keys_here), 1)
        row_pos = lax.broadcasted_iota(jnp.int32, (block, keys_here), 0) + i * block
        allowed = key_pos < jnp.minimum(row_pos + 1, length)
        ctx = None
        logs = []
        for n in range(2):
            mine = (lane < head) if n == 0 else (lane >= head)
            scores = dot_nt(jnp.where(mine, q, 0), k[:keys_here, :])
            scores = jnp.where(allowed, scores, masked_score)
            peak = jnp.max(scores, axis=-1, keepdims=True)
            weights = jnp.exp(scores - peak)
            total = jnp.sum(weights, axis=-1, keepdims=True)
            part = dot_nn(weights.astype(BF16), v[:keys_here, :]) * (scales[n] / total)
            ctx = part if n == 0 else jnp.where(lane < head, ctx, part)
            logs.append(peak + jnp.log(total))
        store(i, ctx.astype(BF16), jnp.where(lane < head, logs[0], logs[1]).T)


def front_kernel(*refs, rows, ffn, block, head, factor, fused):
    (length_ref, scale_ref, x_ref, lg_ref, lb_ref, qb_ref, vb_ref, ob_ref, pg_ref, pb_ref, fg_ref) = refs[:11]
    fb_ref = refs[11]
    comm_in = refs[12 : 18 if fused else 13]
    refs = refs[18 if fused else 13 :]
    h_ref, q_ref, k_ref, v_ref, c_ref, lse_ref, o_ref, x2_ref, h2_ref = refs[:9]
    comm_out = refs[9:12] if fused else ()
    refs = refs[12 if fused else 9 :]
    w_s, q_s, k_s, v_s, c_s, load = refs[:6]
    step = pl.program_id(0)
    seq, width = q_s.shape
    nb = seq // block
    pairs = width // (2 * head)
    last = 2 * nb + pairs - 1

    def load_weights(source):
        copies = [pltpu.make_async_copy(source(i), w_s.at[i], load.at[i]) for i in range(4)]
        for copy in copies:
            copy.start()
        for copy in copies:
            copy.wait()

    late = {}
    if fused:
        place = Place(rows, ffn)
        jobs = gather_jobs(place, comm_in, *comm_out, refs[6:10])
        rounds = gather_rounds(len(jobs), place.depth, ROWS_FIRST)
        cut = 1 + 3 * 6
        opening = sum(rounds[:cut], [])
        table = {}
        for k, keys in enumerate(rounds[cut:]):
            table.setdefault(min(1 + k * STRIDE // 4, last), []).extend(keys)

        def actions(keys):
            return [functools.partial(getattr(jobs[n], name), d) for n, name, d in keys]

        @pl.when(step == 0)
        def _():
            place.enter()
            for job in jobs:
                job.begin_z()
            for action in actions(opening):
                action()
            copies = [pltpu.make_async_copy(comm_out[0].at[:, :, :, i], w_s.at[i], load.at[i]) for i in range(4)]
            for job, copy in zip(jobs, copies):
                job.finish()
                copy.start()
            for copy in copies:
                copy.wait()

        late = {i: actions(keys) for i, keys in table.items() if keys and i < last}
        at_steps(step, late)
    else:

        @pl.when(step == 0)
        def _():
            load_weights(lambda i: comm_in[0].at[i])

    def weight(i):
        return w_s[i].reshape(width, width)

    @pl.when(step < nb)
    def _():
        here = pl.ds(pl.multiple_of(step * block, block), block)
        hat, _ = norm_parts(x_ref[...].astype(F32))
        h = (hat * lg_ref[...] + lb_ref[...]).astype(BF16)
        h_ref[...] = h
        q = ((dot_nn(h, weight(0)) + qb_ref[...]).astype(BF16).astype(F32) * factor).astype(BF16)
        k = dot_nn(h, weight(1)).astype(BF16)
        v = (dot_nn(h, weight(2)) + vb_ref[...]).astype(BF16)
        for scratch, value in ((q_s, q), (k_s, k), (v_s, v)):
            scratch[here, :] = value

    @pl.when((step >= nb) & (step < nb + pairs))
    def _():
        pair = step - nb
        cols = pl.ds(pl.multiple_of(pair * (2 * head), 2 * head), 2 * head)

        def store(i, ctx, logs):
            c_s[i * block : (i + 1) * block, cols] = ctx
            for n in range(2):
                lse_ref[0, n : n + 1, i * block : (i + 1) * block] = logs[n * head : n * head + 1, :]

        for ref, scratch in ((q_ref, q_s), (k_ref, k_s), (v_ref, v_s)):
            ref[...] = scratch[:, cols]
        attend_pair(
            length_ref[0], [scale_ref[2 * pair + n] for n in range(2)],
            lambda i: q_s[i * block : (i + 1) * block, cols], k_s[:, cols], v_s[:, cols], seq, block, head, store,
        )

    @pl.when(step >= nb + pairs)
    def _():
        here = pl.ds(pl.multiple_of((step - nb - pairs) * block, block), block)
        c = c_s[here, :]
        c_ref[...] = c
        o = dot_nn(c, weight(3)) + ob_ref[...]
        o_ref[...] = o
        hat, _ = norm_parts(o)
        x2 = x_ref[...].astype(F32) + (hat * pg_ref[...] + pb_ref[...])
        x2_ref[...] = x2
        hat2, _ = norm_parts(x2)
        h2_ref[...] = (hat2 * fg_ref[...] + fb_ref[...]).astype(BF16)

    if fused:

        @pl.when(step == last)
        def _():
            for action in actions(table.get(last, [])):
                action()
            for job in jobs[4:]:
                job.finish()


def front(length, scale, x, vectors, weights, rows, ffn, block, head, factor, fused):
    seq, width = x.shape
    nb, pairs = seq // block, width // (2 * head)
    steps = 2 * nb + pairs
    x_rows = pl.BlockSpec((block, width), lambda i: (jnp.where(i < nb + pairs, jnp.minimum(i, nb - 1), i - nb - pairs), 0))
    first = pl.BlockSpec((block, width), lambda i: (clip(i, 0, nb), 0))
    final = pl.BlockSpec((block, width), lambda i: (clip(i, nb + pairs, nb), 0))
    smem = pl.BlockSpec(memory_space=pltpu.SMEM)
    hbm = pl.BlockSpec(memory_space=pl.ANY)
    out_specs = [first] + [pl.BlockSpec((None, seq, 2 * head), lambda i: (clip(i, nb, pairs), 0, 0))] * 3
    out_specs += [final, pl.BlockSpec((1, 2, seq), lambda i: (clip(i, nb, pairs), 0, 0))] + [final] * 3
    out_shape = [sds((seq, width), BF16)] + [sds((pairs, seq, 2 * head), BF16)] * 3 + [sds((seq, width), BF16)]
    out_shape += [sds((pairs, 2, seq), F32)] + [sds((seq, width), F32)] * 2
    out_shape += [sds((seq, width), BF16)]
    scratch = [pltpu.VMEM((seq, width), BF16)] * 4 + [pltpu.SemaphoreType.DMA((4,))]
    if fused:
        out_shape += gathered_shapes(rows, ffn, weights)
        out_specs += [hbm] * 3
        scratch = [pltpu.VMEM((4, rows, ffn // 2, 2) + weights[0].shape, BF16)] + scratch
        scratch += gather_sems(8, rows, ffn // 2)
    else:
        scratch = [pltpu.VMEM((4, width, width), BF16)] + scratch
    return pl.pallas_call(
        functools.partial(front_kernel, rows=rows, ffn=ffn, block=block, head=head, factor=factor, fused=fused),
        grid=(steps,),
        in_specs=[smem, smem, x_rows] + [whole((1, width))] * 9 + [hbm] * len(weights),
        out_specs=out_specs,
        out_shape=out_shape,
        scratch_shapes=scratch,
        compiler_params=params(60 * MIB, **comm_params(fused, 0)),
        name="forward_attention",
    )(length, scale, x, *vectors, *weights)


def ffn_kernel(
    length_ref, h2_ref, ct_ref, x2_ref, wup_ref, wdn_ref, ub_ref, mg_ref, mb_ref, db_ref,
    res_ref, dh2_ref, m_ref, du_ref, gub_ref, gmg_ref, gmb_ref, gdb_ref,
    e_s, gp_s, dm_s,
):
    step = pl.program_id(0)
    block, width = h2_ref.shape
    nb, _, hb = wup_ref.shape

    units = nb * hb
    row = lax.broadcasted_iota(jnp.int32, (block, width), 0) + step * block
    valid = row < length_ref[0]
    h2 = h2_ref[...]
    dfr = jnp.where(valid, ct_ref[...].astype(F32), 0.0).astype(BF16)

    @pl.when(step == 0)
    def _():
        gub_ref[...] = jnp.zeros_like(gub_ref)
        gmg_ref[...] = jnp.zeros_like(gmg_ref)
        gmb_ref[...] = jnp.zeros_like(gmb_ref)
        gdb_ref[...] = jnp.zeros_like(gdb_ref)

    gdb_ref[...] += col_sum(dfr.astype(F32))

    def first(j, sums, wait):
        u = dot_nn(h2, wup_ref[j]) + ub_ref[j]
        dm = dot_nn(dfr, wdn_ref[j])
        cdf = 0.5 * (1.0 + lax.erf(u * math.sqrt(0.5)))
        e = u * cdf
        gp = cdf + u * (jnp.exp(u * u * -0.5) * (1.0 / math.sqrt(2.0 * math.pi)))
        dmh = dm * mg_ref[j]
        e_s[j] = e
        gp_s[j] = gp
        dm_s[j] = dm
        terms = (e, e * e, dmh, dmh * e)
        return tuple(s + jnp.sum(t, axis=-1, keepdims=True) for s, t in zip(sums, terms))

    def rows(wait):
        zero = jnp.zeros((block, 1), F32)
        sums = (zero,) * 4
        for j in range(nb):
            sums = first(j, sums, wait)
        sum_e, sum_ee, sum_d, sum_de = sums
        mu = sum_e / units
        inverse = lax.rsqrt(sum_ee / units - mu * mu + epsilon)
        mean_d = sum_d / units
        mean_dh = (sum_de - mu * sum_d) * inverse / units

        def second(j, sums):
            f, dh2 = sums
            ehat = (e_s[j] - mu) * inverse
            dm = dm_s[j]
            m = (ehat * mg_ref[j] + mb_ref[j]).astype(BF16)
            m_ref[j] = m
            f = f + dot_nt(m, wdn_ref[j])
            de = (dm * mg_ref[j] - mean_d - ehat * mean_dh) * inverse
            du = (de * gp_s[j]).astype(BF16)
            du_ref[j] = du
            dh2 = dh2 + dot_nt(du, wup_ref[j])
            gub_ref[j] += col_sum(du.astype(F32))
            gmg_ref[j] += col_sum(dm * ehat)
            gmb_ref[j] += col_sum(dm)
            return f, dh2

        sums = (jnp.zeros((block, width), F32),) * 2
        for j in range(nb):
            sums = second(j, sums)
        f, dh2 = sums
        res_ref[...] = jnp.where(valid, x2_ref[...] + f + db_ref[...], 0.0)
        dh2_ref[...] = dh2

    rows(False)


def feed_forward(length, h2, ct, x2, wup, wdn, ub, mg, mb, db, block):
    seq, width = h2.shape
    nb, _, hb = wup.shape
    rows = pl.BlockSpec((block, width), lambda i: (i, 0))
    smem = pl.BlockSpec(memory_space=pltpu.SMEM)
    hbm = pl.BlockSpec(memory_space=pl.ANY)
    units = whole((nb, 1, hb))
    blocks = pl.BlockSpec((nb, block, hb), lambda i: (0, i, 0))
    sums = out_whole((nb, 1, hb))
    return pl.pallas_call(
        ffn_kernel,
        grid=(seq // block,),
        in_specs=[
            smem, rows, rows, rows, whole((nb, width, hb)), whole((nb, width, hb)),
            units, units, units, whole((1, width)),
        ],
        out_specs=[rows, rows, blocks, blocks, sums, sums, sums, out_whole((1, width))],
        out_shape=[
            sds((seq, width), F32), sds((seq, width), F32), sds((nb, seq, hb), BF16), sds((nb, seq, hb), BF16),
            sds((nb, 1, hb), F32), sds((nb, 1, hb), F32), sds((nb, 1, hb), F32), sds((1, width), F32),
        ],
        scratch_shapes=[pltpu.VMEM((nb, block, hb), F32)] * 3,
        compiler_params=params(60 * MIB),
        cost_estimate=pl.CostEstimate(
            flops=16 * seq * width * nb * hb, bytes_accessed=60 * MIB, transcendentals=2 * seq * nb * hb
        ),
        name="feed_forward",
    )(length, h2, ct, x2, wup, wdn, ub, mg, mb, db)


def ffn_weights_kernel(length_ref, h2_ref, ct_ref, m_ref, du_ref, gup_ref, gdn_ref, h2t_s, dft_s):
    seq, width = h2_ref.shape

    @pl.when(pl.program_id(0) == 0)
    def _():
        row = lax.broadcasted_iota(jnp.int32, (seq, width), 0)
        dfr = jnp.where(row < length_ref[0], ct_ref[...], 0)
        h2t_s[...] = h2_ref[...].T
        dft_s[...] = dfr.T

    gdn_ref[0] = dot_nn(dft_s[...], m_ref[0]).astype(BF16)
    gup_ref[0] = dot_nn(h2t_s[...], du_ref[0]).astype(BF16)


def ffn_weights_pair_kernel(
    length_ref, h2_ref, ct_ref, m_ref, du_ref, gdn_ref, gup_ref, h2t_s, dft_s, grads_s, half_s, send, recv, *, rows, ffn,
):
    step = pl.program_id(0)
    place = Place(rows, ffn)
    seq, width = h2_ref.shape
    depth = place.depth

    def give(a, z):
        return remote(
            grads_s.at[a, z, 1 - place.c], half_s.at[a, z], send.at[a, z], recv.at[a, z],
            place.device(place.r, place.z, 1 - place.c),
        )

    @pl.when(step == 0)
    def _():
        place.enter(near=False)
        row = lax.broadcasted_iota(jnp.int32, (seq, width), 0)
        dfr = jnp.where(row < length_ref[0], ct_ref[...], 0)
        h2t_s[...] = h2_ref[...].T
        dft_s[...] = dfr.T

    @pl.when(step < depth)
    def _():
        @pl.loop(0, 2)
        def _(c):
            grads_s[0, step, c] = dot_nn(dft_s[...], m_ref[c]).astype(BF16)
            grads_s[1, step, c] = dot_nn(h2t_s[...], du_ref[c]).astype(BF16)

        for a in range(2):
            give(a, step).start()

    @pl.when(step > 0)
    def _():
        z = step - 1
        for a, out in enumerate((gdn_ref, gup_ref)):
            give(a, z).wait()
            out[0] = grads_s[a, z, place.c] + half_s[a, z]


def ffn_weight_pair_sums(length, h2, ct, m, du, rows, ffn):
    seq, width = h2.shape
    nb, _, hb = m.shape
    depth = nb // 2
    smem = pl.BlockSpec(memory_space=pltpu.SMEM)
    block = pl.BlockSpec((2, seq, hb), lambda j: (clip(j, 0, depth), 0, 0))
    out = pl.BlockSpec((1, width, hb), lambda j: (clip(j, 1, depth), 0, 0))
    return pl.pallas_call(
        functools.partial(ffn_weights_pair_kernel, rows=rows, ffn=ffn),
        grid=(depth + 1,),
        in_specs=[smem, whole((seq, width)), whole((seq, width)), block, block],
        out_specs=[out, out],
        out_shape=[sds((depth, width, hb), BF16)] * 2,
        scratch_shapes=[pltpu.VMEM((width, seq), BF16)] * 2 + [
            pltpu.VMEM((2, depth, 2, width, hb), BF16),
            pltpu.VMEM((2, depth, width, hb), BF16),
            pltpu.SemaphoreType.DMA((2, depth)),
            pltpu.SemaphoreType.DMA((2, depth)),
        ],
        compiler_params=params(60 * MIB, **comm_params(True, 1)),
        name="ffn_weight_pair_sums",
    )(length, h2, ct, m, du)


def ffn_weight_grads(length, h2, ct, m, du):
    seq, width = h2.shape
    nb, _, hb = m.shape
    smem = pl.BlockSpec(memory_space=pltpu.SMEM)
    block = pl.BlockSpec((1, seq, hb), lambda j: (j, 0, 0))
    out = pl.BlockSpec((1, width, hb), lambda j: (j, 0, 0))
    return pl.pallas_call(
        ffn_weights_kernel,
        grid=(nb,),
        in_specs=[smem, whole((seq, width)), whole((seq, width)), block, block],
        out_specs=[out, out],
        out_shape=[sds((nb, width, hb), BF16)] * 2,
        scratch_shapes=[pltpu.VMEM((width, seq), BF16)] * 2,
        compiler_params=params(),
        cost_estimate=pl.CostEstimate(
            flops=4 * seq * width * nb * hb, bytes_accessed=36 * MIB, transcendentals=0
        ),
        name="ffn_weight_grads",
    )(length, h2, ct, m, du)


def attend_back_pair(length, q_all, k_of, v_of, g_all, lse_ref, inner_row, dq_s, store, seq, block, head):
    lanes = 2 * head
    lane = lax.broadcasted_iota(jnp.int32, (seq, lanes), 1)
    dq_s[...] = jnp.zeros_like(dq_s)
    zero = jnp.zeros_like(q_all)
    q_heads = [jnp.where(lane < head, q_all, zero), jnp.where(lane >= head, q_all, zero)]
    g_heads = [jnp.where(lane < head, g_all, zero), jnp.where(lane >= head, g_all, zero)]
    for j in range(seq // block):
        start = j * block
        width = seq - start
        k, v = k_of(j), v_of(j)
        key_pos = lax.broadcasted_iota(jnp.int32, (block, width), 0) + start
        row_pos = lax.broadcasted_iota(jnp.int32, (block, width), 1) + start
        allowed = (key_pos <= row_pos) & (key_pos < length)
        dk = dv = None
        dqs = []
        for n in range(2):
            q = q_heads[n][start:, :]
            g = g_heads[n][start:, :]
            scores = dot_nt(k, q)
            probs = jnp.where(allowed, jnp.exp(scores - lse_ref[0, n : n + 1, start:]), 0.0)
            grad_probs = dot_nt(v, g)
            grad_scores = (probs * (grad_probs - inner_row(n)[:, start:])).astype(BF16)
            dv_part = dot_nn(probs.astype(BF16), g)
            dk_part = dot_nn(grad_scores, q)
            dv = dv_part if n == 0 else dv + dv_part
            dk = dk_part if n == 0 else dk + dk_part
            dqs.append(dot_tn(grad_scores, k))
        dq_s[start:, :] += jnp.where(lane[start:, :] < head, dqs[0], dqs[1])
        store(j, dk.astype(BF16), dv.astype(BF16))


def norms_back(dh2, x2, o, c, dy, w, fg, pg, hs, head, sums, g_store, dx2_store, dor_store):
    block, width = dh2.shape
    heads = width // head
    hat2, inverse2 = norm_parts(x2)
    dx2 = dy + norm_back(dh2 * fg, hat2, inverse2)
    dx2_store(dx2)
    hat, inverse = norm_parts(o)
    dor = norm_back(dx2 * pg, hat, inverse).astype(BF16)
    dor_store(dor)
    sums(
        col_sum(dor.astype(F32)), col_sum(dx2 * hat), col_sum(dx2), col_sum(dh2 * hat2), col_sum(dh2),
    )
    dc = dot_nt(dor, w)
    g_store((dc * hs).astype(BF16))
    product = dc * c.astype(F32)
    high = product.astype(BF16)
    low = (product - high.astype(F32)).astype(BF16)
    owner = lax.broadcasted_iota(jnp.int32, (heads, width), 1) // head
    pick = (owner == lax.broadcasted_iota(jnp.int32, (heads, width), 0)).astype(BF16)
    return dot_nt(pick, high) + dot_nt(pick, low)


def valid_grad(ct, length, first):
    row = lax.broadcasted_iota(jnp.int32, ct.shape, 0) + first
    return jnp.where(row < length, ct.astype(F32), 0.0)


def back_kernel(
    length_ref, dh2_ref, ct_ref, x2_ref, o_ref, c_ref, w_ref, fg_ref, pg_ref, hs_ref, q_ref, k_ref, v_ref, lse_ref,
    dx2_ref, dor_ref, dq_ref, dk_ref, dv_ref, ghs_ref, sums_ref, g_s, inner_s, dq_s, *, block, head, factor,
):
    step = pl.program_id(0)
    seq, width = g_s.shape
    nb = seq // block

    @pl.when(step == 0)
    def _():
        ghs_ref[...] = jnp.zeros_like(ghs_ref)
        sums_ref[...] = jnp.zeros_like(sums_ref)

    @pl.when(step < nb)
    def _():
        here = pl.ds(pl.multiple_of(step * block, block), block)

        def sums(*parts):
            for n, part in enumerate(parts):
                sums_ref[n : n + 1, :] += part

        def put(ref, *index):
            def store(value):
                ref[index if index else ...] = value

            return store

        inner = norms_back(
            dh2_ref[...], x2_ref[...], o_ref[...], c_ref[...], valid_grad(ct_ref[...], length_ref[0], step * block),
            w_ref[...], fg_ref[...], pg_ref[...], hs_ref[...], head, sums, put(g_s, here, slice(None)), put(dx2_ref),
            put(dor_ref),
        )
        inner_s[step] = inner
        ghs_ref[...] += jnp.broadcast_to(jnp.sum(inner, axis=-1, keepdims=True), ghs_ref.shape)

    @pl.when(step >= nb)
    def _():
        pair = step - nb
        cols = pl.ds(pl.multiple_of(pair * (2 * head), 2 * head), 2 * head)
        inner_rows = [
            jnp.concatenate([inner_s[i, pl.ds(2 * pair + n, 1), :] for i in range(nb)], axis=1) for n in range(2)
        ]

        def store(j, dk, dv):
            dk_ref[j * block : (j + 1) * block, :] = dk
            dv_ref[j * block : (j + 1) * block, :] = dv

        attend_back_pair(
            length_ref[0], q_ref[...], lambda j: k_ref[j * block : (j + 1) * block, :],
            lambda j: v_ref[j * block : (j + 1) * block, :], g_s[:, cols], lse_ref, lambda n: inner_rows[n], dq_s, store,
            seq, block, head,
        )
        dq_ref[...] = (dq_s[...] * factor).astype(BF16)


def back(length, dh2, ct, x2, o, c, w, fg, pg, hs, q, k, v, lse, block, head, factor):
    seq, width = dh2.shape
    nb, pairs, heads = seq // block, width // (2 * head), width // head
    part = pl.BlockSpec((block, width), lambda i: (clip(i, 0, nb), 0))
    cols = pl.BlockSpec((seq, 2 * head), lambda i: (0, clip(i, nb, pairs)))
    heads_in = pl.BlockSpec((None, seq, 2 * head), lambda i: (clip(i, nb, pairs), 0, 0))
    smem = pl.BlockSpec(memory_space=pltpu.SMEM)
    vec = whole((1, width))
    return pl.pallas_call(
        functools.partial(back_kernel, block=block, head=head, factor=factor),
        grid=(nb + pairs,),
        in_specs=[smem] + [part] * 5 + [whole((width, width))] + [vec] * 3 + [heads_in] * 3
        + [pl.BlockSpec((1, 2, seq), lambda i: (clip(i, nb, pairs), 0, 0))],
        out_specs=[part] * 2 + [cols] * 3 + [out_whole((heads, 128)), out_whole((8, width))],
        out_shape=[sds((seq, width), F32)] + [sds((seq, width), BF16)] * 4
        + [sds((heads, 128), F32), sds((8, width), F32)],
        scratch_shapes=[
            pltpu.VMEM((seq, width), BF16), pltpu.VMEM((nb, heads, block), F32), pltpu.VMEM((seq, 2 * head), F32),
        ],
        compiler_params=params(60 * MIB),
        name="backward_attention",
    )(length, dh2, ct, x2, o, c, w, fg, pg, hs, q, k, v, lse)


def weights_kernel(left_ref, right_ref, out_ref, left_s):
    @pl.when(pl.program_id(0) == 0)
    def _():
        left_s[...] = left_ref[...].T

    out_ref[...] = dot_nn(left_s[...], right_ref[...]).astype(BF16)


def weight_grad(left, right, block):
    seq, width = left.shape
    cols = right.shape[1]
    return pl.pallas_call(
        weights_kernel,
        grid=(cols // block,),
        in_specs=[whole((seq, width)), pl.BlockSpec((seq, block), lambda j: (0, j))],
        out_specs=pl.BlockSpec((width, block), lambda j: (0, j)),
        out_shape=sds((width, cols), BF16),
        scratch_shapes=[pltpu.VMEM((width, seq), BF16)],
        compiler_params=params(),
        name="weight_grad",
    )(left, right)


def input_back(dq, dk, dv, w, x, dx2, gain, sums):
    dh = dot_nt(dq, w(0)) + dot_nt(dk, w(1)) + dot_nt(dv, w(2))
    hat, inverse = norm_parts(x.astype(F32))
    sums(col_sum(dh * hat), col_sum(dh), col_sum(dq.astype(F32)), col_sum(dv.astype(F32)))
    return dx2 + norm_back(dh * gain, hat, inverse)


def input_kernel(dq_ref, dk_ref, dv_ref, w_ref, x_ref, dx2_ref, gain_ref, dx_ref, sums_ref):
    @pl.when(pl.program_id(0) == 0)
    def _():
        sums_ref[...] = jnp.zeros_like(sums_ref)

    def sums(*parts):
        for n, part in enumerate(parts):
            sums_ref[n : n + 1, :] += part

    dx_ref[...] = input_back(
        dq_ref[...], dk_ref[...], dv_ref[...], lambda i: w_ref[i], x_ref[...], dx2_ref[...], gain_ref[...], sums
    )


def input_grad(dq, dk, dv, w, x, dx2, gain, block):
    seq, width = dq.shape
    rows = pl.BlockSpec((block, width), lambda i: (i, 0))
    return pl.pallas_call(
        input_kernel,
        grid=(seq // block,),
        in_specs=[rows, rows, rows, whole((3, width, width)), rows, rows, whole((1, width))],
        out_specs=[rows, out_whole((8, width))],
        out_shape=[sds((seq, width), F32), sds((8, width), F32)],
        compiler_params=params(),
        name="input_grad",
    )(dq, dk, dv, w, x, dx2, gain)


class AllSum:
    def __init__(self, place, stages, far, send, recv):
        self.place, self.stages, self.far, self.send, self.recv = place, stages, far, send, recv

    def copy(self, k):
        p = self.place
        device = (
            p.device(p.r, p.z, 1 - p.c), p.device(p.row_flip(p.r, 0), p.z, p.c), p.device(p.row_flip(p.r, 1), p.z, p.c)
        )[k]
        return remote(self.stages.at[k], self.stages.at[3 + k], self.send.at[k], self.recv.at[k], device)

    def along(self, d):
        p = self.place
        return remote(
            self.far.at[p.z], self.far.at[p.z], self.send.at[2 + d], self.recv.at[2 + d], p.device(p.r, p.z_at(d), p.c)
        )

    def begin(self):
        self.copy(0).start()

    def add(self, k):
        self.copy(k).wait_recv()
        total = self.stages[k] + self.stages[3 + k]
        if k < 2:
            self.stages[k + 1] = total
            self.copy(k + 1).start()
        else:
            self.far[self.place.z] = total
            for d in range(1, self.place.depth):
                self.along(d).start()

    def total(self):
        p = self.place
        for d in range(1, p.depth):
            there = self.far.at[p.z_at(-d)]
            pltpu.make_async_copy(there, there, self.recv.at[2 + d]).wait()
        out = self.far[0]
        for z in range(1, p.depth):
            out = out + self.far[z]
        return out

    def finish(self):
        for k in range(3):
            self.copy(k).wait_send()
        for d in range(1, self.place.depth):
            self.along(d).wait_send()


def tail_kernel(
    length_ref, dh2_ref, ct_ref, x2_ref, o_ref, c_ref, x_ref, fg_ref, pg_ref, hs_ref, gain_ref, small_ref,
    q_ref, k_ref, v_ref, lse_ref, wo_ref, h_ref, w_ref, down_ref, up_ref,
    dx_ref, small_out, down_out, up_out, wo_out, wv_out, wk_out, wq_out,
    w_s, g_s, right_s, left_s, dx2_s, inner_s, dqa_s, acc_s, ghs_s, load,
    stage, stage_load, grads, *bufs, rows, ffn, block, head, factor,
):
    dq_s, dk_s, dv_s = (right_s.at[i] for i in range(3))
    step = pl.program_id(0)
    seq, width = g_s.shape
    nb = seq // block
    fine = block // 2
    nf = seq // fine
    pairs = width // (2 * head)
    place = Place(rows, ffn)
    depth = place.depth
    weight_at = nf
    attend_at = weight_at + 1
    input_at = attend_at + pairs
    others_at = input_at + nb
    last = others_at + 2

    take = iter(bufs)
    half_rows = down_out.shape[0] // 2
    ffn_jobs = []
    for n in range(4):
        part = pl.ds(n % 2 * half_rows, half_rows)
        ref = (down_ref, up_ref)[n // 2]
        ffn_jobs.append(
            PairExchange(
                place, lambda r, z, ref=ref, part=part: ref.at[z, r, part], stage.at[n % 2], stage_load.at[n],
                *(next(take) for _ in range(5)),
            )
        )
    proj_jobs = []
    for n in range(4):
        held = grads.at[n % 2]
        proj_jobs.append(
            CoreExchange(place, lambda r, z, c, held=held: held.at[r, z, c], held, *(next(take) for _ in range(6)))
        )
    small, late = (AllSum(place, *(next(take) for _ in range(4))) for _ in range(2))
    outs = (wo_out, wv_out, wk_out, wq_out)

    def matrix(slot, i):
        return pltpu.make_async_copy(w_ref.at[:, :, :, i], w_s.at[slot], load.at[slot])

    h_copy = pltpu.make_async_copy(h_ref, g_s, load.at[3])

    def start():
        place.enter()
        for i in range(3):
            matrix(i, i).start()
        ffn_jobs[0].leave()
        ffn_jobs[1].leave()
        acc_s[...] = jnp.zeros_like(acc_s)
        ghs_s[...] = jnp.zeros_like(ghs_s)

    def start_small():
        small.stages[0] = small_ref[...]
        small.stages[0, 0:5, :] = acc_s[4:9, :]
        small.stages[0, 6:7, 0 : ghs_s.shape[0]] = ghs_s[...].T[0:1, :]
        small.begin()

    def start_late():
        late.stages[0] = acc_s[0:8, :]
        late.begin()

    def take_h():
        h_copy.wait()
        left_s[...] = g_s[...].T

    at_steps(step, {
        0: [start],
        weight_at: [start_small],
        attend_at: [ffn_jobs[0].one, functools.partial(small.add, 0), ffn_jobs[2].leave],
        attend_at + 2: [ffn_jobs[1].one, functools.partial(small.add, 1)],
        attend_at + 3: [ffn_jobs[0].two, proj_jobs[0].leave, ffn_jobs[3].leave],
        attend_at + 6: [ffn_jobs[2].one, functools.partial(small.add, 2)],
        attend_at + 7: [ffn_jobs[1].two, proj_jobs[0].one],
        input_at: [h_copy.start, matrix(0, 0).wait, matrix(1, 1).wait, matrix(2, 2).wait],
        input_at + 2: [ffn_jobs[3].one, ffn_jobs[2].two, proj_jobs[0].two],
        others_at: [start_late, take_h, ffn_jobs[3].two],
        others_at + 1: [proj_jobs[1].leave, functools.partial(late.add, 0)],
        others_at + 2: [proj_jobs[2].leave, proj_jobs[1].one, functools.partial(late.add, 1)],
    })

    def sums_from(first):
        def sums(*parts):
            for n, part in enumerate(parts):
                acc_s[first + n : first + n + 1, :] += part

        return sums

    @pl.when(step < nf)
    def _():
        here = pl.ds(pl.multiple_of(step * fine, fine), fine)

        def put(ref):
            def store(value):
                ref[here, :] = value

            return store

        c = c_ref[...]
        left_s[:, here] = c.T
        inner = norms_back(
            dh2_ref[...], x2_ref[...], o_ref[...], c, valid_grad(ct_ref[...], length_ref[0], step * fine),
            wo_ref[...].reshape(width, width), fg_ref[...], pg_ref[...], hs_ref[...], head, sums_from(4), put(g_s), put(dx2_s),
            put(dq_s),
        )
        inner_s[step] = inner
        ghs_s[...] += jnp.broadcast_to(jnp.sum(inner, axis=-1, keepdims=True), ghs_s.shape)

    @pl.when((step == weight_at) | (step >= others_at))
    def _():
        first = step == weight_at
        right = right_s.at[jnp.where(first, 0, last - step)]
        slot = jnp.where(first, 0, lax.rem(step - others_at + 1, 2))
        cut = width // 2

        @pl.loop(0, 2)
        def _(i):
            cols = pl.ds(pl.multiple_of(i * cut, cut), cut)
            value = dot_nn(left_s[...], right[:, cols]).astype(BF16)
            grads[slot, ..., cols] = value.reshape(grads.shape[1:-1] + (cut,))

    at_steps(step, {weight_at: [proj_jobs[0].begin], **{others_at + n: [proj_jobs[n + 1].begin] for n in range(3)}})

    @pl.when((step >= attend_at) & (step < input_at))
    def _():
        pair = step - attend_at
        cols = pl.ds(pl.multiple_of(pair * (2 * head), 2 * head), 2 * head)
        inner_rows = [
            jnp.concatenate([inner_s[i, pl.ds(2 * pair + n, 1), :] for i in range(nf)], axis=1) for n in range(2)
        ]

        def store(j, dk, dv):
            dk_s[j * block : (j + 1) * block, cols] = dk
            dv_s[j * block : (j + 1) * block, cols] = dv

        attend_back_pair(
            length_ref[0], q_ref[...], lambda j: k_ref[j * block : (j + 1) * block, :],
            lambda j: v_ref[j * block : (j + 1) * block, :], g_s[:, cols], lse_ref, lambda n: inner_rows[n], dqa_s, store,
            seq, block, head,
        )
        dq_s[:, cols] = (dqa_s[...] * factor).astype(BF16)

    @pl.when((step >= input_at) & (step < others_at))
    def _():
        here = pl.ds(pl.multiple_of((step - input_at) * block, block), block)
        dx_ref[...] = input_back(
            dq_s[here, :], dk_s[here, :], dv_s[here, :], lambda i: w_s[i].reshape(width, width), x_ref[...], dx2_s[here, :],
            gain_ref[...], sums_from(0),
        )

    @pl.when(step == last)
    def _():
        _, wv, wk, wq = proj_jobs
        for action in (
            wq.leave, functools.partial(late.add, 2), wk.one, wv.two, wq.one, wk.two, wq.two,
        ):
            action()
        for n, job in enumerate(ffn_jobs):
            (down_out, up_out)[n // 2][n % 2 * half_rows : (n % 2 + 1) * half_rows, :] = job.total()
        small_out[0:8, :] = late.total()
        small_out[8:, :] = small.total()
        for job in (small, late):
            job.finish()
        for job, out in zip(proj_jobs, outs):
            out[...] = job.total()


def tail(
    length, dh2, ct, x2, o, c, x, fg, pg, hs, gain, small, q, k, v, lse, h, w, down, up, rows, ffn, block, head, factor
):
    seq, width = dh2.shape
    nb, pairs, heads = seq // block, width // (2 * head), width // head
    depth = ffn // 2
    fine = block // 2
    nf = seq // fine
    input_at = nf + 1 + pairs
    first = pl.BlockSpec((fine, width), lambda i: (clip(i, 0, nf), 0))
    final = pl.BlockSpec((block, width), lambda i: (clip(i, input_at, nb), 0))
    cols = pl.BlockSpec((None, seq, 2 * head), lambda i: (clip(i, nf + 1, pairs), 0, 0))
    smem = pl.BlockSpec(memory_space=pltpu.SMEM)
    hbm = pl.BlockSpec(memory_space=pl.ANY)
    vmem = pl.BlockSpec(memory_space=pltpu.VMEM)
    vec = whole((1, width))
    out_weight = pl.BlockSpec(
        (rows, depth, 2, None) + w.shape[4:], lambda i: (0, 0, 0, 3, 0, 0), pipeline_mode=pl.Buffered(1)
    )
    unit = down.shape[2:]
    piece = (unit[0] // 2, unit[1])
    proj = (width // (rows * ffn), width)
    dma = pltpu.SemaphoreType.DMA

    def arrivals(shape):
        return [pltpu.VMEM((depth, 2) + shape, BF16), pltpu.VMEM((depth,) + shape, BF16), pltpu.VMEM((depth,) + shape, BF16)]

    scratch = [
        pltpu.VMEM((3, rows, depth, 2) + proj, BF16),
        pltpu.VMEM((seq, width), BF16), pltpu.VMEM((3, seq, width), BF16), pltpu.VMEM((width, seq), BF16),
        pltpu.VMEM((seq, width), F32),
        pltpu.VMEM((nf, heads, fine), F32), pltpu.VMEM((seq, 2 * head), F32), pltpu.VMEM((16, width), F32),
        pltpu.VMEM((heads, 128), F32), dma((4,)),
        pltpu.VMEM((2, depth, 2) + piece, BF16), dma((4, depth, 2)), pltpu.VMEM((2, rows, depth, 2) + proj, BF16),
    ]
    for _ in range(4):
        scratch += arrivals(piece) + [dma((4,)), dma((4, depth))]
    for _ in range(4):
        scratch += [pltpu.VMEM((depth, rows) + proj, BF16)] + arrivals(proj) + [dma((4,)), dma((8, depth))]
    late = (8, width)
    for shape in (small.shape, late):
        scratch += [pltpu.VMEM((6,) + shape, F32), pltpu.VMEM((depth,) + shape, F32), dma((2 + depth,)), dma((2 + depth,))]
    return pl.pallas_call(
        functools.partial(tail_kernel, rows=rows, ffn=ffn, block=block, head=head, factor=factor),
        grid=(input_at + nb + 3,),
        in_specs=[smem] + [first] * 5 + [final] + [vec] * 4 + [whole(small.shape)] + [cols] * 3
        + [pl.BlockSpec((1, 2, seq), lambda i: (clip(i, nf + 1, pairs), 0, 0)), out_weight] + [hbm] * 4,
        out_specs=[final] + [vmem] * 7,
        out_shape=[sds((seq, width), F32), sds((8 + small.shape[0], width), F32), sds(unit, F32), sds(unit, F32)] + [sds(proj, F32)] * 4,
        scratch_shapes=scratch,
        compiler_params=params(62 * MIB, **comm_params(True, 2)),
        name="backward_and_sums",
    )(length, dh2, ct, x2, o, c, x, fg, pg, hs, gain, small, q, k, v, lse, w, h, w, down, up)


def widen(blocks, lanes):
    nb, rows, hb = blocks.shape
    group = max(1, lanes // hb)
    if group == 1:
        return blocks
    return blocks.reshape(nb // group, group, rows, hb).transpose(0, 2, 1, 3).reshape(nb // group, rows, group * hb)


def narrow(blocks, hb):
    nb, rows, lanes = blocks.shape
    group = lanes // hb
    if group == 1:
        return blocks
    return blocks.reshape(nb, rows, group, hb).transpose(0, 2, 1, 3).reshape(nb * group, rows, hb)


def rows_of(vector):
    return vector.reshape(1, -1)


def shards(
    tokens, lengths, cotangent, ln_attn_gain, ln_attn_bias, w_query, query_bias, w_key, w_value, value_bias,
    head_scale, w_out, out_bias, post_gain, post_bias, ffn_gain, ffn_bias, w_up, up_bias, mid_gain, mid_bias,
    w_down, down_bias,
):
    seq, width = tokens.shape
    heads = head_scale.shape[0]
    head = width // heads
    factor = head ** (-0.5)
    block = min(seq, 256)
    rows, ffn = lax.axis_size("rows"), lax.axis_size("ffn")
    own_units = w_up.shape[1]
    hidden = own_units * ffn
    fused = ffn == 8 and w_query.shape[0] % 16 == 0 and own_units % 512 == 0
    weights = (w_query, w_key, w_value, w_out, w_down, w_up)
    vectors = [
        rows_of(v)
        for v in (
            ln_attn_gain, ln_attn_bias, query_bias, value_bias, out_bias, post_gain, post_bias, ffn_gain, ffn_bias,
        )
    ]
    if not fused:
        attn, down_all, up_all = gather_all(rows, ffn, weights)
        attn = attn.transpose(3, 0, 1, 2, 4, 5).reshape(4, width, width)
        weights = (attn,)
    h, q, k, v, c, lse, o, x2, h2, *gathered = front(
        lengths, head_scale, tokens, vectors, weights, rows, ffn, block, head, factor, fused
    )
    if fused:
        attn, down_all, up_all = gathered
    wup = widen(up_all.reshape(ffn, width, own_units), 512)
    wdn = widen(down_all.reshape(ffn, width, own_units), 512)
    nb, _, hb = wup.shape
    units = lambda vector: vector.reshape(nb, 1, hb)
    result, dh2, m, du, g_ub, g_mg, g_mb, g_db = feed_forward(
        lengths, h2, cotangent, x2, wup, wdn, units(up_bias), units(mid_gain), units(mid_bias), rows_of(down_bias),
        block,
    )
    scale_cols = rows_of(jnp.repeat(head_scale, head))
    wide = [part.reshape(-1, width) for part in (g_ub, g_mg, g_mb)]
    above = jnp.concatenate([g_db, jnp.zeros((1, width), F32)] + wide, axis=0)
    above = jnp.pad(above, ((5, -(5 + above.shape[0]) % 8), (0, 0)))
    if fused:
        g_dn, g_up = (
            part.reshape((ffn // 2, rows) + w_up.shape)
            for part in ffn_weight_pair_sums(lengths, h2, cotangent, m, du, rows, ffn)
        )
        dx, small, grad_down, grad_up, g_wo, g_wv, g_wk, g_wq = tail(
            lengths, dh2, cotangent, x2, o, c, tokens, rows_of(ffn_gain), rows_of(post_gain), scale_cols,
            rows_of(ln_attn_gain), above, q, k, v, lse, h, attn, g_dn, g_up, rows, ffn, block, head, factor,
        )
    else:
        g_up, g_dn = ffn_weight_grads(lengths, h2, cotangent, m, du)
        dx2, dor, dq, dk, dv, g_hs, late = back(
            lengths, dh2, cotangent, x2, o, c, attn[3], rows_of(ffn_gain), rows_of(post_gain), scale_cols, q, k, v, lse,
            block, head, factor,
        )
        dx, early = input_grad(dq, dk, dv, attn[:3], tokens, dx2, rows_of(ln_attn_gain), block)
        g_hs = jnp.pad(g_hs[:, :1].T, ((0, 0), (0, width - heads)))
        small = jnp.concatenate([early, late[:5], above[5:6], g_hs, above[7:]], axis=0)
        small = lax.psum(small, BOTH)
        grad_down, grad_up = (
            scatter_sum(rows, ffn, narrow(part, own_units).reshape((ffn // 2, 2, rows) + w_up.shape), by_unit)
            for part in (g_dn, g_up)
        )
        g_wo, g_wv, g_wk, g_wq = (
            scatter_sum(
                rows, ffn, weight_grad(left, right, 512).reshape((rows, ffn // 2, 2) + w_query.shape), by_device
            )
            for left, right in ((c, dor), (h, dv), (h, dk), (h, dq))
        )
    n = hidden // width
    vectors = jnp.concatenate([small[:4], small[8:14]], axis=0)
    owned = small[15 : 15 + 3 * n].reshape(3, ffn, own_units)
    if fused:
        (
            dx, grad_up, grad_down, g_wq, g_wk, g_wv, g_wo, g_lg, g_lb, g_qb, g_vb, g_ob, g_pg, g_pb, g_fg, g_fb, g_db,
        ) = hand_on(dx, grad_up, grad_down, g_wq, g_wk, g_wv, g_wo, vectors)
    else:
        g_lg, g_lb, g_qb, g_vb, g_ob, g_pg, g_pb, g_fg, g_fb, g_db = vectors
    g_hs = small[14, :heads] / head_scale
    mine = lax.dynamic_index_in_dim(owned, lax.axis_index("ffn"), axis=1, keepdims=False)
    return (
        result, dx, g_lg, g_lb, g_wq, g_qb, g_wk, g_wv, g_vb, g_hs, g_wo, g_ob, g_pg, g_pb, g_fg, g_fb, grad_up, mine[0],
        mine[1], mine[2], grad_down, g_db,
    )


def hand_on_kernel(*refs):
    ins, vectors, outs, lines = refs[:7], refs[7], refs[8:15], refs[15:]
    outs[0][...] = ins[0][...]

    @pl.when(pl.program_id(0) == 0)
    def _():
        for src, out in zip(ins[1:], outs[1:]):
            out[...] = src[...]
        for n, line in enumerate(lines):
            line[...] = vectors[n, :]


def hand_on(dx, *rest):
    *grads, vectors = rest
    seq, width = dx.shape
    n = vectors.shape[0]
    block = seq // 4
    rows = pl.BlockSpec((block, width), lambda i: (i, 0))
    return pl.pallas_call(
        hand_on_kernel,
        grid=(4,),
        in_specs=[rows] + [whole(a.shape) for a in grads] + [whole(vectors.shape)],
        out_specs=[rows] + [out_whole(a.shape) for a in grads] + [out_whole((width,))] * n,
        out_shape=[sds(a.shape, F32) for a in (dx, *grads)] + [sds((width,), F32)] * n,
        compiler_params=params(),
        name="hand_on",
    )(dx, *grads, vectors)


def solution(mesh):
    split = P(BOTH, None)
    tiles = P("rows", "ffn")
    one = P()
    return jax.shard_map(
        shards,
        mesh=mesh,
        in_specs=(
            split, P(BOTH), split, one, one, split, one, split, split, one, one, split, one, one, one, one, one,
            tiles, one, one, one, tiles, one,
        ),
        out_specs=(
            split, split, one, one, split, one, split, split, one, one, split, one, one, one, one, one,
            tiles, P("ffn"), P("ffn"), P("ffn"), tiles, one,
        ),
        check_vma=False,
    )
```
